32 devices in a mesh: comp: 2 (over y), gx: 8 (over z, core), gy: 2 (over x).
Axes of the slice: x: 2, y: 2, z: 4, core: 2. Of those that a mesh axis runs over, the one named last changes fastest.
Arguments:
- state: float32 [2, 7, 256, 64, 128], P('comp', None, 'gx', 'gy'), may hold values from -6 to 6
- diffusivity: float32 [2, 7], replicated, may hold values from 0.01 to 0.06
- advection: float32 [2, 7], replicated, may hold values from 0.05 to 0.3
- solid_mask: int32 [256, 64, 128], P('gx', 'gy'), may hold values 0 or 1
- iface_map: int32 [64], P('gy'), may hold values from 0 to 63, each once
Outputs:
- new_state: float32 [2, 7, 256, 64, 128], P('comp', None, 'gx', 'gy')
The draws below stay inside these ranges and needn't reach their ends.
Inputs may be any that keep to these rules, and one draw needn't show every extreme that they name: `iface_map`: each turbine inlet row takes exactly one combustor exit-plane row, and every exit-plane row is taken once.
All inputs are finite; a program needn't handle non-finite values. No bound on the sum of `solid_mask` on one device may be relied on, other than what follows from the above.
Results may differ from the reference program's by a relative error of at most 0.0014.
Values may be sent and summed in bfloat16 or wider, within the bound.
No kernel may reach another device: no remote copies, remote signals or barrier semaphores. Data moves between devices by JAX's collectives and lax.ppermute only.
A program may use at most 64 MiB of HBM per device.

```python
import math
import jax
import jax.numpy as jnp
from jax import lax

FIELDS = 7
NX = 256
NY = 64
NZ = 128


def plant(drawn, own_key, smallest, high):
    longest = drawn.shape.index(max(drawn.shape))
    spots = []
    for shift in (0, 1):
        where = [jax.random.randint(jax.random.fold_in(own_key, axis), (), 0, length) for axis, length in enumerate(drawn.shape)]
        where[longest] = (where[longest] + shift) % drawn.shape[longest]
        spots.append(tuple(where))
    return drawn.at[spots[0]].set(smallest).at[spots[1]].set(high)


def block_levels(stream_key, extent, shards, low, largest):
    factor_of = 1.0
    for position, shards_of in shards:
        steps = jax.random.uniform(jax.random.fold_in(jax.random.fold_in(stream_key, 6), position), (shards_of,), jnp.float32, low / len(shards), largest / len(shards))
        factor_of = factor_of * jnp.repeat(jnp.exp(steps), extent[position] // shards_of).reshape((-1,) + (1,) * (len(extent) - 1 - position))
    return factor_of


def noise(stream_key, shape, scale, reach, pieces=(), dtype=jnp.bfloat16):
    gain = block_levels(stream_key, shape, pieces, -0.22, 0.18) if pieces else 1.0
    result = jax.random.normal(stream_key, shape, jnp.float32) * scale * gain
    return jnp.minimum(jnp.maximum(result, -reach), reach).astype(dtype)


def setup_inputs(seed: int = 0) -> dict:
    arg_keys = jax.random.split(jax.random.key(seed), 6)
    return {
        "state": noise(arg_keys[0], (2, FIELDS, NX, NY, NZ), 1.0, 6.0, ((0, 2), (2, 8), (3, 2)), jnp.float32),
        "diffusivity": jnp.clip(jnp.exp(jax.random.uniform(arg_keys[1], (2, FIELDS), jnp.float32, math.log(0.01), math.log(0.06))), 0.01, 0.06),
        "advection": jnp.clip(jax.random.uniform(arg_keys[2], (2, FIELDS), jnp.float32, 0.05, 0.3), 0.05, 0.3),
        "solid_mask": plant((jax.random.randint(arg_keys[3], (NX, NY, NZ), 0, 3) < 1).astype(jnp.int32), jax.random.fold_in(arg_keys[3], 1), 0, 1),
        "iface_map": jax.random.permutation(arg_keys[4], NY).astype(jnp.int32),
    }


RATIO = 1.5
GAIN = 0.4


def field_rates(qpad, gpad, diff, speed, solid):
    mid = qpad[1:-1]
    east = qpad[2:]
    west = qpad[:-2]
    gmid = gpad[1:-1]
    geast = gpad[2:]
    gwest = gpad[:-2]
    north = jnp.roll(mid, -1, 1)
    south = jnp.roll(mid, 1, 1)
    gnorth = jnp.roll(gmid, -1, 1)
    gsouth = jnp.roll(gmid, 1, 1)
    upper = jnp.roll(mid, -1, 2)
    lower = jnp.roll(mid, 1, 2)
    gupper = jnp.roll(gmid, -1, 2)
    glower = jnp.roll(gmid, 1, 2)
    along_x = 0.5 * (gmid + geast) * (east - mid) - 0.5 * (gmid + gwest) * (mid - west)
    along_y = 0.5 * (gmid + gnorth) * (north - mid) - 0.5 * (gmid + gsouth) * (mid - south)
    along_z = 0.5 * (gmid + gupper) * (upper - mid) - 0.5 * (gmid + glower) * (mid - lower)
    diffusion = along_x + along_y + along_z
    fluid = diff * diffusion - speed * (0.5 * (east - west))
    return jnp.where(solid, RATIO * diff * diffusion, fluid)


def component_rates(fields, ghost, diff, speed, solid):
    zero_layer = jnp.zeros((1,) + fields.shape[2:], jnp.float32)
    theta = jnp.concatenate([ghost[4][None], fields[4], zero_layer], 0)
    gpad = jnp.exp(GAIN * jnp.tanh(theta))

    def one_field(items):
        qf, gf, dval, cval = items
        qpad = jnp.concatenate([gf[None], qf, zero_layer], 0)
        return field_rates(qpad, gpad, dval, cval, solid)

    return lax.map(one_field, (fields, ghost, diff, speed))


def heun_step(fields, ghost, diff, speed, solid):
    first = fields + component_rates(fields, ghost, diff, speed, solid)
    return 0.5 * fields + 0.5 * (first + component_rates(first, ghost, diff, speed, solid))


def reference(state, diffusivity, advection, solid_mask, iface_map):
    inlet = jnp.take(state[0][:, 0], iface_map, axis=1)
    backfeed = jnp.zeros_like(inlet).at[:, iface_map].set(state[1][:, 0])
    no_solid = jnp.zeros(state.shape[2:], bool)
    burner = heun_step(state[0], backfeed, diffusivity[0], -advection[0], no_solid)
    turbine = heun_step(state[1], inlet, diffusivity[1], advection[1], solid_mask == 1)
    return jnp.stack([burner, turbine])
```

```python
import functools

import jax
import jax.numpy as jnp
from jax import lax
from jax.experimental import pallas as pl
from jax.experimental.pallas import tpu as pltpu
from jax.sharding import PartitionSpec as P

RATIO = 1.5
GAIN = 0.4
BF = jnp.bfloat16
F32 = jnp.float32


def gain(q):
    return 0.5 * jnp.exp(GAIN * jnp.tanh(q))


def shift_matrix(nz):
    row = lax.broadcasted_iota(jnp.int32, (nz, 2 * nz), 0)
    col = lax.broadcasted_iota(jnp.int32, (nz, 2 * nz), 1)
    k = jnp.where(col < nz, col, col - nz)
    up = jnp.where(k + 1 == nz, 0, k + 1)
    down = jnp.where(k == 0, nz - 1, k - 1)
    one = lambda c: jnp.where(c, 1.0, 0.0)
    own = one(row == k)
    return jnp.where(col < nz, one(row == up) - own, own - one(row == down)).astype(BF)


def scalars(dif, adv, nf):
    comp = lax.axis_index("comp")
    sign = (2 * comp - 1).astype(F32)
    return [dif[comp, f] for f in range(nf)], [adv[comp, f] * sign for f in range(nf)], 2 - comp


def masks(solid):
    return jnp.where(solid, RATIO, 1.0), jnp.where(solid, 0.0, 0.5)


def section_kernel(dims, second, *refs):
    nf, nx, ny, nz = dims
    if second:
        dif, adv, base_ref, q_ref, s_ref, o_ref, fx, sm = refs
    else:
        dif, adv, q_ref, s_ref, o_ref, fx, sm = refs
    d, c, level = scalars(dif, adv, nf)
    fx[...] = jnp.zeros_like(fx)
    sm[...] = shift_matrix(nz)
    step_x = 2

    def at(x):
        return pl.ds(pl.multiple_of(x * ny, ny), ny)

    def step(i, gc):
        diffs = []
        for k in range(step_x):
            rows = q_ref[:, at(i * step_x + k)].astype(BF).reshape(nf * ny, nz)
            diffs.append(jnp.dot(rows, sm[...], preferred_element_type=F32))
        for k in range(step_x):
            x = i * step_x + k
            here, east, west = at(x), at(jnp.minimum(x + 1, nx - 1)), at(jnp.maximum(x - 1, 0))
            ge = gain(q_ref[4, east])
            gx, gy, gz = gc + ge, gc + pltpu.roll(gc, ny - 1, 0), gc + pltpu.roll(gc, nz - 1, 1)
            gzl = pltpu.roll(gz, 1, 1)
            m, a = masks(s_ref[here] >= level)
            for f in range(nf):
                q, qe, qw = q_ref[f, here], q_ref[f, east], q_ref[f, west]
                flux = gx * (qe - q)
                total = flux - fx[f]
                fx[f] = flux
                fy = gy * (pltpu.roll(q, ny - 1, 0) - q)
                total += fy - pltpu.roll(fy, 1, 0)
                z = diffs[k][f * ny : (f + 1) * ny]
                total += gz * z[:, :nz] - gzl * z[:, nz:]
                new = q + (d[f] * (m * total) - c[f] * (a * (qe - qw)))
                if second:
                    new = 0.5 * (base_ref[f, here] + new)
                o_ref[f, here] = new
            gc = ge
        return gc

    lax.fori_loop(0, nx // step_x, step, gain(q_ref[4, at(0)]))


def border_kernel(dims, two, *refs):
    nf, nx, ny, nz = dims
    if two:
        dif, adv, imap, q_ref, first_ref, main_ref, s_ref, a_ref, b_ref, c1_ref, c2l_ref, c2h_ref = refs[:12]
        rest = refs[12:]
    else:
        (dif, adv, imap, q_ref, first_ref, main_ref, s_ref, a_ref, b_ref, c1_ref, c2l_ref, c2h_ref,
         face_ref, map_ref) = refs[:14]
        rest = refs[14:]
    out_ref, sm, lay, cor, fl, fp, ol, strips, sem = rest
    d, c, level = scalars(dif, adv, nf)
    comp = lax.axis_index("comp")
    stream, last = lax.axis_index("gx"), lax.axis_size("gx") - 1
    even = stream % 2 == 0
    sm[...] = shift_matrix(nz)

    mids = []
    for f in range(nf):
        mids.append(pltpu.make_async_copy(
            main_ref.at[f, pl.ds(2, nx - 4), pl.ds(8, ny - 16)],
            out_ref.at[f, pl.ds(2, nx - 4), pl.ds(8, ny - 16)], sem.at[0, f]))
        mids[-1].start()
    cuts = []
    for k, row in enumerate((0, ny - 8)):
        cuts.append(pltpu.make_async_copy(main_ref.at[:, :, pl.ds(row, 8)], strips.at[k], sem.at[1, k]))
        cuts[-1].start()

    LF, LN, HN, HF = range(4)
    for f in range(nf):
        av = [a_ref[2 * f].astype(F32), a_ref[2 * f + 1].astype(F32)]
        bv = [b_ref[2 * f].astype(F32), b_ref[2 * f + 1].astype(F32)]
        lay[LF, f] = jnp.where(even, bv[0], av[0])
        lay[LN, f] = jnp.where(even, bv[1], av[1])
        zero = jnp.where(stream == last, 0.0, 1.0)
        lay[HN, f] = jnp.where(even, av[0], bv[0]) * zero
        lay[HF, f] = jnp.where(even, av[1], bv[1]) * zero
        lo, hi = c2l_ref[f, pl.ds(ny, 16)].astype(F32), c2h_ref[f, pl.ds(ny, 16)].astype(F32)
        lo_b, hi_b = c2l_ref[f, pl.ds(ny - 16, 16)].astype(F32), c2h_ref[f, pl.ds(0, 16)].astype(F32)
        cor[0, f : f + 1] = jnp.where(even, lo[5:6], lo[3:4])
        cor[1, f : f + 1] = jnp.where(even, hi[4:5], hi[2:3])
        cor[2, f : f + 1] = jnp.where(even, lo[1:2], lo_b[15:16]) * zero
        cor[3, f : f + 1] = jnp.where(even, hi[0:1], hi_b[0:1]) * zero

    @pl.when(stream == 0)
    def _():
        start = lax.axis_index("gy") * ny
        if two:
            whole = 2 * ny
            mine = jnp.broadcast_to(imap[...].astype(F32), (1, ny))
            other = c2l_ref[0, pl.ds(ny, 16)].astype(F32)[6:7, :ny]
            mapping = jnp.concatenate([mine, other], axis=1)
            order = start
        else:
            whole = face_ref.shape[1]
            mapping = map_ref[...].astype(F32)
            order = 0
        rows = 40
        r = lax.broadcasted_iota(jnp.int32, (rows, whole), 0)
        want = jnp.where(r < ny, r, jnp.where(r == ny, whole - 1, ny)) + start
        want = jnp.where(want >= whole, want - whole, want).astype(F32)
        t = lax.broadcasted_iota(jnp.int32, (rows, whole), 1) + order
        t = jnp.where(t >= whole, t - whole, t).astype(F32)
        u = lax.broadcasted_iota(jnp.int32, (whole, whole), 0) + order
        u = jnp.where(u >= whole, u - whole, u).astype(F32)
        one = lambda x: jnp.where(x, 1.0, 0.0)
        pick = one(t == want).astype(BF)
        targets = one(jnp.broadcast_to(mapping, (whole, whole)) == u).astype(BF)
        inlet = lax.dot_general(pick, targets, (((1,), (1,)), ((), ())), preferred_element_type=F32)
        feed = one(jnp.broadcast_to(mapping, (rows, whole)) == want)
        choose = jnp.where(comp == 1, inlet, feed).astype(BF)
        for f in range(nf):
            if two:
                layer = jnp.concatenate([b_ref[2 * f], c2l_ref[f, pl.ds(0, ny)]], axis=0)
            else:
                layer = face_ref[f]
            ghost = jnp.dot(choose, layer, preferred_element_type=F32)
            lay[LN, f] = ghost[:ny]
            cor[0, f : f + 1] = ghost[ny : ny + 1]
            cor[1, f : f + 1] = ghost[ny + 1 : ny + 2]

    row = lax.broadcasted_iota(jnp.int32, (ny, nz), 0)

    def slab(center, before, after, low, high, solid, along_outer):
        rows = jnp.concatenate([center(f).astype(BF) for f in range(nf)], axis=0)
        diffs = jnp.dot(rows, sm[...], preferred_element_type=F32)

        def ups(v, h):
            return jnp.where(row == ny - 1, h, pltpu.roll(v, ny - 1, 0))

        def downs(v, l):
            return jnp.where(row == 0, l, pltpu.roll(v, 1, 0))

        g = gain(center(4))
        gb, ga = g + gain(before(4)), g + gain(after(4))
        gu, gd = g + ups(g, gain(high(4))), g + downs(g, gain(low(4)))
        gz = g + pltpu.roll(g, nz - 1, 1)
        gzl = pltpu.roll(gz, 1, 1)
        m, a = masks(solid)
        res = []
        for f in range(nf):
            q = center(f)
            qa, qb = after(f), before(f)
            qu, qd = ups(q, high(f)), downs(q, low(f))
            z = diffs[f * ny : (f + 1) * ny]
            total = ga * (qa - q) - gb * (q - qb) + (gu * (qu - q) - gd * (q - qd))
            total += gz * z[:, :nz] - gzl * z[:, nz:]
            grad = qa - qb if along_outer else qu - qd
            res.append(q + (d[f] * (m * total) - c[f] * (a * grad)))
        return res

    def q_layer(x):
        return lambda f: q_ref[f, x * ny : (x + 1) * ny]

    def q_plane(y):
        return lambda f: q_ref[f, pl.ds(y, nx, stride=ny)]

    def halo(k):
        return lambda f: lay[k, f]

    def corner(k):
        return lambda f: cor[k, f : f + 1]

    plane = {-2: 2 * nf + 1, -1: 3 * nf + 1, ny: 0, ny + 1: nf}

    def c_plane(y):
        return lambda f: c1_ref[plane[y] + f].astype(F32)

    def line(src, k):
        return lambda f: src(f)[k : k + 1]

    s_lay = lambda x: s_ref[x * ny : (x + 1) * ny] >= level
    s_pla = lambda y: s_ref[pl.ds(y, nx, stride=ny)] >= level
    level_f = level.astype(F32)
    m_low = jnp.where(even, b_ref[2 * nf], a_ref[2 * nf]).astype(F32) >= level_f
    m_high = jnp.where(even, a_ref[2 * nf], b_ref[2 * nf]).astype(F32) >= level_f

    def put(dst, k, vals):
        for f in range(nf):
            dst[k, f] = vals[f]

    put(fl, 0, slab(halo(LN), halo(LF), q_layer(0), corner(0), corner(1), m_low, True))

    @pl.when(stream == 0)
    def _():
        for f in range(nf):
            fl[0, f] = lay[LN, f]

    def y_line(y, x):
        return lambda f: c1_ref[plane[y] + f, pl.ds(x // 16 * 16, 16)].astype(F32)[x % 16 : x % 16 + 1]

    put(fl, 1, slab(q_layer(0), halo(LN), q_layer(1), y_line(-1, 0), y_line(ny, 0), s_lay(0), True))
    put(fl, 6, slab(q_layer(nx - 1), q_layer(nx - 2), halo(HN), y_line(-1, nx - 1), y_line(ny, nx - 1),
                    s_lay(nx - 1), True))
    put(fl, 7, slab(halo(HN), q_layer(nx - 1), halo(HF), corner(2), corner(3), m_high, True))

    @pl.when(stream == last)
    def _():
        for f in range(nf):
            fl[7, f] = jnp.zeros((ny, nz), F32)

    put(fp, 0, slab(c_plane(-1), c_plane(-2), q_plane(0), corner(0), corner(2),
                    c1_ref[4 * nf + 1].astype(F32) >= level_f, False))
    put(fp, 1, slab(q_plane(0), c_plane(-1), q_plane(1), line(halo(LN), 0), line(halo(HN), 0), s_pla(0), False))
    put(fp, 6, slab(q_plane(ny - 1), q_plane(ny - 2), c_plane(ny), line(halo(LN), ny - 1),
                    line(halo(HN), ny - 1), s_pla(ny - 1), False))
    put(fp, 7, slab(c_plane(ny), q_plane(ny - 1), c_plane(ny + 1), corner(1), corner(3),
                    c1_ref[2 * nf].astype(F32) >= level_f, False))

    for f in range(nf):
        for k, x in ((2, 1), (3, 2), (4, nx - 3), (5, nx - 2)):
            fl[k, f] = first_ref[f, x * ny : (x + 1) * ny]
            fl[k, f, 0:1] = fp[1, f, x : x + 1]
            fl[k, f, ny - 1 : ny] = fp[6, f, x : x + 1]
        for k, y in ((2, 1), (3, 2), (4, ny - 3), (5, ny - 2)):
            fp[k, f] = first_ref[f, pl.ds(y, nx, stride=ny)]
            fp[k, f, 0:1] = fl[1, f, y : y + 1]
            fp[k, f, nx - 1 : nx] = fl[6, f, y : y + 1]

    def got(src, k):
        return lambda f: src[k, f]

    def got_line(src, k, r):
        return lambda f: src[k, f, r : r + 1]

    layers = []
    for k, (n, x) in enumerate(((1, 0), (2, 1), (5, nx - 2), (6, nx - 1))):
        vals = slab(got(fl, n), got(fl, n - 1), got(fl, n + 1), got_line(fp, 0, x), got_line(fp, 7, x), s_lay(x), True)
        for f in range(nf):
            ol[k, f] = 0.5 * (q_layer(x)(f) + vals[f])
        layers.append(pltpu.make_async_copy(ol.at[k], out_ref.at[:, x], sem.at[2, k]))
        layers[-1].start()
    for copy in cuts:
        copy.wait()
    edges = []
    for k, (n, y, side, r) in enumerate(((1, 0, 0, 0), (2, 1, 0, 1), (5, ny - 2, 1, 6), (6, ny - 1, 1, 7))):
        vals = slab(got(fp, n), got(fp, n - 1), got(fp, n + 1), got_line(fl, 0, y), got_line(fl, 7, y), s_pla(y), False)
        for f in range(nf):
            strips[side, f, :, r] = 0.5 * (q_plane(y)(f) + vals[f])
        if k % 2:
            edges.append(pltpu.make_async_copy(
                strips.at[side, :, pl.ds(2, nx - 4)],
                out_ref.at[:, pl.ds(2, nx - 4), pl.ds(side * (ny - 8), 8)], sem.at[3, side]))
            edges[-1].start()
    for copy in mids + layers + edges:
        copy.wait()


VM = pl.BlockSpec(memory_space=pltpu.VMEM)
SM = pl.BlockSpec(memory_space=pltpu.SMEM)
HB = pl.BlockSpec(memory_space=pl.ANY)


def body(sizes, state, diffusivity, advection, solid_mask, iface_map):
    ngx, ngy = sizes
    q = state[0]
    nf, nx, ny, nz = q.shape
    dims = nf, nx, ny, nz
    two = ngy == 2
    even = lax.axis_index("gx") % 2 == 0

    def planes(rows, solid_row):
        return jnp.concatenate([q[:, :, r] for r in rows] + [solid_mask[None, :, solid_row].astype(F32)], 0).astype(BF)

    if two:
        swap = [(0, 1), (1, 0)]
        c1 = lax.ppermute(jnp.concatenate([planes((0, 1), 0), planes((ny - 2, ny - 1), ny - 1)], 0), "gy", swap)
    else:
        up = [(j, (j + 1) % ngy) for j in range(ngy)]
        down = [(b, a) for a, b in up]
        c1 = jnp.concatenate([lax.ppermute(planes((0, 1), 0), "gy", down),
                              lax.ppermute(planes((ny - 2, ny - 1), ny - 1), "gy", up)], 0)

    def layers(at_end):
        start = jnp.where(at_end, nx - 2, 0)
        edge = jnp.where(at_end, nx - 1, 0)
        fields = lax.dynamic_slice_in_dim(q, start, 2, 1).reshape(2 * nf, ny, nz)
        solid = lax.dynamic_slice_in_dim(solid_mask, edge, 1, 0)
        return jnp.concatenate([fields, solid.astype(F32)], 0).astype(BF)

    def both(pairs):
        return pairs + [(b, a) for a, b in pairs]

    inner = both([(k, k + 1) for k in range(0, ngx, 2)])
    a = lax.ppermute(layers(even), "gx", inner)
    outer = [(k * ngx + i, k * ngx + i + 1) for k in range(2) for i in range(1, ngx - 1, 2)]
    b = lax.ppermute(layers(~even), ("comp", "gx"), both(outer + [(0, ngx)]))

    a4, b4 = a[: 2 * nf].reshape(nf, 2, ny, nz), b[: 2 * nf].reshape(nf, 2, ny, nz)
    map_row = jnp.pad(iface_map.astype(BF), (0, nz - ny)).reshape(1, 1, nz)
    pick = lambda v, l: [v[:, l, 0:1], v[:, l, ny - 1 : ny]]
    extra = jnp.concatenate(
        [b4[:, 0]] + pick(a4, 0) + pick(a4, 1) + pick(b4, 1)
        + [jnp.broadcast_to(map_row, (nf, 1, nz)), jnp.zeros((nf, 9, nz), BF)], 1)
    if two:
        c2 = lax.ppermute(extra, "gy", swap)
        c2l, c2h, more = c2, c2, []
    else:
        c2l, c2h = lax.ppermute(extra, "gy", up), lax.ppermute(extra, "gy", down)
        more = [lax.all_gather(b4[:, 0], "gy", axis=1, tiled=True),
                lax.all_gather(iface_map, "gy", axis=0, tiled=True).reshape(1, -1)]

    flat = q.reshape(nf, nx * ny, nz)
    solid = solid_mask.reshape(nx * ny, nz)
    shape = jax.ShapeDtypeStruct((nf, nx * ny, nz), F32)
    cells = nf * nx * ny * nz

    def section(second, *args):
        return pl.pallas_call(
            functools.partial(section_kernel, dims, second),
            out_shape=shape,
            in_specs=[SM, SM] + [VM] * (len(args) + 1),
            out_specs=VM,
            scratch_shapes=[pltpu.VMEM((nf, ny, nz), F32), pltpu.VMEM((nz, 2 * nz), BF)],
            compiler_params=pltpu.CompilerParams(vmem_limit_bytes=20 << 20),
            cost_estimate=pl.CostEstimate(flops=20 * cells, bytes_accessed=8 * cells, transcendentals=cells // 4),
        )(diffusivity, advection, *args, solid)

    first = section(False, flat)
    main = section(True, flat, first)
    mb = pltpu.VMEM
    return pl.pallas_call(
        functools.partial(border_kernel, dims, two),
        out_shape=jax.ShapeDtypeStruct((nf, nx, ny, nz), F32),
        in_specs=[SM, SM, VM] + [VM] * (9 + len(more)),
        out_specs=HB,
        scratch_shapes=[
            mb((nz, 2 * nz), BF), mb((4, nf, ny, nz), F32), mb((4, 8, nz), F32), mb((8, nf, ny, nz), F32),
            mb((8, nf, nx, nz), F32), mb((4, nf, ny, nz), F32), mb((2, nf, nx, 8, nz), F32),
            pltpu.SemaphoreType.DMA((4, 8)),
        ],
        compiler_params=pltpu.CompilerParams(vmem_limit_bytes=40 << 20),
        cost_estimate=pl.CostEstimate(flops=10 * cells, bytes_accessed=8 * cells, transcendentals=cells // 4),
    )(diffusivity, advection, iface_map.reshape(1, ny), flat, first, main.reshape(nf, nx, ny, nz), solid,
      a, b, c1, c2l, c2h, *more)[None]


def solution(mesh):
    sizes = mesh.shape["gx"], mesh.shape["gy"]
    return jax.shard_map(
        functools.partial(body, sizes),
        mesh=mesh,
        in_specs=(P("comp", None, "gx", "gy", None), P(), P(), P("gx", "gy", None), P("gy")),
        out_specs=P("comp", None, "gx", "gy", None),
        check_vma=False,
    )
```

```python
import functools

import jax
import jax.numpy as jnp
from jax import lax
from jax.experimental import pallas as pl
from jax.experimental.pallas import tpu as pltpu
from jax.sharding import PartitionSpec as P

RATIO = 1.5
GAIN = 0.4
BF = jnp.bfloat16
F32 = jnp.float32


def gain(q):
    return 0.5 * jnp.exp(GAIN * jnp.tanh(q))


def shift_matrix(nz):
    row = lax.broadcasted_iota(jnp.int32, (nz, 2 * nz), 0)
    col = lax.broadcasted_iota(jnp.int32, (nz, 2 * nz), 1)
    k = jnp.where(col < nz, col, col - nz)
    up = jnp.where(k + 1 == nz, 0, k + 1)
    down = jnp.where(k == 0, nz - 1, k - 1)
    one = lambda c: jnp.where(c, 1.0, 0.0)
    own = one(row == k)
    return jnp.where(col < nz, one(row == up) - own, own - one(row == down)).astype(BF)


def scalars(dif, adv, nf):
    comp = lax.axis_index("comp")
    sign = (2 * comp - 1).astype(F32)
    return [dif[comp, f] for f in range(nf)], [adv[comp, f] * sign for f in range(nf)], 2 - comp


def masks(solid):
    return jnp.where(solid, RATIO, 1.0), jnp.where(solid, 0.0, 0.5)


def gather_kernel(dims, q_ref, s_ref, a_ref, b_ref, c_ref):
    nf, nx, ny, nz = dims
    even = lax.axis_index("gx") % 2 == 0
    def layer(ref, f, k):
        at = pl.multiple_of(k * ny, ny)
        return (ref[pl.ds(at, ny)] if f is None else ref[f, pl.ds(at, ny)]).astype(F32).astype(BF)

    a0, b0 = jnp.where(even, nx - 2, 0), jnp.where(even, 0, nx - 2)
    a1, b1 = jnp.where(even, nx - 1, 0), jnp.where(even, 0, nx - 1)
    for f in range(nf):
        for k in range(2):
            a_ref[2 * f + k] = layer(q_ref, f, a0 + k)
            b_ref[2 * f + k] = layer(q_ref, f, b0 + k)
        for k, y in enumerate((0, 1, ny - 2, ny - 1)):
            c_ref[k * nf + k // 2 + f] = q_ref[f, pl.ds(y, nx, stride=ny)].astype(BF)
    a_ref[2 * nf] = layer(s_ref, None, a1)
    b_ref[2 * nf] = layer(s_ref, None, b1)
    for k, y in ((2 * nf, 0), (4 * nf + 1, ny - 1)):
        c_ref[k] = s_ref[pl.ds(y, nx, stride=ny)].astype(F32).astype(BF)


def relay_kernel(dims, imap, a_ref, b_ref, o_ref, rows):
    nf, nx, ny, nz = dims
    rows[...] = jnp.zeros_like(rows)
    rows[6:7, :ny] = imap[...].astype(F32)
    for f in range(nf):
        o_ref[f, :ny] = b_ref[2 * f]
        for k, (src, n) in enumerate(((a_ref, 2 * f), (a_ref, 2 * f + 1), (b_ref, 2 * f + 1))):
            block = src[n].astype(F32)
            rows[2 * k : 2 * k + 1] = block[:1]
            rows[2 * k + 1 : 2 * k + 2] = block[ny - 1 :]
        o_ref[f, ny:] = rows[...].astype(BF)


def section_kernel(dims, second, *refs):
    nf, nx, ny, nz = dims
    if second:
        dif, adv, base_ref, q_ref, s_ref, o_ref, fx, sm = refs
    else:
        dif, adv, q_ref, s_ref, o_ref, fx, sm = refs
    d, c, level = scalars(dif, adv, nf)
    fx[...] = jnp.zeros_like(fx)
    sm[...] = shift_matrix(nz)
    step_x = 2

    def at(x):
        return pl.ds(pl.multiple_of(x * ny, ny), ny)

    def step(i, gc):
        diffs = []
        for k in range(step_x):
            rows = q_ref[:, at(i * step_x + k)].astype(BF).reshape(nf * ny, nz)
            diffs.append(jnp.dot(rows, sm[...], preferred_element_type=F32))
        for k in range(step_x):
            x = i * step_x + k
            here, east, west = at(x), at(jnp.minimum(x + 1, nx - 1)), at(jnp.maximum(x - 1, 0))
            ge = gain(q_ref[4, east])
            gx, gy, gz = gc + ge, gc + pltpu.roll(gc, ny - 1, 0), gc + pltpu.roll(gc, nz - 1, 1)
            gzl = pltpu.roll(gz, 1, 1)
            m, a = masks(s_ref[here] >= level)
            for f in range(nf):
                q, qe, qw = q_ref[f, here], q_ref[f, east], q_ref[f, west]
                flux = gx * (qe - q)
                total = flux - fx[f]
                fx[f] = flux
                fy = gy * (pltpu.roll(q, ny - 1, 0) - q)
                total += fy - pltpu.roll(fy, 1, 0)
                z = diffs[k][f * ny : (f + 1) * ny]
                total += gz * z[:, :nz] - gzl * z[:, nz:]
                new = q + (d[f] * (m * total) - c[f] * (a * (qe - qw)))
                if second:
                    new = 0.5 * (base_ref[f, here] + new)
                o_ref[f, here] = new
            gc = ge
        return gc

    lax.fori_loop(0, nx // step_x, step, gain(q_ref[4, at(0)]))


def border_kernel(dims, two, *refs):
    nf, nx, ny, nz = dims
    if two:
        dif, adv, imap, q_ref, first_ref, main_ref, s_ref, a_ref, b_ref, c1_ref, c2l_ref, c2h_ref = refs[:12]
        rest = refs[12:]
    else:
        (dif, adv, imap, q_ref, first_ref, main_ref, s_ref, a_ref, b_ref, c1_ref, c2l_ref, c2h_ref,
         face_ref, map_ref) = refs[:14]
        rest = refs[14:]
    out_ref, sm, lay, cor, fl, fp, ol, strips, sem = rest
    d, c, level = scalars(dif, adv, nf)
    comp = lax.axis_index("comp")
    stream, last = lax.axis_index("gx"), lax.axis_size("gx") - 1
    even = stream % 2 == 0
    sm[...] = shift_matrix(nz)

    mids = []
    for f in range(nf):
        mids.append(pltpu.make_async_copy(
            main_ref.at[f, pl.ds(2, nx - 4), pl.ds(8, ny - 16)],
            out_ref.at[f, pl.ds(2, nx - 4), pl.ds(8, ny - 16)], sem.at[0, f]))
        mids[-1].start()
    cuts = []
    for k, row in enumerate((0, ny - 8)):
        cuts.append(pltpu.make_async_copy(main_ref.at[:, :, pl.ds(row, 8)], strips.at[k], sem.at[1, k]))
        cuts[-1].start()

    LF, LN, HN, HF = range(4)
    for f in range(nf):
        av = [a_ref[2 * f].astype(F32), a_ref[2 * f + 1].astype(F32)]
        bv = [b_ref[2 * f].astype(F32), b_ref[2 * f + 1].astype(F32)]
        lay[LF, f] = jnp.where(even, bv[0], av[0])
        lay[LN, f] = jnp.where(even, bv[1], av[1])
        zero = jnp.where(stream == last, 0.0, 1.0)
        lay[HN, f] = jnp.where(even, av[0], bv[0]) * zero
        lay[HF, f] = jnp.where(even, av[1], bv[1]) * zero
        lo, hi = c2l_ref[f, pl.ds(ny, 16)].astype(F32), c2h_ref[f, pl.ds(ny, 16)].astype(F32)
        lo_b, hi_b = c2l_ref[f, pl.ds(ny - 16, 16)].astype(F32), c2h_ref[f, pl.ds(0, 16)].astype(F32)
        cor[0, f : f + 1] = jnp.where(even, lo[5:6], lo[3:4])
        cor[1, f : f + 1] = jnp.where(even, hi[4:5], hi[2:3])
        cor[2, f : f + 1] = jnp.where(even, lo[1:2], lo_b[15:16]) * zero
        cor[3, f : f + 1] = jnp.where(even, hi[0:1], hi_b[0:1]) * zero

    @pl.when(stream == 0)
    def _():
        start = lax.axis_index("gy") * ny
        if two:
            whole = 2 * ny
            mine = jnp.broadcast_to(imap[...].astype(F32), (1, ny))
            other = c2l_ref[0, pl.ds(ny, 16)].astype(F32)[6:7, :ny]
            mapping = jnp.concatenate([mine, other], axis=1)
            order = start
        else:
            whole = face_ref.shape[1]
            mapping = map_ref[...].astype(F32)
            order = 0
        rows = 40
        r = lax.broadcasted_iota(jnp.int32, (rows, whole), 0)
        want = jnp.where(r < ny, r, jnp.where(r == ny, whole - 1, ny)) + start
        want = jnp.where(want >= whole, want - whole, want).astype(F32)
        t = lax.broadcasted_iota(jnp.int32, (rows, whole), 1) + order
        t = jnp.where(t >= whole, t - whole, t).astype(F32)
        u = lax.broadcasted_iota(jnp.int32, (whole, whole), 0) + order
        u = jnp.where(u >= whole, u - whole, u).astype(F32)
        one = lambda x: jnp.where(x, 1.0, 0.0)
        pick = one(t == want).astype(BF)
        targets = one(jnp.broadcast_to(mapping, (whole, whole)) == u).astype(BF)
        inlet = lax.dot_general(pick, targets, (((1,), (1,)), ((), ())), preferred_element_type=F32)
        feed = one(jnp.broadcast_to(mapping, (rows, whole)) == want)
        choose = jnp.where(comp == 1, inlet, feed).astype(BF)
        for f in range(nf):
            if two:
                layer = jnp.concatenate([b_ref[2 * f], c2l_ref[f, pl.ds(0, ny)]], axis=0)
            else:
                layer = face_ref[f]
            ghost = jnp.dot(choose, layer, preferred_element_type=F32)
            lay[LN, f] = ghost[:ny]
            cor[0, f : f + 1] = ghost[ny : ny + 1]
            cor[1, f : f + 1] = ghost[ny + 1 : ny + 2]

    row = lax.broadcasted_iota(jnp.int32, (ny, nz), 0)

    def slab(center, before, after, low, high, solid, along_outer):
        rows = jnp.concatenate([center(f).astype(BF) for f in range(nf)], axis=0)
        diffs = jnp.dot(rows, sm[...], preferred_element_type=F32)

        def ups(v, h):
            return jnp.where(row == ny - 1, h, pltpu.roll(v, ny - 1, 0))

        def downs(v, l):
            return jnp.where(row == 0, l, pltpu.roll(v, 1, 0))

        g = gain(center(4))
        gb, ga = g + gain(before(4)), g + gain(after(4))
        gu, gd = g + ups(g, gain(high(4))), g + downs(g, gain(low(4)))
        gz = g + pltpu.roll(g, nz - 1, 1)
        gzl = pltpu.roll(gz, 1, 1)
        m, a = masks(solid)
        res = []
        for f in range(nf):
            q = center(f)
            qa, qb = after(f), before(f)
            qu, qd = ups(q, high(f)), downs(q, low(f))
            z = diffs[f * ny : (f + 1) * ny]
            total = ga * (qa - q) - gb * (q - qb) + (gu * (qu - q) - gd * (q - qd))
            total += gz * z[:, :nz] - gzl * z[:, nz:]
            grad = qa - qb if along_outer else qu - qd
            res.append(q + (d[f] * (m * total) - c[f] * (a * grad)))
        return res

    def q_layer(x):
        return lambda f: q_ref[f, x * ny : (x + 1) * ny]

    def q_plane(y):
        return lambda f: q_ref[f, pl.ds(y, nx, stride=ny)]

    def halo(k):
        return lambda f: lay[k, f]

    def corner(k):
        return lambda f: cor[k, f : f + 1]

    plane = {-2: 2 * nf + 1, -1: 3 * nf + 1, ny: 0, ny + 1: nf}

    def c_plane(y):
        return lambda f: c1_ref[plane[y] + f].astype(F32)

    def line(src, k):
        return lambda f: src(f)[k : k + 1]

    s_lay = lambda x: s_ref[x * ny : (x + 1) * ny] >= level
    s_pla = lambda y: s_ref[pl.ds(y, nx, stride=ny)] >= level
    level_f = level.astype(F32)
    m_low = jnp.where(even, b_ref[2 * nf], a_ref[2 * nf]).astype(F32) >= level_f
    m_high = jnp.where(even, a_ref[2 * nf], b_ref[2 * nf]).astype(F32) >= level_f

    def put(dst, k, vals):
        for f in range(nf):
            dst[k, f] = vals[f]

    put(fl, 0, slab(halo(LN), halo(LF), q_layer(0), corner(0), corner(1), m_low, True))

    @pl.when(stream == 0)
    def _():
        for f in range(nf):
            fl[0, f] = lay[LN, f]

    def y_line(y, x):
        return lambda f: c1_ref[plane[y] + f, pl.ds(x // 16 * 16, 16)].astype(F32)[x % 16 : x % 16 + 1]

    put(fl, 1, slab(q_layer(0), halo(LN), q_layer(1), y_line(-1, 0), y_line(ny, 0), s_lay(0), True))
    put(fl, 6, slab(q_layer(nx - 1), q_layer(nx - 2), halo(HN), y_line(-1, nx - 1), y_line(ny, nx - 1),
                    s_lay(nx - 1), True))
    put(fl, 7, slab(halo(HN), q_layer(nx - 1), halo(HF), corner(2), corner(3), m_high, True))

    @pl.when(stream == last)
    def _():
        for f in range(nf):
            fl[7, f] = jnp.zeros((ny, nz), F32)

    put(fp, 0, slab(c_plane(-1), c_plane(-2), q_plane(0), corner(0), corner(2),
                    c1_ref[4 * nf + 1].astype(F32) >= level_f, False))
    put(fp, 1, slab(q_plane(0), c_plane(-1), q_plane(1), line(halo(LN), 0), line(halo(HN), 0), s_pla(0), False))
    put(fp, 6, slab(q_plane(ny - 1), q_plane(ny - 2), c_plane(ny), line(halo(LN), ny - 1),
                    line(halo(HN), ny - 1), s_pla(ny - 1), False))
    put(fp, 7, slab(c_plane(ny), q_plane(ny - 1), c_plane(ny + 1), corner(1), corner(3),
                    c1_ref[2 * nf].astype(F32) >= level_f, False))

    for f in range(nf):
        for k, x in ((2, 1), (3, 2), (4, nx - 3), (5, nx - 2)):
            fl[k, f] = first_ref[f, x * ny : (x + 1) * ny]
            fl[k, f, 0:1] = fp[1, f, x : x + 1]
            fl[k, f, ny - 1 : ny] = fp[6, f, x : x + 1]
        for k, y in ((2, 1), (3, 2), (4, ny - 3), (5, ny - 2)):
            fp[k, f] = first_ref[f, pl.ds(y, nx, stride=ny)]
            fp[k, f, 0:1] = fl[1, f, y : y + 1]
            fp[k, f, nx - 1 : nx] = fl[6, f, y : y + 1]

    def got(src, k):
        return lambda f: src[k, f]

    def got_line(src, k, r):
        return lambda f: src[k, f, r : r + 1]

    layers = []
    for k, (n, x) in enumerate(((1, 0), (2, 1), (5, nx - 2), (6, nx - 1))):
        vals = slab(got(fl, n), got(fl, n - 1), got(fl, n + 1), got_line(fp, 0, x), got_line(fp, 7, x), s_lay(x), True)
        for f in range(nf):
            ol[k, f] = 0.5 * (q_layer(x)(f) + vals[f])
        layers.append(pltpu.make_async_copy(ol.at[k], out_ref.at[:, x], sem.at[2, k]))
        layers[-1].start()
    for copy in cuts:
        copy.wait()
    edges = []
    for k, (n, y, side, r) in enumerate(((1, 0, 0, 0), (2, 1, 0, 1), (5, ny - 2, 1, 6), (6, ny - 1, 1, 7))):
        vals = slab(got(fp, n), got(fp, n - 1), got(fp, n + 1), got_line(fl, 0, y), got_line(fl, 7, y), s_pla(y), False)
        for f in range(nf):
            strips[side, f, :, r] = 0.5 * (q_plane(y)(f) + vals[f])
        if k % 2:
            edges.append(pltpu.make_async_copy(
                strips.at[side, :, pl.ds(2, nx - 4)],
                out_ref.at[:, pl.ds(2, nx - 4), pl.ds(side * (ny - 8), 8)], sem.at[3, side]))
            edges[-1].start()
    for copy in mids + layers + edges:
        copy.wait()


VM = pl.BlockSpec(memory_space=pltpu.VMEM)
SM = pl.BlockSpec(memory_space=pltpu.SMEM)
HB = pl.BlockSpec(memory_space=pl.ANY)


def body(sizes, state, diffusivity, advection, solid_mask, iface_map):
    ngx, ngy = sizes
    q = state[0]
    nf, nx, ny, nz = q.shape
    dims = nf, nx, ny, nz
    two = ngy == 2

    flat, solid = q.reshape(nf, nx * ny, nz), solid_mask.reshape(nx * ny, nz)
    send_a, send_b, send_c = pl.pallas_call(
        functools.partial(gather_kernel, dims),
        out_shape=[jax.ShapeDtypeStruct((n, ny, nz), BF) for n in (2 * nf + 1, 2 * nf + 1, 4 * nf + 2)],
        in_specs=[VM] * 2,
        out_specs=[VM] * 3,
        compiler_params=pltpu.CompilerParams(vmem_limit_bytes=2 << 20),
    )(flat, solid)

    if two:
        swap = [(0, 1), (1, 0)]
        c1 = lax.ppermute(send_c, "gy", swap)
    else:
        up = [(j, (j + 1) % ngy) for j in range(ngy)]
        down = [(b, a) for a, b in up]
        half = 2 * nf + 1
        c1 = jnp.concatenate([lax.ppermute(send_c[:half], "gy", down), lax.ppermute(send_c[half:], "gy", up)], 0)

    def both(pairs):
        return pairs + [(b, a) for a, b in pairs]

    inner = both([(k, k + 1) for k in range(0, ngx, 2)])
    a = lax.ppermute(send_a, "gx", inner)
    outer = [(k * ngx + i, k * ngx + i + 1) for k in range(2) for i in range(1, ngx - 1, 2)]
    b = lax.ppermute(send_b, ("comp", "gx"), both(outer + [(0, ngx)]))

    map_line = iface_map.reshape(1, ny)
    extra = pl.pallas_call(
        functools.partial(relay_kernel, dims),
        out_shape=jax.ShapeDtypeStruct((nf, ny + 16, nz), BF),
        in_specs=[VM] * 3,
        out_specs=VM,
        scratch_shapes=[pltpu.VMEM((16, nz), F32)],
        compiler_params=pltpu.CompilerParams(vmem_limit_bytes=1 << 20),
    )(map_line, a, b)
    if two:
        c2 = lax.ppermute(extra, "gy", swap)
        c2l, c2h, more = c2, c2, []
    else:
        c2l, c2h = lax.ppermute(extra, "gy", up), lax.ppermute(extra, "gy", down)
        more = [lax.all_gather(b[: 2 * nf : 2], "gy", axis=1, tiled=True),
                lax.all_gather(iface_map, "gy", axis=0, tiled=True).reshape(1, -1)]

    shape = jax.ShapeDtypeStruct((nf, nx * ny, nz), F32)
    cells = nf * nx * ny * nz

    def section(second, *args):
        return pl.pallas_call(
            functools.partial(section_kernel, dims, second),
            out_shape=shape,
            in_specs=[SM, SM] + [VM] * (len(args) + 1),
            out_specs=VM,
            scratch_shapes=[pltpu.VMEM((nf, ny, nz), F32), pltpu.VMEM((nz, 2 * nz), BF)],
            compiler_params=pltpu.CompilerParams(vmem_limit_bytes=3 << 20),
            cost_estimate=pl.CostEstimate(flops=20 * cells, bytes_accessed=8 * cells, transcendentals=cells // 4),
        )(diffusivity, advection, *args, solid)

    first = section(False, flat)
    main = section(True, flat, first)
    mb = pltpu.VMEM
    return pl.pallas_call(
        functools.partial(border_kernel, dims, two),
        out_shape=jax.ShapeDtypeStruct((nf, nx, ny, nz), F32),
        in_specs=[SM, SM, VM] + [VM] * (9 + len(more)),
        out_specs=HB,
        scratch_shapes=[
            mb((nz, 2 * nz), BF), mb((4, nf, ny, nz), F32), mb((4, 8, nz), F32), mb((8, nf, ny, nz), F32),
            mb((8, nf, nx, nz), F32), mb((4, nf, ny, nz), F32), mb((2, nf, nx, 8, nz), F32),
            pltpu.SemaphoreType.DMA((4, 8)),
        ],
        compiler_params=pltpu.CompilerParams(vmem_limit_bytes=10 << 20),
        cost_estimate=pl.CostEstimate(flops=10 * cells, bytes_accessed=8 * cells, transcendentals=cells // 4),
    )(diffusivity, advection, map_line, flat, first, main.reshape(nf, nx, ny, nz), solid,
      a, b, c1, c2l, c2h, *more)[None]


def solution(mesh):
    sizes = mesh.shape["gx"], mesh.shape["gy"]
    return jax.shard_map(
        functools.partial(body, sizes),
        mesh=mesh,
        in_specs=(P("comp", None, "gx", "gy", None), P(), P(), P("gx", "gy", None), P("gy")),
        out_specs=P("comp", None, "gx", "gy", None),
        check_vma=False,
    )
```

```python
import functools

import jax
import jax.numpy as jnp
from jax import lax
from jax.experimental import pallas as pl
from jax.experimental.pallas import tpu as pltpu
from jax.sharding import PartitionSpec as P

RATIO = 1.5
GAIN = 0.4
BF = jnp.bfloat16
F32 = jnp.float32


def gain(q):
    return 0.5 * jnp.exp(GAIN * jnp.tanh(q))


def shift_matrix(nz):
    row = lax.broadcasted_iota(jnp.int32, (nz, 2 * nz), 0)
    col = lax.broadcasted_iota(jnp.int32, (nz, 2 * nz), 1)
    k = jnp.where(col < nz, col, col - nz)
    up = jnp.where(k + 1 == nz, 0, k + 1)
    down = jnp.where(k == 0, nz - 1, k - 1)
    one = lambda c: jnp.where(c, 1.0, 0.0)
    own = one(row == k)
    return jnp.where(col < nz, one(row == up) - own, own - one(row == down)).astype(BF)


def scalars(dif, adv, nf):
    comp = lax.axis_index("comp")
    sign = (2 * comp - 1).astype(F32)
    return [dif[comp, f] for f in range(nf)], [adv[comp, f] * sign for f in range(nf)], 2 - comp


def masks(solid):
    return jnp.where(solid, RATIO, 1.0), jnp.where(solid, 0.0, 0.5)


def gather_kernel(dims, q_ref, s_ref, a_ref, b_ref, c_ref):
    nf, nx, ny, nz = dims
    even = lax.axis_index("gx") % 2 == 0
    def layer(ref, f, k):
        at = pl.multiple_of(k * ny, ny)
        return (ref[pl.ds(at, ny)] if f is None else ref[f, pl.ds(at, ny)]).astype(F32).astype(BF)

    a0, b0 = jnp.where(even, nx - 2, 0), jnp.where(even, 0, nx - 2)
    a1, b1 = jnp.where(even, nx - 1, 0), jnp.where(even, 0, nx - 1)
    for f in range(nf):
        for k in range(2):
            a_ref[2 * f + k] = layer(q_ref, f, a0 + k)
            b_ref[2 * f + k] = layer(q_ref, f, b0 + k)
        for k, y in enumerate((0, 1, ny - 2, ny - 1)):
            c_ref[k * nf + k // 2 + f] = q_ref[f, pl.ds(y, nx, stride=ny)].astype(BF)
    a_ref[2 * nf] = layer(s_ref, None, a1)
    b_ref[2 * nf] = layer(s_ref, None, b1)
    for k, y in ((2 * nf, 0), (4 * nf + 1, ny - 1)):
        c_ref[k] = s_ref[pl.ds(y, nx, stride=ny)].astype(F32).astype(BF)


def relay_kernel(dims, imap, a_ref, b_ref, after_ref, o_ref, rows):
    nf, nx, ny, nz = dims
    rows[...] = jnp.zeros_like(rows)
    rows[6:7, :ny] = imap[...].astype(F32)
    for f in range(nf):
        o_ref[f, :ny] = b_ref[2 * f]
        for k, (src, n) in enumerate(((a_ref, 2 * f), (a_ref, 2 * f + 1), (b_ref, 2 * f + 1))):
            block = src[n].astype(F32)
            rows[2 * k : 2 * k + 1] = block[:1]
            rows[2 * k + 1 : 2 * k + 2] = block[ny - 1 :]
        o_ref[f, ny:] = rows[...].astype(BF)


def shift_pair(nz, down):
    row = lax.broadcasted_iota(jnp.int32, (2 * nz, 2 * nz), 0)
    col = lax.broadcasted_iota(jnp.int32, (2 * nz, 2 * nz), 1)
    second = col >= nz
    k = jnp.where(second, col - nz, col)
    if down:
        other = jnp.where(k == 0, nz - 1, k - 1)
    else:
        other = jnp.where(k == nz - 1, 0, k + 1)
    other = jnp.where(second, other + nz, other)
    one = lambda c: jnp.where(c, 1.0, 0.0)
    diff = one(row == other) - one(row == col)
    return (-diff if down else diff).astype(BF)


def section_kernel(dims, second, *refs):
    nf, nx, ny, nz = dims
    pairs = [(6, None), (4, 5), (0, 1), (2, 3)]
    parts = ny // 8

    def run(*accs):
        if second:
            dif, adv, base_ref, q_ref, s_ref, o_ref, fx, gs = refs
        else:
            dif, adv, q_ref, s_ref, o_ref, fx, gs = refs
        n = len(pairs)
        ups, downs = (accs[:n], accs[n : 2 * n]), (accs[2 * n : 3 * n], accs[3 * n :])
        d, c, level = scalars(dif, adv, nf)
        fx[...] = jnp.zeros_like(fx)
        pltpu.matmul_push_rhs(shift_pair(nz, False), staging_register=0, mxu_index=0)
        pltpu.matmul_push_rhs(shift_pair(nz, True), staging_register=0, mxu_index=1)

        def at(x, k):
            return pl.ds(x * ny + k, 8, stride=parts)

        def layer(f, x):
            return [q_ref[f, at(x, k)] for k in range(parts)]

        def tall(v):
            return jnp.concatenate(v, 0).astype(BF)

        def push(x, bank, g, load=None):
            for p, (f0, f1) in enumerate(pairs):
                lhs = jnp.concatenate([tall(layer(f0, x)), tall(g if f1 is None else layer(f1, x))], 1)
                pltpu.matmul_acc_lhs(ups[bank][p], lhs, load_staged_rhs=load)
                pltpu.matmul_acc_lhs(downs[bank][p], lhs, load_staged_rhs=load)
                load = None

        def prepare(x, bank, g):
            ge = [gain(v) for v in layer(4, jnp.minimum(x + 1, nx - 1))]
            for k in range(parts):
                gs[bank, 0, k] = g[k] + ge[k]
                gs[bank, 1, k] = g[k] + (g[k + 1] if k + 1 < parts else pltpu.roll(g[0], 7, 0))
                gs[bank, 2, k] = g[k] + g[k]
                m, a = masks(s_ref[at(jnp.minimum(x, nx - 1), k)] >= level)
                gs[bank, 3, k] = m
                gs[bank, 4, k] = a
            return ge

        def compute(x, bank):
            xe, xw = jnp.minimum(x + 1, nx - 1), jnp.maximum(x - 1, 0)
            for p, pair in enumerate(pairs):
                up, down = pltpu.matmul_pop(ups[bank][p]), pltpu.matmul_pop(downs[bank][p])
                piece = lambda v, k, h: v[8 * k : 8 * k + 8, h * nz : (h + 1) * nz]
                if pair[1] is None:
                    gz = [gs[bank, 2, k] + piece(up, k, 1) for k in range(parts)]
                    gzl = [gs[bank, 2, k] - piece(down, k, 1) for k in range(parts)]
                for h, f in enumerate(pair):
                    if f is None:
                        continue
                    q = layer(f, x)
                    fy = [gs[bank, 1, k] * ((q[k + 1] if k + 1 < parts else pltpu.roll(q[0], 7, 0)) - q[k])
                          for k in range(parts)]
                    for k in range(parts):
                        qe, qw = q_ref[f, at(xe, k)], q_ref[f, at(xw, k)]
                        flux = gs[bank, 0, k] * (qe - q[k])
                        total = flux - fx[f, k]
                        fx[f, k] = flux
                        total += fy[k] - (fy[k - 1] if k else pltpu.roll(fy[-1], 1, 0))
                        total += gz[k] * piece(up, k, h) - gzl[k] * piece(down, k, h)
                        new = q[k] + (d[f] * (gs[bank, 3, k] * total) - c[f] * (gs[bank, 4, k] * (qe - qw)))
                        if second:
                            new = 0.5 * (base_ref[f, at(x, k)] + new)
                        o_ref[f, at(x, k)] = new

        def step(i, g):
            x = 2 * i
            push(x + 1, 1, g)
            g = prepare(x + 1, 1, g)
            compute(x, 0)
            push(jnp.minimum(x + 2, nx - 1), 0, g)
            g = prepare(x + 2, 0, g)
            compute(x + 1, 1)
            return g

        g = [gain(v) for v in layer(4, 0)]
        push(0, 0, g, 0)
        lax.fori_loop(0, nx // 2, step, prepare(0, 0, g))
        for acc in ups[0] + downs[0]:
            pltpu.matmul_pop(acc)

    accs = [pltpu.ACC(m)((ny, 2 * nz), F32) for m in (0, 1) for _ in range(2 * len(pairs))]
    pl.run_scoped(run, *accs)


def border_kernel(dims, two, *refs):
    nf, nx, ny, nz = dims
    if two:
        dif, adv, imap, q_ref, first_ref, main_ref, s_ref, a_ref, b_ref, c1_ref, c2l_ref, c2h_ref = refs[:12]
        rest = refs[12:]
    else:
        (dif, adv, imap, q_ref, first_ref, main_ref, s_ref, a_ref, b_ref, c1_ref, c2l_ref, c2h_ref,
         face_ref, map_ref) = refs[:14]
        rest = refs[14:]
    out_ref, sm, lay, cor, fl, fp, ol, strips, sem = rest
    d, c, level = scalars(dif, adv, nf)
    comp = lax.axis_index("comp")
    stream, last = lax.axis_index("gx"), lax.axis_size("gx") - 1
    even = stream % 2 == 0
    sm[...] = shift_matrix(nz)

    mids = []
    for f in range(nf):
        mids.append(pltpu.make_async_copy(
            main_ref.at[f, pl.ds(2, nx - 4), pl.ds(8, ny - 16)],
            out_ref.at[f, pl.ds(2, nx - 4), pl.ds(8, ny - 16)], sem.at[0, f]))
        mids[-1].start()
    cuts = []
    for k, row in enumerate((0, ny - 8)):
        cuts.append(pltpu.make_async_copy(main_ref.at[:, :, pl.ds(row, 8)], strips.at[k], sem.at[1, k]))
        cuts[-1].start()

    LF, LN, HN, HF = range(4)
    for f in range(nf):
        av = [a_ref[2 * f].astype(F32), a_ref[2 * f + 1].astype(F32)]
        bv = [b_ref[2 * f].astype(F32), b_ref[2 * f + 1].astype(F32)]
        lay[LF, f] = jnp.where(even, bv[0], av[0])
        lay[LN, f] = jnp.where(even, bv[1], av[1])
        zero = jnp.where(stream == last, 0.0, 1.0)
        lay[HN, f] = jnp.where(even, av[0], bv[0]) * zero
        lay[HF, f] = jnp.where(even, av[1], bv[1]) * zero
        lo, hi = c2l_ref[f, pl.ds(ny, 16)].astype(F32), c2h_ref[f, pl.ds(ny, 16)].astype(F32)
        lo_b, hi_b = c2l_ref[f, pl.ds(ny - 16, 16)].astype(F32), c2h_ref[f, pl.ds(0, 16)].astype(F32)
        cor[0, f : f + 1] = jnp.where(even, lo[5:6], lo[3:4])
        cor[1, f : f + 1] = jnp.where(even, hi[4:5], hi[2:3])
        cor[2, f : f + 1] = jnp.where(even, lo[1:2], lo_b[15:16]) * zero
        cor[3, f : f + 1] = jnp.where(even, hi[0:1], hi_b[0:1]) * zero

    @pl.when(stream == 0)
    def _():
        start = lax.axis_index("gy") * ny
        if two:
            whole = 2 * ny
            mine = jnp.broadcast_to(imap[...].astype(F32), (1, ny))
            other = c2l_ref[0, pl.ds(ny, 16)].astype(F32)[6:7, :ny]
            mapping = jnp.concatenate([mine, other], axis=1)
            order = start
        else:
            whole = face_ref.shape[1]
            mapping = map_ref[...].astype(F32)
            order = 0
        rows = 40
        r = lax.broadcasted_iota(jnp.int32, (rows, whole), 0)
        want = jnp.where(r < ny, r, jnp.where(r == ny, whole - 1, ny)) + start
        want = jnp.where(want >= whole, want - whole, want).astype(F32)
        t = lax.broadcasted_iota(jnp.int32, (rows, whole), 1) + order
        t = jnp.where(t >= whole, t - whole, t).astype(F32)
        u = lax.broadcasted_iota(jnp.int32, (whole, whole), 0) + order
        u = jnp.where(u >= whole, u - whole, u).astype(F32)
        one = lambda x: jnp.where(x, 1.0, 0.0)
        pick = one(t == want).astype(BF)
        targets = one(jnp.broadcast_to(mapping, (whole, whole)) == u).astype(BF)
        inlet = lax.dot_general(pick, targets, (((1,), (1,)), ((), ())), preferred_element_type=F32)
        feed = one(jnp.broadcast_to(mapping, (rows, whole)) == want)
        choose = jnp.where(comp == 1, inlet, feed).astype(BF)
        for f in range(nf):
            if two:
                layer = jnp.concatenate([b_ref[2 * f], c2l_ref[f, pl.ds(0, ny)]], axis=0)
            else:
                layer = face_ref[f]
            ghost = jnp.dot(choose, layer, preferred_element_type=F32)
            lay[LN, f] = ghost[:ny]
            cor[0, f : f + 1] = ghost[ny : ny + 1]
            cor[1, f : f + 1] = ghost[ny + 1 : ny + 2]

    row = lax.broadcasted_iota(jnp.int32, (ny, nz), 0)

    def slab(center, before, after, low, high, solid, along_outer):
        rows = jnp.concatenate([center(f).astype(BF) for f in range(nf)], axis=0)
        diffs = jnp.dot(rows, sm[...], preferred_element_type=F32)

        def ups(v, h):
            return jnp.where(row == ny - 1, h, pltpu.roll(v, ny - 1, 0))

        def downs(v, l):
            return jnp.where(row == 0, l, pltpu.roll(v, 1, 0))

        g = gain(center(4))
        gb, ga = g + gain(before(4)), g + gain(after(4))
        gu, gd = g + ups(g, gain(high(4))), g + downs(g, gain(low(4)))
        gz = g + pltpu.roll(g, nz - 1, 1)
        gzl = pltpu.roll(gz, 1, 1)
        m, a = masks(solid)
        res = []
        for f in range(nf):
            q = center(f)
            qa, qb = after(f), before(f)
            qu, qd = ups(q, high(f)), downs(q, low(f))
            z = diffs[f * ny : (f + 1) * ny]
            total = ga * (qa - q) - gb * (q - qb) + (gu * (qu - q) - gd * (q - qd))
            total += gz * z[:, :nz] - gzl * z[:, nz:]
            grad = qa - qb if along_outer else qu - qd
            res.append(q + (d[f] * (m * total) - c[f] * (a * grad)))
        return res

    def q_layer(x):
        return lambda f: q_ref[f, x * ny : (x + 1) * ny]

    def q_plane(y):
        return lambda f: q_ref[f, pl.ds(y, nx, stride=ny)]

    def halo(k):
        return lambda f: lay[k, f]

    def corner(k):
        return lambda f: cor[k, f : f + 1]

    plane = {-2: 2 * nf + 1, -1: 3 * nf + 1, ny: 0, ny + 1: nf}

    def c_plane(y):
        return lambda f: c1_ref[plane[y] + f].astype(F32)

    def line(src, k):
        return lambda f: src(f)[k : k + 1]

    s_lay = lambda x: s_ref[x * ny : (x + 1) * ny] >= level
    s_pla = lambda y: s_ref[pl.ds(y, nx, stride=ny)] >= level
    level_f = level.astype(F32)
    m_low = jnp.where(even, b_ref[2 * nf], a_ref[2 * nf]).astype(F32) >= level_f
    m_high = jnp.where(even, a_ref[2 * nf], b_ref[2 * nf]).astype(F32) >= level_f

    def put(dst, k, vals):
        for f in range(nf):
            dst[k, f] = vals[f]

    put(fl, 0, slab(halo(LN), halo(LF), q_layer(0), corner(0), corner(1), m_low, True))

    @pl.when(stream == 0)
    def _():
        for f in range(nf):
            fl[0, f] = lay[LN, f]

    def y_line(y, x):
        return lambda f: c1_ref[plane[y] + f, pl.ds(x // 16 * 16, 16)].astype(F32)[x % 16 : x % 16 + 1]

    put(fl, 1, slab(q_layer(0), halo(LN), q_layer(1), y_line(-1, 0), y_line(ny, 0), s_lay(0), True))
    put(fl, 6, slab(q_layer(nx - 1), q_layer(nx - 2), halo(HN), y_line(-1, nx - 1), y_line(ny, nx - 1),
                    s_lay(nx - 1), True))
    put(fl, 7, slab(halo(HN), q_layer(nx - 1), halo(HF), corner(2), corner(3), m_high, True))

    @pl.when(stream == last)
    def _():
        for f in range(nf):
            fl[7, f] = jnp.zeros((ny, nz), F32)

    put(fp, 0, slab(c_plane(-1), c_plane(-2), q_plane(0), corner(0), corner(2),
                    c1_ref[4 * nf + 1].astype(F32) >= level_f, False))
    put(fp, 1, slab(q_plane(0), c_plane(-1), q_plane(1), line(halo(LN), 0), line(halo(HN), 0), s_pla(0), False))
    put(fp, 6, slab(q_plane(ny - 1), q_plane(ny - 2), c_plane(ny), line(halo(LN), ny - 1),
                    line(halo(HN), ny - 1), s_pla(ny - 1), False))
    put(fp, 7, slab(c_plane(ny), q_plane(ny - 1), c_plane(ny + 1), corner(1), corner(3),
                    c1_ref[2 * nf].astype(F32) >= level_f, False))

    for f in range(nf):
        for k, x in ((2, 1), (3, 2), (4, nx - 3), (5, nx - 2)):
            fl[k, f] = first_ref[f, x * ny : (x + 1) * ny]
            fl[k, f, 0:1] = fp[1, f, x : x + 1]
            fl[k, f, ny - 1 : ny] = fp[6, f, x : x + 1]
        for k, y in ((2, 1), (3, 2), (4, ny - 3), (5, ny - 2)):
            fp[k, f] = first_ref[f, pl.ds(y, nx, stride=ny)]
            fp[k, f, 0:1] = fl[1, f, y : y + 1]
            fp[k, f, nx - 1 : nx] = fl[6, f, y : y + 1]

    def got(src, k):
        return lambda f: src[k, f]

    def got_line(src, k, r):
        return lambda f: src[k, f, r : r + 1]

    layers = []
    for k, (n, x) in enumerate(((1, 0), (2, 1), (5, nx - 2), (6, nx - 1))):
        vals = slab(got(fl, n), got(fl, n - 1), got(fl, n + 1), got_line(fp, 0, x), got_line(fp, 7, x), s_lay(x), True)
        for f in range(nf):
            ol[k, f] = 0.5 * (q_layer(x)(f) + vals[f])
        layers.append(pltpu.make_async_copy(ol.at[k], out_ref.at[:, x], sem.at[2, k]))
        layers[-1].start()
    for copy in cuts:
        copy.wait()
    edges = []
    for k, (n, y, side, r) in enumerate(((1, 0, 0, 0), (2, 1, 0, 1), (5, ny - 2, 1, 6), (6, ny - 1, 1, 7))):
        vals = slab(got(fp, n), got(fp, n - 1), got(fp, n + 1), got_line(fl, 0, y), got_line(fl, 7, y), s_pla(y), False)
        for f in range(nf):
            strips[side, f, :, r] = 0.5 * (q_plane(y)(f) + vals[f])
        if k % 2:
            edges.append(pltpu.make_async_copy(
                strips.at[side, :, pl.ds(2, nx - 4)],
                out_ref.at[:, pl.ds(2, nx - 4), pl.ds(side * (ny - 8), 8)], sem.at[3, side]))
            edges[-1].start()
    for copy in mids + layers + edges:
        copy.wait()


VM = pl.BlockSpec(memory_space=pltpu.VMEM)
SM = pl.BlockSpec(memory_space=pltpu.SMEM)
HB = pl.BlockSpec(memory_space=pl.ANY)


def body(sizes, state, diffusivity, advection, solid_mask, iface_map):
    ngx, ngy = sizes
    q = state[0]
    nf, nx, ny, nz = q.shape
    dims = nf, nx, ny, nz
    two = ngy == 2

    flat, solid = q.reshape(nf, nx * ny, nz), solid_mask.reshape(nx * ny, nz)
    send_a, send_b, send_c = pl.pallas_call(
        functools.partial(gather_kernel, dims),
        out_shape=[jax.ShapeDtypeStruct((n, ny, nz), BF) for n in (2 * nf + 1, 2 * nf + 1, 4 * nf + 2)],
        in_specs=[VM] * 2,
        out_specs=[VM] * 3,
        compiler_params=pltpu.CompilerParams(vmem_limit_bytes=2 << 20),
    )(flat, solid)

    if two:
        swap = [(0, 1), (1, 0)]
        c1 = lax.ppermute(send_c, "gy", swap)
    else:
        up = [(j, (j + 1) % ngy) for j in range(ngy)]
        down = [(b, a) for a, b in up]
        half = 2 * nf + 1
        c1 = jnp.concatenate([lax.ppermute(send_c[:half], "gy", down), lax.ppermute(send_c[half:], "gy", up)], 0)

    def both(pairs):
        return pairs + [(b, a) for a, b in pairs]

    inner = both([(k, k + 1) for k in range(0, ngx, 2)])
    a = lax.ppermute(send_a, "gx", inner)
    outer = [(k * ngx + i, k * ngx + i + 1) for k in range(2) for i in range(1, ngx - 1, 2)]
    b = lax.ppermute(send_b, ("comp", "gx"), both(outer + [(0, ngx)]))

    shape = jax.ShapeDtypeStruct((nf, nx * ny, nz), F32)
    cells = nf * nx * ny * nz

    def section(second, *args):
        return pl.pallas_call(
            functools.partial(section_kernel, dims, second),
            out_shape=shape,
            in_specs=[SM, SM] + [VM] * (len(args) + 1),
            out_specs=VM,
            scratch_shapes=[pltpu.VMEM((nf, ny // 8, 8, nz), F32), pltpu.VMEM((2, 5, ny // 8, 8, nz), F32)],
            compiler_params=pltpu.CompilerParams(vmem_limit_bytes=3 << 20),
            cost_estimate=pl.CostEstimate(flops=20 * cells, bytes_accessed=8 * cells, transcendentals=cells // 4),
        )(diffusivity, advection, *args, solid)

    first = section(False, flat)
    map_line = iface_map.reshape(1, ny)
    extra = pl.pallas_call(
        functools.partial(relay_kernel, dims),
        out_shape=jax.ShapeDtypeStruct((nf, ny + 16, nz), BF),
        in_specs=[VM] * 3 + [HB],
        out_specs=VM,
        scratch_shapes=[pltpu.VMEM((16, nz), F32)],
        compiler_params=pltpu.CompilerParams(vmem_limit_bytes=1 << 20),
    )(map_line, a, b, first)
    if two:
        c2 = lax.ppermute(extra, "gy", swap)
        c2l, c2h, more = c2, c2, []
    else:
        c2l, c2h = lax.ppermute(extra, "gy", up), lax.ppermute(extra, "gy", down)
        more = [lax.all_gather(b[: 2 * nf : 2], "gy", axis=1, tiled=True),
                lax.all_gather(iface_map, "gy", axis=0, tiled=True).reshape(1, -1)]

    main = section(True, flat, first)
    mb = pltpu.VMEM
    return pl.pallas_call(
        functools.partial(border_kernel, dims, two),
        out_shape=jax.ShapeDtypeStruct((nf, nx, ny, nz), F32),
        in_specs=[SM, SM, VM] + [VM] * (9 + len(more)),
        out_specs=HB,
        scratch_shapes=[
            mb((nz, 2 * nz), BF), mb((4, nf, ny, nz), F32), mb((4, 8, nz), F32), mb((8, nf, ny, nz), F32),
            mb((8, nf, nx, nz), F32), mb((4, nf, ny, nz), F32), mb((2, nf, nx, 8, nz), F32),
            pltpu.SemaphoreType.DMA((4, 8)),
        ],
        compiler_params=pltpu.CompilerParams(vmem_limit_bytes=10 << 20),
        cost_estimate=pl.CostEstimate(flops=10 * cells, bytes_accessed=8 * cells, transcendentals=cells // 4),
    )(diffusivity, advection, map_line, flat, first, main.reshape(nf, nx, ny, nz), solid,
      a, b, c1, c2l, c2h, *more)[None]


def solution(mesh):
    sizes = mesh.shape["gx"], mesh.shape["gy"]
    return jax.shard_map(
        functools.partial(body, sizes),
        mesh=mesh,
        in_specs=(P("comp", None, "gx", "gy", None), P(), P(), P("gx", "gy", None), P("gy")),
        out_specs=P("comp", None, "gx", "gy", None),
        check_vma=False,
    )
```

```python
import functools

import jax
import jax.numpy as jnp
from jax import lax
from jax.experimental import pallas as pl
from jax.experimental.pallas import tpu as pltpu
from jax.sharding import PartitionSpec as P

RATIO = 1.5
GAIN = 0.4
LOG2E = 1.4426950408889634
BF = jnp.bfloat16
F32 = jnp.float32


def gain(q):
    return jnp.exp2(GAIN * LOG2E * jnp.tanh(q) - 1.0)


def shift_matrix(nz):
    row = lax.broadcasted_iota(jnp.int32, (nz, 2 * nz), 0)
    col = lax.broadcasted_iota(jnp.int32, (nz, 2 * nz), 1)
    k = jnp.where(col < nz, col, col - nz)
    up = jnp.where(k + 1 == nz, 0, k + 1)
    down = jnp.where(k == 0, nz - 1, k - 1)
    one = lambda c: jnp.where(c, 1.0, 0.0)
    own = one(row == k)
    return jnp.where(col < nz, one(row == up) - own, own - one(row == down)).astype(BF)


def scalars(dif, adv, nf):
    comp = lax.axis_index("comp")
    sign = (2 * comp - 1).astype(F32)
    return [dif[comp, f] for f in range(nf)], [adv[comp, f] * sign for f in range(nf)], 2 - comp


def masks(solid):
    return jnp.where(solid, RATIO, 1.0), jnp.where(solid, 0.0, 0.5)


def gather_kernel(dims, q_ref, s_ref, a_ref, b_ref, c_ref):
    nf, nx, ny, nz = dims
    even = lax.axis_index("gx") % 2 == 0
    def layer(ref, f, k):
        at = pl.multiple_of(k * ny, ny)
        return (ref[pl.ds(at, ny)] if f is None else ref[f, pl.ds(at, ny)]).astype(F32).astype(BF)

    a0, b0 = jnp.where(even, nx - 2, 0), jnp.where(even, 0, nx - 2)
    a1, b1 = jnp.where(even, nx - 1, 0), jnp.where(even, 0, nx - 1)
    for f in range(nf):
        for k in range(2):
            a_ref[2 * f + k] = layer(q_ref, f, a0 + k)
            b_ref[2 * f + k] = layer(q_ref, f, b0 + k)
        for k, y in enumerate((0, 1, ny - 2, ny - 1)):
            c_ref[k * nf + k // 2 + f] = q_ref[f, pl.ds(y, nx, stride=ny)].astype(BF)
    a_ref[2 * nf] = layer(s_ref, None, a1)
    b_ref[2 * nf] = layer(s_ref, None, b1)
    for k, y in ((2 * nf, 0), (4 * nf + 1, ny - 1)):
        c_ref[k] = s_ref[pl.ds(y, nx, stride=ny)].astype(F32).astype(BF)


def relay_kernel(dims, imap, a_ref, b_ref, after_ref, o_ref, rows):
    nf, nx, ny, nz = dims
    rows[...] = jnp.zeros_like(rows)
    rows[6:7, :ny] = imap[...].astype(F32)
    for f in range(nf):
        o_ref[f, :ny] = b_ref[2 * f]
        for k, (src, n) in enumerate(((a_ref, 2 * f), (a_ref, 2 * f + 1), (b_ref, 2 * f + 1))):
            block = src[n].astype(F32)
            rows[2 * k : 2 * k + 1] = block[:1]
            rows[2 * k + 1 : 2 * k + 2] = block[ny - 1 :]
        o_ref[f, ny:] = rows[...].astype(BF)


def shift_pair(nz, down):
    row = lax.broadcasted_iota(jnp.int32, (2 * nz, 2 * nz), 0)
    col = lax.broadcasted_iota(jnp.int32, (2 * nz, 2 * nz), 1)
    second = col >= nz
    k = jnp.where(second, col - nz, col)
    if down:
        other = jnp.where(k == 0, nz - 1, k - 1)
    else:
        other = jnp.where(k == nz - 1, 0, k + 1)
    other = jnp.where(second, other + nz, other)
    one = lambda c: jnp.where(c, 1.0, 0.0)
    diff = one(row == other) - one(row == col)
    return (-diff if down else diff).astype(BF)


def section_kernel(dims, second, *refs):
    nf, nx, ny, nz = dims
    pairs = [(6, None), (4, 5), (0, 1), (2, 3)]
    parts = ny // 8

    def run(*accs):
        if second:
            dif, adv, base_ref, q_ref, s_ref, o_ref, fx, gs = refs
        else:
            dif, adv, q_ref, s_ref, o_ref, fx, gs = refs
        n = len(pairs)
        ups, downs = (accs[:n], accs[n : 2 * n]), (accs[2 * n : 3 * n], accs[3 * n :])
        d, c, level = scalars(dif, adv, nf)
        lo, hi = (1, nx - 2) if second else (0, nx - 1)
        closed = (0, ny - 2) if second else (ny - 1,)
        sub = lax.broadcasted_iota(jnp.int32, (8, nz), 0)
        fx[...] = jnp.zeros_like(fx)
        pltpu.matmul_push_rhs(shift_pair(nz, False), staging_register=0, mxu_index=0)
        pltpu.matmul_push_rhs(shift_pair(nz, True), staging_register=0, mxu_index=1)

        def at(x, k):
            return pl.ds(x * ny + k, 8, stride=parts)

        def layer(f, x):
            return [q_ref[f, at(x, k)] for k in range(parts)]

        def tall(v):
            return jnp.concatenate(v, 0).astype(BF)

        def push(x, bank, g, load=None):
            for p, (f0, f1) in enumerate(pairs):
                lhs = jnp.concatenate([tall(layer(f0, x)), tall(g if f1 is None else layer(f1, x))], 1)
                pltpu.matmul_acc_lhs(ups[bank][p], lhs, load_staged_rhs=load)
                pltpu.matmul_acc_lhs(downs[bank][p], lhs, load_staged_rhs=load)
                load = None

        def prepare(x, bank, g):
            ge = [gain(v) for v in layer(4, jnp.minimum(x + 1, hi))]
            for k in range(parts):
                gs[bank, 0, k] = g[k] + ge[k]
                face = g[k] + (g[k + 1] if k + 1 < parts else pltpu.roll(g[0], 7, 0))
                for y in closed:
                    if y % parts == k:
                        face = jnp.where(sub == y // parts, 0.0, face)
                gs[bank, 1, k] = face
                gs[bank, 2, k] = g[k] + g[k]
                m, a = masks(s_ref[at(jnp.minimum(x, hi), k)] >= level)
                gs[bank, 3, k] = m
                gs[bank, 4, k] = a
            return ge

        def compute(x, bank):
            xe, xw = jnp.minimum(x + 1, hi), jnp.maximum(x - 1, lo)
            for p, pair in enumerate(pairs):
                up, down = pltpu.matmul_pop(ups[bank][p]), pltpu.matmul_pop(downs[bank][p])
                piece = lambda v, k, h: v[8 * k : 8 * k + 8, h * nz : (h + 1) * nz]
                if pair[1] is None:
                    gz = [gs[bank, 2, k] + piece(up, k, 1) for k in range(parts)]
                    gzl = [gs[bank, 2, k] - piece(down, k, 1) for k in range(parts)]
                for h, f in enumerate(pair):
                    if f is None:
                        continue
                    q = layer(f, x)
                    fy = [gs[bank, 1, k] * ((q[k + 1] if k + 1 < parts else pltpu.roll(q[0], 7, 0)) - q[k])
                          for k in range(parts)]
                    for k in range(parts):
                        qe, qw = q_ref[f, at(xe, k)], q_ref[f, at(xw, k)]
                        flux = gs[bank, 0, k] * (qe - q[k])
                        total = flux - fx[f, k]
                        fx[f, k] = flux
                        total += fy[k] - (fy[k - 1] if k else pltpu.roll(fy[-1], 1, 0))
                        total += gz[k] * piece(up, k, h) - gzl[k] * piece(down, k, h)
                        new = q[k] + (d[f] * (gs[bank, 3, k] * total) - c[f] * (gs[bank, 4, k] * (qe - qw)))
                        if second:
                            new = 0.5 * (base_ref[f, at(x, k)] + new)
                        o_ref[f, at(x, k)] = new

        def step(i, g):
            x = 2 * i + lo
            push(x + 1, 1, g)
            g = prepare(x + 1, 1, g)
            compute(x, 0)
            push(jnp.minimum(x + 2, hi), 0, g)
            g = prepare(x + 2, 0, g)
            compute(x + 1, 1)
            return g

        g = [gain(v) for v in layer(4, lo)]
        push(lo, 0, g, 0)
        lax.fori_loop(0, (hi + 1 - lo) // 2, step, prepare(lo, 0, g))
        for acc in ups[0] + downs[0]:
            pltpu.matmul_pop(acc)

    accs = [pltpu.ACC(m)((ny, 2 * nz), F32) for m in (0, 1) for _ in range(2 * len(pairs))]
    pl.run_scoped(run, *accs)


def border_kernel(dims, two, *refs):
    nf, nx, ny, nz = dims
    if two:
        dif, adv, imap, q_ref, first_ref, main_ref, s_ref, a_ref, b_ref, c1_ref, c2l_ref, c2h_ref = refs[:12]
        rest = refs[12:]
    else:
        (dif, adv, imap, q_ref, first_ref, main_ref, s_ref, a_ref, b_ref, c1_ref, c2l_ref, c2h_ref,
         face_ref, map_ref) = refs[:14]
        rest = refs[14:]
    out_ref, sm, lay, pla, ms, cor, fl, fp, cx, cy, ol, strips, zin, zout, sem = rest
    d, c, level = scalars(dif, adv, nf)
    comp = lax.axis_index("comp")
    stream, last = lax.axis_index("gx"), lax.axis_size("gx") - 1
    even = stream % 2 == 0
    parts = ny // 8
    sm[...] = shift_matrix(nz)

    mids = []
    for f in range(nf):
        mids.append(pltpu.make_async_copy(
            main_ref.at[f, pl.ds(2, nx - 4), pl.ds(8, ny - 16)],
            out_ref.at[f, pl.ds(2, nx - 4), pl.ds(8, ny - 16)], sem.at[0, f]))
        mids[-1].start()
    cuts = []
    for k, row in enumerate((0, ny - 8)):
        cuts.append(pltpu.make_async_copy(main_ref.at[:, :, pl.ds(row, 8)], strips.at[k], sem.at[1, k]))
        cuts[-1].start()

    FAR_LO, LO, HI, FAR_HI = range(4)
    inside = jnp.where(stream == last, 0.0, 1.0)
    for f in range(nf):
        av = [a_ref[2 * f].astype(F32), a_ref[2 * f + 1].astype(F32)]
        bv = [b_ref[2 * f].astype(F32), b_ref[2 * f + 1].astype(F32)]
        lay[FAR_LO, f] = jnp.where(even, bv[0], av[0])
        lay[LO, f] = jnp.where(even, bv[1], av[1])
        lay[HI, f] = jnp.where(even, av[0], bv[0]) * inside
        lay[FAR_HI, f] = jnp.where(even, av[1], bv[1]) * inside
        for n, k in enumerate((2 * nf + 1, 3 * nf + 1, 0, nf)):
            pla[n, f] = c1_ref[k + f].astype(F32)
        lo, hi = c2l_ref[f, pl.ds(ny, 16)].astype(F32), c2h_ref[f, pl.ds(ny, 16)].astype(F32)
        lo_b, hi_b = c2l_ref[f, pl.ds(ny - 16, 16)].astype(F32), c2h_ref[f, pl.ds(0, 16)].astype(F32)
        cor[0, f : f + 1] = jnp.where(even, lo[5:6], lo[3:4])
        cor[1, f : f + 1] = jnp.where(even, hi[4:5], hi[2:3])
        cor[2, f : f + 1] = jnp.where(even, lo[1:2], lo_b[15:16]) * inside
        cor[3, f : f + 1] = jnp.where(even, hi[0:1], hi_b[0:1]) * inside
    am, bm = a_ref[2 * nf].astype(F32), b_ref[2 * nf].astype(F32)
    ms[0] = jnp.where(even, bm, am)
    ms[1] = jnp.where(even, am, bm)
    ms[2] = c1_ref[4 * nf + 1].astype(F32)
    ms[3] = c1_ref[2 * nf].astype(F32)

    @pl.when(stream == 0)
    def _():
        start = lax.axis_index("gy") * ny
        if two:
            whole = 2 * ny
            mine = jnp.broadcast_to(imap[...].astype(F32), (1, ny))
            other = c2l_ref[0, pl.ds(ny, 16)].astype(F32)[6:7, :ny]
            mapping = jnp.concatenate([mine, other], axis=1)
            order = start
        else:
            whole = face_ref.shape[1]
            mapping = map_ref[...].astype(F32)
            order = 0
        rows = ny + 8
        r = lax.broadcasted_iota(jnp.int32, (rows, whole), 0)
        want = jnp.where(r < ny, r, jnp.where(r == ny, whole - 1, ny)) + start
        want = jnp.where(want >= whole, want - whole, want).astype(F32)
        t = lax.broadcasted_iota(jnp.int32, (rows, whole), 1) + order
        t = jnp.where(t >= whole, t - whole, t).astype(F32)
        u = lax.broadcasted_iota(jnp.int32, (whole, whole), 0) + order
        u = jnp.where(u >= whole, u - whole, u).astype(F32)
        one = lambda x: jnp.where(x, 1.0, 0.0)
        pick = one(t == want).astype(BF)
        targets = one(jnp.broadcast_to(mapping, (whole, whole)) == u).astype(BF)
        inlet = lax.dot_general(pick, targets, (((1,), (1,)), ((), ())), preferred_element_type=F32)
        feed = one(jnp.broadcast_to(mapping, (rows, whole)) == want)
        choose = jnp.where(comp == 1, inlet, feed).astype(BF)
        for f in range(nf):
            if two:
                face = jnp.concatenate([b_ref[2 * f], c2l_ref[f, pl.ds(0, ny)]], axis=0)
            else:
                face = face_ref[f]
            ghost = jnp.dot(choose, face, preferred_element_type=F32)
            lay[LO, f] = ghost[:ny]
            cor[0, f : f + 1] = ghost[ny : ny + 1]
            cor[1, f : f + 1] = ghost[ny + 1 : ny + 2]

    sub = lax.broadcasted_iota(jnp.int32, (8, nz), 0)
    every = range(parts)

    def held(ref, *at):
        return lambda f, k: ref[(*at, f, pl.ds(k, 8, stride=parts))]

    def q_layer(x):
        return lambda f, k: q_ref[f, pl.ds(x * ny + k, 8, stride=parts)]

    def q_plane(y):
        return lambda f, k: q_ref[f, pl.ds(k * ny + y, 8, stride=parts * ny)]

    def s_layer(x):
        return lambda k: s_ref[pl.ds(x * ny + k, 8, stride=parts)] >= level

    def s_plane(y):
        return lambda k: s_ref[pl.ds(k * ny + y, 8, stride=parts * ny)] >= level

    def s_halo(n):
        edge = level.astype(F32)
        return lambda k: ms[n, pl.ds(k, 8, stride=parts)] >= edge

    def gains(src):
        return [gain(src(4, k)) for k in every]

    def line(src, r):
        return lambda f: src(f, r % parts)[r // parts : r // parts + 1]

    def corner(n):
        return lambda f: cor[n, f : f + 1]

    def got_line(ref, n, r):
        return lambda f: ref[n, f, r : r + 1]

    def put(ref, n, vals):
        for f in range(nf):
            for k in every:
                ref[n, f, pl.ds(k, 8, stride=parts)] = vals[f][k]

    def products(centers):
        gs = []
        for n, src in enumerate(centers):
            gs.append(gains(src))
            tall = [src(f, k) for f in range(nf) for k in every] + gs[-1]
            zin[pl.ds(n * (nf + 1) * ny, (nf + 1) * ny)] = jnp.concatenate(tall, 0).astype(BF)
        zout[...] = jnp.dot(zin[...], sm[...], preferred_element_type=F32)
        return gs

    def slab(n, g, center, before, after, low, high, solid, along_outer):
        def z(f, k, h):
            return zout[(n * (nf + 1) + f) * ny + 8 * k : (n * (nf + 1) + f) * ny + 8 * k + 8, h * nz : (h + 1) * nz]

        def ups(v, edge):
            return v[1:] + [jnp.where(sub == 7, edge, pltpu.roll(v[0], 7, 0))]

        def downs(v, edge):
            return [jnp.where(sub == 0, edge, pltpu.roll(v[-1], 1, 0))] + v[:-1]

        gb, ga = gains(before), gains(after)
        gu, gd = ups(g, gain(high(4))), downs(g, gain(low(4)))
        ga, gb, gu, gd = ([x + y for x, y in zip(g, v)] for v in (ga, gb, gu, gd))
        gz = [2.0 * g[k] + z(nf, k, 0) for k in every]
        gzl = [2.0 * g[k] - z(nf, k, 1) for k in every]
        ma = [masks(solid(k)) for k in every]
        res = []
        for f in range(nf):
            q = [center(f, k) for k in every]
            qu, qd = ups(q, high(f)), downs(q, low(f))
            vals = []
            for k in every:
                da, db, du, dd = after(f, k) - q[k], q[k] - before(f, k), qu[k] - q[k], q[k] - qd[k]
                total = ga[k] * da - gb[k] * db + (gu[k] * du - gd[k] * dd)
                total += gz[k] * z(f, k, 0) - gzl[k] * z(f, k, 1)
                grad = da + db if along_outer else du + dd
                vals.append(q[k] + (d[f] * (ma[k][0] * total) - c[f] * (ma[k][1] * grad)))
            res.append(vals)
        return res

    def passed(here, there, solid, along_x, ahead):
        g = [x + y for x, y in zip(gains(here), gains(there))]
        ma = [masks(solid(k)) for k in every]
        res = []
        for f in range(nf):
            vals = []
            for k in every:
                diff = there(f, k) - here(f, k)
                add = d[f] * (ma[k][0] * (g[k] * diff))
                if along_x:
                    half = c[f] * (ma[k][1] * diff)
                    add = add - half if ahead else add + half
                vals.append(add)
            res.append(vals)
        return res

    g = products([held(lay, LO), held(lay, HI), held(pla, LO), held(pla, HI)])
    put(fl, 0, slab(0, g[0], held(lay, LO), held(lay, FAR_LO), q_layer(0), corner(0), corner(1), s_halo(0), True))
    put(fl, 5, slab(1, g[1], held(lay, HI), q_layer(nx - 1), held(lay, FAR_HI), corner(2), corner(3), s_halo(1), True))
    put(fp, 0, slab(2, g[2], held(pla, LO), held(pla, FAR_LO), q_plane(0), corner(0), corner(2), s_halo(2), False))
    put(fp, 5, slab(3, g[3], held(pla, HI), q_plane(ny - 1), held(pla, FAR_HI), corner(1), corner(3), s_halo(3), False))

    @pl.when(stream == 0)
    def _():
        fl[0] = lay[LO]

    @pl.when(stream == last)
    def _():
        fl[5] = jnp.zeros(fl.shape[1:], F32)

    put(cx, 0, passed(q_layer(0), held(lay, LO), s_layer(0), True, False))
    put(cx, 1, passed(q_layer(nx - 1), held(lay, HI), s_layer(nx - 1), True, True))
    put(cy, 0, passed(q_plane(0), held(pla, LO), s_plane(0), False, False))
    put(cy, 1, passed(q_plane(ny - 1), held(pla, HI), s_plane(ny - 1), False, True))
    for f in range(nf):
        for n, x in ((1, 0), (2, 1), (3, nx - 2), (4, nx - 1)):
            v = first_ref[f, x * ny : (x + 1) * ny]
            fl[n, f] = v + cx[n // 4, f] if n in (1, 4) else v
            fl[n, f, 0:1] += cy[0, f, x : x + 1]
            fl[n, f, ny - 1 : ny] += cy[1, f, x : x + 1]
        for n, y in ((1, 0), (2, 1), (3, ny - 2), (4, ny - 1)):
            v = first_ref[f, pl.ds(y, nx, stride=ny)]
            fp[n, f] = v + cy[n // 4, f] if n in (1, 4) else v
            fp[n, f, 0:1] += cx[0, f, y : y + 1]
            fp[n, f, nx - 1 : nx] += cx[1, f, y : y + 1]

    g = products([held(fl, 1), held(fl, 4), held(fp, 1), held(fp, 4)])

    def ended(src, vals):
        return [[0.5 * (src(f, k) + vals[f][k]) for k in every] for f in range(nf)]

    copies = []
    for n, (m, x) in enumerate(((1, 0), (4, nx - 1))):
        vals = slab(n, g[n], held(fl, m), held(fl, m - 1), held(fl, m + 1), got_line(fp, 0, x), got_line(fp, 5, x),
                    s_layer(x), True)
        put(ol, 3 * n, ended(q_layer(x), vals))
        copies.append(pltpu.make_async_copy(ol.at[3 * n], out_ref.at[:, x], sem.at[2, 3 * n]))
        copies[-1].start()
    for n, (m, y) in enumerate(((1, 0), (4, ny - 1))):
        vals = slab(2 + n, g[2 + n], held(fp, m), held(fp, m - 1), held(fp, m + 1), got_line(fl, 0, y),
                    got_line(fl, 5, y), s_plane(y), False)
        put(cy, n, ended(q_plane(y), vals))
    put(fp, 0, passed(held(fp, 2), held(fp, 1), s_plane(1), False, False))
    put(fp, 5, passed(held(fp, 3), held(fp, 4), s_plane(ny - 2), False, True))
    put(cx, 0, passed(held(fl, 2), held(fl, 1), s_layer(1), True, False))
    put(cx, 1, passed(held(fl, 3), held(fl, 4), s_layer(nx - 2), True, True))
    for n, x in ((0, 1), (1, nx - 2)):
        for f in range(nf):
            k = n + 1
            ol[k, f] = main_ref[f, x] + 0.5 * cx[n, f]
            ol[k, f, 0:1] = cy[0, f, x : x + 1]
            ol[k, f, 1:2] += 0.5 * fp[0, f, x : x + 1]
            ol[k, f, ny - 2 : ny - 1] += 0.5 * fp[5, f, x : x + 1]
            ol[k, f, ny - 1 : ny] = cy[1, f, x : x + 1]
        copies.append(pltpu.make_async_copy(ol.at[n + 1], out_ref.at[:, x], sem.at[2, n + 1]))
        copies[-1].start()
    for n, (end, near) in enumerate(((0, 1), (7, 6))):
        cuts[n].wait()
        for f in range(nf):
            strips[n, f, :, end] = cy[n, f]
            strips[n, f, :, near] += 0.5 * fp[5 * n, f]
        copies.append(pltpu.make_async_copy(
            strips.at[n, :, pl.ds(2, nx - 4)],
            out_ref.at[:, pl.ds(2, nx - 4), pl.ds(n * (ny - 8), 8)], sem.at[3, n]))
        copies[-1].start()
    for copy in mids + copies:
        copy.wait()


VM = pl.BlockSpec(memory_space=pltpu.VMEM)
SM = pl.BlockSpec(memory_space=pltpu.SMEM)
HB = pl.BlockSpec(memory_space=pl.ANY)


def body(sizes, state, diffusivity, advection, solid_mask, iface_map):
    ngx, ngy = sizes
    q = state[0]
    nf, nx, ny, nz = q.shape
    dims = nf, nx, ny, nz
    two = ngy == 2

    flat, solid = q.reshape(nf, nx * ny, nz), solid_mask.reshape(nx * ny, nz)
    send_a, send_b, send_c = pl.pallas_call(
        functools.partial(gather_kernel, dims),
        out_shape=[jax.ShapeDtypeStruct((n, ny, nz), BF) for n in (2 * nf + 1, 2 * nf + 1, 4 * nf + 2)],
        in_specs=[VM] * 2,
        out_specs=[VM] * 3,
        compiler_params=pltpu.CompilerParams(vmem_limit_bytes=2 << 20),
    )(flat, solid)

    if two:
        swap = [(0, 1), (1, 0)]
        c1 = lax.ppermute(send_c, "gy", swap)
    else:
        up = [(j, (j + 1) % ngy) for j in range(ngy)]
        down = [(b, a) for a, b in up]
        half = 2 * nf + 1
        c1 = jnp.concatenate([lax.ppermute(send_c[:half], "gy", down), lax.ppermute(send_c[half:], "gy", up)], 0)

    def both(pairs):
        return pairs + [(b, a) for a, b in pairs]

    inner = both([(k, k + 1) for k in range(0, ngx, 2)])
    a = lax.ppermute(send_a, "gx", inner)
    outer = [(k * ngx + i, k * ngx + i + 1) for k in range(2) for i in range(1, ngx - 1, 2)]
    b = lax.ppermute(send_b, ("comp", "gx"), both(outer + [(0, ngx)]))

    shape = jax.ShapeDtypeStruct((nf, nx * ny, nz), F32)
    cells = nf * nx * ny * nz

    def section(second, *args):
        return pl.pallas_call(
            functools.partial(section_kernel, dims, second),
            out_shape=shape,
            in_specs=[SM, SM] + [VM] * (len(args) + 1),
            out_specs=VM,
            scratch_shapes=[pltpu.VMEM((nf, ny // 8, 8, nz), F32), pltpu.VMEM((2, 5, ny // 8, 8, nz), F32)],
            compiler_params=pltpu.CompilerParams(vmem_limit_bytes=3 << 20),
            cost_estimate=pl.CostEstimate(flops=20 * cells, bytes_accessed=8 * cells, transcendentals=cells // 4),
        )(diffusivity, advection, *args, solid)

    first = section(False, flat)
    map_line = iface_map.reshape(1, ny)
    extra = pl.pallas_call(
        functools.partial(relay_kernel, dims),
        out_shape=jax.ShapeDtypeStruct((nf, ny + 16, nz), BF),
        in_specs=[VM] * 3 + [HB],
        out_specs=VM,
        scratch_shapes=[pltpu.VMEM((16, nz), F32)],
        compiler_params=pltpu.CompilerParams(vmem_limit_bytes=1 << 20),
    )(map_line, a, b, first)
    if two:
        c2 = lax.ppermute(extra, "gy", swap)
        c2l, c2h, more = c2, c2, []
    else:
        c2l, c2h = lax.ppermute(extra, "gy", up), lax.ppermute(extra, "gy", down)
        more = [lax.all_gather(b[: 2 * nf : 2], "gy", axis=1, tiled=True),
                lax.all_gather(iface_map, "gy", axis=0, tiled=True).reshape(1, -1)]

    main = section(True, flat, first)
    mb = pltpu.VMEM
    return pl.pallas_call(
        functools.partial(border_kernel, dims, two),
        out_shape=jax.ShapeDtypeStruct((nf, nx, ny, nz), F32),
        in_specs=[SM, SM, VM] + [VM] * (9 + len(more)),
        out_specs=HB,
        scratch_shapes=[
            mb((nz, 2 * nz), BF), mb((4, nf, ny, nz), F32), mb((4, nf, nx, nz), F32), mb((4, ny, nz), F32),
            mb((4, 8, nz), F32), mb((6, nf, ny, nz), F32), mb((6, nf, nx, nz), F32), mb((2, nf, ny, nz), F32),
            mb((2, nf, nx, nz), F32), mb((4, nf, ny, nz), F32), mb((2, nf, nx, 8, nz), F32),
            mb((4 * (nf + 1) * ny, nz), BF), mb((4 * (nf + 1) * ny, 2 * nz), F32),
            pltpu.SemaphoreType.DMA((4, 8)),
        ],
        compiler_params=pltpu.CompilerParams(vmem_limit_bytes=10 << 20),
        cost_estimate=pl.CostEstimate(flops=10 * cells, bytes_accessed=8 * cells, transcendentals=cells // 4),
    )(diffusivity, advection, map_line, flat, first, main.reshape(nf, nx, ny, nz), solid,
      a, b, c1, c2l, c2h, *more)[None]


def solution(mesh):
    sizes = mesh.shape["gx"], mesh.shape["gy"]
    return jax.shard_map(
        functools.partial(body, sizes),
        mesh=mesh,
        in_specs=(P("comp", None, "gx", "gy", None), P(), P(), P("gx", "gy", None), P("gy")),
        out_specs=P("comp", None, "gx", "gy", None),
        check_vma=False,
    )
```

```python
import functools

import jax
import jax.numpy as jnp
from jax import lax
from jax.experimental import pallas as pl
from jax.experimental.pallas import tpu as pltpu
from jax.sharding import PartitionSpec as P

RATIO = 1.5
GAIN = 0.4
LOG2E = 1.4426950408889634
BF = jnp.bfloat16
F32 = jnp.float32


def gain(q):
    return jnp.exp2(GAIN * LOG2E * jnp.tanh(q) - 1.0)


def shift_matrix(nz):
    row = lax.broadcasted_iota(jnp.int32, (nz, 2 * nz), 0)
    col = lax.broadcasted_iota(jnp.int32, (nz, 2 * nz), 1)
    k = jnp.where(col < nz, col, col - nz)
    up = jnp.where(k + 1 == nz, 0, k + 1)
    down = jnp.where(k == 0, nz - 1, k - 1)
    one = lambda c: jnp.where(c, 1.0, 0.0)
    own = one(row == k)
    return jnp.where(col < nz, one(row == up) - own, own - one(row == down)).astype(BF)


def scalars(dif, adv, nf):
    comp = lax.axis_index("comp")
    sign = (2 * comp - 1).astype(F32)
    return [dif[comp, f] for f in range(nf)], [adv[comp, f] * sign for f in range(nf)], 2 - comp


def masks(solid):
    return jnp.where(solid, RATIO, 1.0), jnp.where(solid, 0.0, 0.5)


def gather_kernel(dims, q_ref, s_ref, a_ref, b_ref, c_ref):
    nf, nx, ny, nz = dims
    even = lax.axis_index("gx") % 2 == 0
    def layer(ref, f, k):
        at = pl.multiple_of(k * ny, ny)
        return (ref[pl.ds(at, ny)] if f is None else ref[f, pl.ds(at, ny)]).astype(F32).astype(BF)

    a0, b0 = jnp.where(even, nx - 2, 0), jnp.where(even, 0, nx - 2)
    a1, b1 = jnp.where(even, nx - 1, 0), jnp.where(even, 0, nx - 1)
    for f in range(nf):
        for k in range(2):
            a_ref[2 * f + k] = layer(q_ref, f, a0 + k)
            b_ref[2 * f + k] = layer(q_ref, f, b0 + k)
        for k, y in enumerate((0, 1, ny - 2, ny - 1)):
            c_ref[k * nf + k // 2 + f] = q_ref[f, pl.ds(y, nx, stride=ny)].astype(BF)
    a_ref[2 * nf] = layer(s_ref, None, a1)
    b_ref[2 * nf] = layer(s_ref, None, b1)
    for k, y in ((2 * nf, 0), (4 * nf + 1, ny - 1)):
        c_ref[k] = s_ref[pl.ds(y, nx, stride=ny)].astype(F32).astype(BF)


def relay_kernel(dims, imap, a_ref, b_ref, after_ref, o_ref, rows):
    nf, nx, ny, nz = dims
    rows[...] = jnp.zeros_like(rows)
    rows[6:7, :ny] = imap[...].astype(F32)
    for f in range(nf):
        o_ref[f, :ny] = b_ref[2 * f]
        for k, (src, n) in enumerate(((a_ref, 2 * f), (a_ref, 2 * f + 1), (b_ref, 2 * f + 1))):
            block = src[n].astype(F32)
            rows[2 * k : 2 * k + 1] = block[:1]
            rows[2 * k + 1 : 2 * k + 2] = block[ny - 1 :]
        o_ref[f, ny:] = rows[...].astype(BF)


def shift_pair(nz, down):
    row = lax.broadcasted_iota(jnp.int32, (2 * nz, 2 * nz), 0)
    col = lax.broadcasted_iota(jnp.int32, (2 * nz, 2 * nz), 1)
    second = col >= nz
    k = jnp.where(second, col - nz, col)
    if down:
        other = jnp.where(k == 0, nz - 1, k - 1)
    else:
        other = jnp.where(k == nz - 1, 0, k + 1)
    other = jnp.where(second, other + nz, other)
    one = lambda c: jnp.where(c, 1.0, 0.0)
    diff = one(row == other) - one(row == col)
    return (-diff if down else diff).astype(BF)


def section_kernel(dims, second, *refs):
    nf, nx, ny, nz = dims
    pairs = [(6, None), (4, 5), (0, 1), (2, 3)]
    parts = ny // 8

    def run(*accs):
        if second:
            dif, adv, base_ref, q_ref, s_ref, o_ref, fx, gs = refs
        else:
            dif, adv, q_ref, s_ref, o_ref, fx, gs = refs
        n = len(pairs)
        ups, downs = (accs[:n], accs[n : 2 * n]), (accs[2 * n : 3 * n], accs[3 * n :])
        d, c, level = scalars(dif, adv, nf)
        lo, hi = (1, nx - 2) if second else (0, nx - 1)
        closed = (0, ny - 2) if second else (ny - 1,)
        sub = lax.broadcasted_iota(jnp.int32, (8, nz), 0)
        fx[...] = jnp.zeros_like(fx)
        pltpu.matmul_push_rhs(shift_pair(nz, False), staging_register=0, mxu_index=0)
        pltpu.matmul_push_rhs(shift_pair(nz, True), staging_register=0, mxu_index=1)

        def at(x, k):
            return pl.ds(x * ny + k, 8, stride=parts)

        def layer(f, x):
            return [q_ref[f, at(x, k)] for k in range(parts)]

        def tall(v):
            return jnp.concatenate(v, 0).astype(BF)

        def push(x, bank, g, load=None):
            for p, (f0, f1) in enumerate(pairs):
                lhs = jnp.concatenate([tall(layer(f0, x)), tall(g if f1 is None else layer(f1, x))], 1)
                pltpu.matmul_acc_lhs(ups[bank][p], lhs, load_staged_rhs=load)
                pltpu.matmul_acc_lhs(downs[bank][p], lhs, load_staged_rhs=load)
                load = None

        def prepare(x, bank, g):
            ge = [gain(v) for v in layer(4, jnp.minimum(x + 1, hi))]
            for k in range(parts):
                gs[bank, 0, k] = g[k] + ge[k]
                face = g[k] + (g[k + 1] if k + 1 < parts else pltpu.roll(g[0], 7, 0))
                for y in closed:
                    if y % parts == k:
                        face = jnp.where(sub == y // parts, 0.0, face)
                gs[bank, 1, k] = face
                gs[bank, 2, k] = g[k] + g[k]
                m, a = masks(s_ref[at(jnp.minimum(x, hi), k)] >= level)
                gs[bank, 3, k] = m
                gs[bank, 4, k] = a
            return ge

        def compute(x, bank):
            xe, xw = jnp.minimum(x + 1, hi), jnp.maximum(x - 1, lo)
            for p, pair in enumerate(pairs):
                up, down = pltpu.matmul_pop(ups[bank][p]), pltpu.matmul_pop(downs[bank][p])
                piece = lambda v, k, h: v[8 * k : 8 * k + 8, h * nz : (h + 1) * nz]
                if pair[1] is None:
                    gz = [gs[bank, 2, k] + piece(up, k, 1) for k in range(parts)]
                    gzl = [gs[bank, 2, k] - piece(down, k, 1) for k in range(parts)]
                for h, f in enumerate(pair):
                    if f is None:
                        continue
                    q = layer(f, x)
                    fy = [gs[bank, 1, k] * ((q[k + 1] if k + 1 < parts else pltpu.roll(q[0], 7, 0)) - q[k])
                          for k in range(parts)]
                    for k in range(parts):
                        qe, qw = q_ref[f, at(xe, k)], q_ref[f, at(xw, k)]
                        flux = gs[bank, 0, k] * (qe - q[k])
                        total = flux - fx[f, k]
                        fx[f, k] = flux
                        total += fy[k] - (fy[k - 1] if k else pltpu.roll(fy[-1], 1, 0))
                        total += gz[k] * piece(up, k, h) - gzl[k] * piece(down, k, h)
                        new = q[k] + (d[f] * (gs[bank, 3, k] * total) - c[f] * (gs[bank, 4, k] * (qe - qw)))
                        if second:
                            new = 0.5 * (base_ref[f, at(x, k)] + new)
                        o_ref[f, at(x, k)] = new

        def step(i, g):
            x = 2 * i + lo
            push(x + 1, 1, g)
            g = prepare(x + 1, 1, g)
            compute(x, 0)
            push(jnp.minimum(x + 2, hi), 0, g)
            g = prepare(x + 2, 0, g)
            compute(x + 1, 1)
            return g

        g = [gain(v) for v in layer(4, lo)]
        push(lo, 0, g, 0)
        lax.fori_loop(0, (hi + 1 - lo) // 2, step, prepare(lo, 0, g))
        for acc in ups[0] + downs[0]:
            pltpu.matmul_pop(acc)

    accs = [pltpu.ACC(m)((ny, 2 * nz), F32) for m in (0, 1) for _ in range(2 * len(pairs))]
    pl.run_scoped(run, *accs)


def border_kernel(dims, two, *refs):
    nf, nx, ny, nz = dims
    if two:
        dif, adv, imap, q_ref, first_ref, main_ref, s_ref, a_ref, b_ref, c1_ref, c2l_ref, c2h_ref = refs[:12]
        rest = refs[12:]
    else:
        (dif, adv, imap, q_ref, first_ref, main_ref, s_ref, a_ref, b_ref, c1_ref, c2l_ref, c2h_ref,
         face_ref, map_ref) = refs[:14]
        rest = refs[14:]
    out_ref, sm, lay, pla, qp, ms, cor, fl, fp, cx, cy, ep, ol, strips, zin, zout, sem = rest
    d, c, level = scalars(dif, adv, nf)
    comp = lax.axis_index("comp")
    stream, last = lax.axis_index("gx"), lax.axis_size("gx") - 1
    even = stream % 2 == 0
    parts = ny // 8
    sm[...] = shift_matrix(nz)

    mids = []
    for f in range(nf):
        mids.append(pltpu.make_async_copy(
            main_ref.at[f, pl.ds(2, nx - 4), pl.ds(8, ny - 16)],
            out_ref.at[f, pl.ds(2, nx - 4), pl.ds(8, ny - 16)], sem.at[0, f]))
        mids[-1].start()
    cuts = []
    for k, row in enumerate((0, ny - 8)):
        cuts.append(pltpu.make_async_copy(main_ref.at[:, :, pl.ds(row, 8)], strips.at[k], sem.at[1, k]))
        cuts[-1].start()

    FAR_LO, LO, HI, FAR_HI = range(4)
    inside = jnp.where(stream == last, 0.0, 1.0)
    for f in range(nf):
        av = [a_ref[2 * f].astype(F32), a_ref[2 * f + 1].astype(F32)]
        bv = [b_ref[2 * f].astype(F32), b_ref[2 * f + 1].astype(F32)]
        lay[FAR_LO, f] = jnp.where(even, bv[0], av[0])
        lay[LO, f] = jnp.where(even, bv[1], av[1])
        lay[HI, f] = jnp.where(even, av[0], bv[0]) * inside
        lay[FAR_HI, f] = jnp.where(even, av[1], bv[1]) * inside
        for n, k in enumerate((2 * nf + 1, 3 * nf + 1, 0, nf)):
            pla[n, f] = c1_ref[k + f].astype(F32)
        for n, y in enumerate((0, ny - 1)):
            qp[n, f] = q_ref[f, pl.ds(y, nx, stride=ny)]
        lo, hi = c2l_ref[f, pl.ds(ny, 16)].astype(F32), c2h_ref[f, pl.ds(ny, 16)].astype(F32)
        lo_b, hi_b = c2l_ref[f, pl.ds(ny - 16, 16)].astype(F32), c2h_ref[f, pl.ds(0, 16)].astype(F32)
        cor[0, f : f + 1] = jnp.where(even, lo[5:6], lo[3:4])
        cor[1, f : f + 1] = jnp.where(even, hi[4:5], hi[2:3])
        cor[2, f : f + 1] = jnp.where(even, lo[1:2], lo_b[15:16]) * inside
        cor[3, f : f + 1] = jnp.where(even, hi[0:1], hi_b[0:1]) * inside
    am, bm = a_ref[2 * nf].astype(F32), b_ref[2 * nf].astype(F32)
    ms[0] = jnp.where(even, bm, am)
    ms[1] = jnp.where(even, am, bm)
    ms[2] = c1_ref[4 * nf + 1].astype(F32)
    ms[3] = c1_ref[2 * nf].astype(F32)

    @pl.when(stream == 0)
    def _():
        start = lax.axis_index("gy") * ny
        if two:
            whole = 2 * ny
            mine = jnp.broadcast_to(imap[...].astype(F32), (1, ny))
            other = c2l_ref[0, pl.ds(ny, 16)].astype(F32)[6:7, :ny]
            mapping = jnp.concatenate([mine, other], axis=1)
            order = start
        else:
            whole = face_ref.shape[1]
            mapping = map_ref[...].astype(F32)
            order = 0
        rows = ny + 8
        r = lax.broadcasted_iota(jnp.int32, (rows, whole), 0)
        want = jnp.where(r < ny, r, jnp.where(r == ny, whole - 1, ny)) + start
        want = jnp.where(want >= whole, want - whole, want).astype(F32)
        t = lax.broadcasted_iota(jnp.int32, (rows, whole), 1) + order
        t = jnp.where(t >= whole, t - whole, t).astype(F32)
        u = lax.broadcasted_iota(jnp.int32, (whole, whole), 0) + order
        u = jnp.where(u >= whole, u - whole, u).astype(F32)
        one = lambda x: jnp.where(x, 1.0, 0.0)
        pick = one(t == want).astype(BF)
        targets = one(jnp.broadcast_to(mapping, (whole, whole)) == u).astype(BF)
        inlet = lax.dot_general(pick, targets, (((1,), (1,)), ((), ())), preferred_element_type=F32)
        feed = one(jnp.broadcast_to(mapping, (rows, whole)) == want)
        choose = jnp.where(comp == 1, inlet, feed).astype(BF)
        for f in range(nf):
            if two:
                face = jnp.concatenate([b_ref[2 * f], c2l_ref[f, pl.ds(0, ny)]], axis=0)
            else:
                face = face_ref[f]
            ghost = jnp.dot(choose, face, preferred_element_type=F32)
            lay[LO, f] = ghost[:ny]
            cor[0, f : f + 1] = ghost[ny : ny + 1]
            cor[1, f : f + 1] = ghost[ny + 1 : ny + 2]

    sub = lax.broadcasted_iota(jnp.int32, (8, nz), 0)
    every = range(parts)

    def held(ref, *at):
        return lambda f, k: ref[(*at, f, pl.ds(k, 8, stride=parts))]

    def q_layer(x):
        return lambda f, k: q_ref[f, pl.ds(x * ny + k, 8, stride=parts)]

    def q_plane(y):
        return held(qp, 0 if y == 0 else 1)

    def s_layer(x):
        return lambda k: s_ref[pl.ds(x * ny + k, 8, stride=parts)] >= level

    def s_plane(y):
        return lambda k: s_ref[pl.ds(k * ny + y, 8, stride=parts * ny)] >= level

    def s_halo(n):
        edge = level.astype(F32)
        return lambda k: ms[n, pl.ds(k, 8, stride=parts)] >= edge

    def gains(src):
        return [gain(src(4, k)) for k in every]

    def line(src, r):
        return lambda f: src(f, r % parts)[r // parts : r // parts + 1]

    def corner(n):
        return lambda f: cor[n, f : f + 1]

    def got_line(ref, n, r):
        return lambda f: ref[n, f, r : r + 1]

    def put(ref, n, vals):
        for f in range(nf):
            for k in every:
                ref[n, f, pl.ds(k, 8, stride=parts)] = vals[f][k]

    def products(centers):
        gs = []
        for n, src in enumerate(centers):
            gs.append(gains(src))
            tall = [src(f, k) for f in range(nf) for k in every] + gs[-1]
            zin[pl.ds(n * (nf + 1) * ny, (nf + 1) * ny)] = jnp.concatenate(tall, 0).astype(BF)
        zout[...] = jnp.dot(zin[...], sm[...], preferred_element_type=F32)
        return gs

    def slab(n, g, center, before, after, low, high, solid, along_outer):
        def z(f, k, h):
            return zout[(n * (nf + 1) + f) * ny + 8 * k : (n * (nf + 1) + f) * ny + 8 * k + 8, h * nz : (h + 1) * nz]

        def ups(v, edge):
            return v[1:] + [jnp.where(sub == 7, edge, pltpu.roll(v[0], 7, 0))]

        def downs(v, edge):
            return [jnp.where(sub == 0, edge, pltpu.roll(v[-1], 1, 0))] + v[:-1]

        gb, ga = gains(before), gains(after)
        gu, gd = ups(g, gain(high(4))), downs(g, gain(low(4)))
        ga, gb, gu, gd = ([x + y for x, y in zip(g, v)] for v in (ga, gb, gu, gd))
        gz = [2.0 * g[k] + z(nf, k, 0) for k in every]
        gzl = [2.0 * g[k] - z(nf, k, 1) for k in every]
        ma = [masks(solid(k)) for k in every]
        res = []
        for f in range(nf):
            q = [center(f, k) for k in every]
            qu, qd = ups(q, high(f)), downs(q, low(f))
            vals = []
            for k in every:
                da, db, du, dd = after(f, k) - q[k], q[k] - before(f, k), qu[k] - q[k], q[k] - qd[k]
                total = ga[k] * da - gb[k] * db + (gu[k] * du - gd[k] * dd)
                total += gz[k] * z(f, k, 0) - gzl[k] * z(f, k, 1)
                grad = da + db if along_outer else du + dd
                vals.append(q[k] + (d[f] * (ma[k][0] * total) - c[f] * (ma[k][1] * grad)))
            res.append(vals)
        return res

    def passed(here, there, solid, along_x, ahead):
        g = [x + y for x, y in zip(gains(here), gains(there))]
        ma = [masks(solid(k)) for k in every]
        res = []
        for f in range(nf):
            vals = []
            for k in every:
                diff = there(f, k) - here(f, k)
                add = d[f] * (ma[k][0] * (g[k] * diff))
                if along_x:
                    half = c[f] * (ma[k][1] * diff)
                    add = add - half if ahead else add + half
                vals.append(add)
            res.append(vals)
        return res

    g = products([held(lay, LO), held(lay, HI), held(pla, LO), held(pla, HI)])
    put(fl, 0, slab(0, g[0], held(lay, LO), held(lay, FAR_LO), q_layer(0), corner(0), corner(1), s_halo(0), True))
    put(fl, 5, slab(1, g[1], held(lay, HI), q_layer(nx - 1), held(lay, FAR_HI), corner(2), corner(3), s_halo(1), True))
    put(fp, 0, slab(2, g[2], held(pla, LO), held(pla, FAR_LO), q_plane(0), corner(0), corner(2), s_halo(2), False))
    put(fp, 5, slab(3, g[3], held(pla, HI), q_plane(ny - 1), held(pla, FAR_HI), corner(1), corner(3), s_halo(3), False))

    @pl.when(stream == 0)
    def _():
        fl[0] = lay[LO]

    @pl.when(stream == last)
    def _():
        fl[5] = jnp.zeros(fl.shape[1:], F32)

    put(cx, 0, passed(q_layer(0), held(lay, LO), s_layer(0), True, False))
    put(cx, 1, passed(q_layer(nx - 1), held(lay, HI), s_layer(nx - 1), True, True))
    put(cy, 0, passed(q_plane(0), held(pla, LO), s_plane(0), False, False))
    put(cy, 1, passed(q_plane(ny - 1), held(pla, HI), s_plane(ny - 1), False, True))
    for f in range(nf):
        for n, x in ((1, 0), (2, 1), (3, nx - 2), (4, nx - 1)):
            v = first_ref[f, x * ny : (x + 1) * ny]
            fl[n, f] = v + cx[n // 4, f] if n in (1, 4) else v
            fl[n, f, 0:1] += cy[0, f, x : x + 1]
            fl[n, f, ny - 1 : ny] += cy[1, f, x : x + 1]
        for n, y in ((1, 0), (2, 1), (3, ny - 2), (4, ny - 1)):
            v = first_ref[f, pl.ds(y, nx, stride=ny)]
            fp[n, f] = v + cy[n // 4, f] if n in (1, 4) else v
            fp[n, f, 0:1] += cx[0, f, y : y + 1]
            fp[n, f, nx - 1 : nx] += cx[1, f, y : y + 1]

    g = products([held(fl, 1), held(fl, 4), held(fp, 1), held(fp, 4)])

    def ended(src, vals):
        return [[0.5 * (src(f, k) + vals[f][k]) for k in every] for f in range(nf)]

    copies = []
    put(ep, 0, passed(held(fp, 2), held(fp, 1), s_plane(1), False, False))
    put(ep, 1, passed(held(fp, 3), held(fp, 4), s_plane(ny - 2), False, True))
    for n, (m, y, end, near) in enumerate(((1, 0, 0, 1), (4, ny - 1, 7, 6))):
        vals = slab(2 + n, g[2 + n], held(fp, m), held(fp, m - 1), held(fp, m + 1), got_line(fl, 0, y),
                    got_line(fl, 5, y), s_plane(y), False)
        put(cy, n, ended(q_plane(y), vals))
        cuts[n].wait()
        for f in range(nf):
            strips[n, f, :, end] = cy[n, f]
            strips[n, f, :, near] += 0.5 * ep[n, f]
        copies.append(pltpu.make_async_copy(
            strips.at[n, :, pl.ds(2, nx - 4)],
            out_ref.at[:, pl.ds(2, nx - 4), pl.ds(n * (ny - 8), 8)], sem.at[3, n]))
        copies[-1].start()
    put(cx, 0, passed(held(fl, 2), held(fl, 1), s_layer(1), True, False))
    put(cx, 1, passed(held(fl, 3), held(fl, 4), s_layer(nx - 2), True, True))
    for n, (m, x, near) in enumerate(((1, 0, 1), (4, nx - 1, nx - 2))):
        for f in range(nf):
            k = n + 1
            ol[k, f] = main_ref[f, near] + 0.5 * cx[n, f]
            ol[k, f, 0:1] = cy[0, f, near : near + 1]
            ol[k, f, 1:2] += 0.5 * ep[0, f, near : near + 1]
            ol[k, f, ny - 2 : ny - 1] += 0.5 * ep[1, f, near : near + 1]
            ol[k, f, ny - 1 : ny] = cy[1, f, near : near + 1]
        copies.append(pltpu.make_async_copy(ol.at[k], out_ref.at[:, near], sem.at[2, k]))
        copies[-1].start()
        vals = slab(n, g[n], held(fl, m), held(fl, m - 1), held(fl, m + 1), got_line(fp, 0, x), got_line(fp, 5, x),
                    s_layer(x), True)
        put(ol, 3 * n, ended(q_layer(x), vals))
        copies.append(pltpu.make_async_copy(ol.at[3 * n], out_ref.at[:, x], sem.at[2, 3 * n]))
        copies[-1].start()
    for copy in mids + copies:
        copy.wait()


VM = pl.BlockSpec(memory_space=pltpu.VMEM)
SM = pl.BlockSpec(memory_space=pltpu.SMEM)
HB = pl.BlockSpec(memory_space=pl.ANY)


def body(sizes, state, diffusivity, advection, solid_mask, iface_map):
    ngx, ngy = sizes
    q = state[0]
    nf, nx, ny, nz = q.shape
    dims = nf, nx, ny, nz
    two = ngy == 2

    flat, solid = q.reshape(nf, nx * ny, nz), solid_mask.reshape(nx * ny, nz)
    send_a, send_b, send_c = pl.pallas_call(
        functools.partial(gather_kernel, dims),
        out_shape=[jax.ShapeDtypeStruct((n, ny, nz), BF) for n in (2 * nf + 1, 2 * nf + 1, 4 * nf + 2)],
        in_specs=[VM] * 2,
        out_specs=[VM] * 3,
        compiler_params=pltpu.CompilerParams(vmem_limit_bytes=2 << 20),
    )(flat, solid)

    if two:
        swap = [(0, 1), (1, 0)]
        c1 = lax.ppermute(send_c, "gy", swap)
    else:
        up = [(j, (j + 1) % ngy) for j in range(ngy)]
        down = [(b, a) for a, b in up]
        half = 2 * nf + 1
        c1 = jnp.concatenate([lax.ppermute(send_c[:half], "gy", down), lax.ppermute(send_c[half:], "gy", up)], 0)

    def both(pairs):
        return pairs + [(b, a) for a, b in pairs]

    inner = both([(k, k + 1) for k in range(0, ngx, 2)])
    a = lax.ppermute(send_a, "gx", inner)
    outer = [(k * ngx + i, k * ngx + i + 1) for k in range(2) for i in range(1, ngx - 1, 2)]
    b = lax.ppermute(send_b, ("comp", "gx"), both(outer + [(0, ngx)]))

    shape = jax.ShapeDtypeStruct((nf, nx * ny, nz), F32)
    cells = nf * nx * ny * nz

    def section(second, *args):
        return pl.pallas_call(
            functools.partial(section_kernel, dims, second),
            out_shape=shape,
            in_specs=[SM, SM] + [VM] * (len(args) + 1),
            out_specs=VM,
            scratch_shapes=[pltpu.VMEM((nf, ny // 8, 8, nz), F32), pltpu.VMEM((2, 5, ny // 8, 8, nz), F32)],
            compiler_params=pltpu.CompilerParams(vmem_limit_bytes=3 << 20),
            cost_estimate=pl.CostEstimate(flops=20 * cells, bytes_accessed=8 * cells, transcendentals=cells // 4),
        )(diffusivity, advection, *args, solid)

    first = section(False, flat)
    map_line = iface_map.reshape(1, ny)
    extra = pl.pallas_call(
        functools.partial(relay_kernel, dims),
        out_shape=jax.ShapeDtypeStruct((nf, ny + 16, nz), BF),
        in_specs=[VM] * 3 + [HB],
        out_specs=VM,
        scratch_shapes=[pltpu.VMEM((16, nz), F32)],
        compiler_params=pltpu.CompilerParams(vmem_limit_bytes=1 << 20),
    )(map_line, a, b, first)
    if two:
        c2 = lax.ppermute(extra, "gy", swap)
        c2l, c2h, more = c2, c2, []
    else:
        c2l, c2h = lax.ppermute(extra, "gy", up), lax.ppermute(extra, "gy", down)
        more = [lax.all_gather(b[: 2 * nf : 2], "gy", axis=1, tiled=True),
                lax.all_gather(iface_map, "gy", axis=0, tiled=True).reshape(1, -1)]

    main = section(True, flat, first)
    mb = pltpu.VMEM
    return pl.pallas_call(
        functools.partial(border_kernel, dims, two),
        out_shape=jax.ShapeDtypeStruct((nf, nx, ny, nz), F32),
        in_specs=[SM, SM, VM] + [VM] * (9 + len(more)),
        out_specs=HB,
        scratch_shapes=[
            mb((nz, 2 * nz), BF), mb((4, nf, ny, nz), F32), mb((4, nf, nx, nz), F32), mb((2, nf, nx, nz), F32), mb((4, ny, nz), F32),
            mb((4, 8, nz), F32), mb((6, nf, ny, nz), F32), mb((6, nf, nx, nz), F32), mb((2, nf, ny, nz), F32),
            mb((2, nf, nx, nz), F32), mb((2, nf, nx, nz), F32), mb((4, nf, ny, nz), F32), mb((2, nf, nx, 8, nz), F32),
            mb((4 * (nf + 1) * ny, nz), BF), mb((4 * (nf + 1) * ny, 2 * nz), F32),
            pltpu.SemaphoreType.DMA((4, 8)),
        ],
        compiler_params=pltpu.CompilerParams(vmem_limit_bytes=10 << 20),
        cost_estimate=pl.CostEstimate(flops=10 * cells, bytes_accessed=8 * cells, transcendentals=cells // 4),
    )(diffusivity, advection, map_line, flat, first, main.reshape(nf, nx, ny, nz), solid,
      a, b, c1, c2l, c2h, *more)[None]


def solution(mesh):
    sizes = mesh.shape["gx"], mesh.shape["gy"]
    return jax.shard_map(
        functools.partial(body, sizes),
        mesh=mesh,
        in_specs=(P("comp", None, "gx", "gy", None), P(), P(), P("gx", "gy", None), P("gy")),
        out_specs=P("comp", None, "gx", "gy", None),
        check_vma=False,
    )
```

```python
import functools

import jax
import jax.numpy as jnp
from jax import lax
from jax.experimental import pallas as pl
from jax.experimental.pallas import tpu as pltpu
from jax.sharding import PartitionSpec as P

RATIO = 1.5
GAIN = 0.4
LOG2E = 1.4426950408889634
BF = jnp.bfloat16
F32 = jnp.float32


def gain(q):
    return jnp.exp2(GAIN * LOG2E * jnp.tanh(q) - 1.0)


def shift_matrix(nz):
    row = lax.broadcasted_iota(jnp.int32, (nz, 2 * nz), 0)
    col = lax.broadcasted_iota(jnp.int32, (nz, 2 * nz), 1)
    k = jnp.where(col < nz, col, col - nz)
    up = jnp.where(k + 1 == nz, 0, k + 1)
    down = jnp.where(k == 0, nz - 1, k - 1)
    one = lambda c: jnp.where(c, 1.0, 0.0)
    own = one(row == k)
    return jnp.where(col < nz, one(row == up) - own, own - one(row == down)).astype(BF)


def scalars(dif, adv, nf):
    comp = lax.axis_index("comp")
    sign = (2 * comp - 1).astype(F32)
    return [dif[comp, f] for f in range(nf)], [adv[comp, f] * sign for f in range(nf)], 2 - comp


def masks(solid):
    return jnp.where(solid, RATIO, 1.0), jnp.where(solid, 0.0, 0.5)


def gather_kernel(dims, q_ref, s_ref, a_ref, b_ref, c_ref):
    nf, nx, ny, nz = dims
    even = lax.axis_index("gx") % 2 == 0
    def layer(ref, f, k):
        at = pl.multiple_of(k * ny, ny)
        return (ref[pl.ds(at, ny)] if f is None else ref[f, pl.ds(at, ny)]).astype(F32).astype(BF)

    a0, b0 = jnp.where(even, nx - 2, 0), jnp.where(even, 0, nx - 2)
    a1, b1 = jnp.where(even, nx - 1, 0), jnp.where(even, 0, nx - 1)
    for f in range(nf):
        for k in range(2):
            a_ref[2 * f + k] = layer(q_ref, f, a0 + k)
            b_ref[2 * f + k] = layer(q_ref, f, b0 + k)
        for k, y in enumerate((0, 1, ny - 2, ny - 1)):
            c_ref[k * nf + k // 2 + f] = q_ref[f, pl.ds(y, nx, stride=ny)].astype(BF)
    a_ref[2 * nf] = layer(s_ref, None, a1)
    b_ref[2 * nf] = layer(s_ref, None, b1)
    for k, y in ((2 * nf, 0), (4 * nf + 1, ny - 1)):
        c_ref[k] = s_ref[pl.ds(y, nx, stride=ny)].astype(F32).astype(BF)


def relay_kernel(dims, imap, a_ref, b_ref, after_ref, o_ref, rows):
    nf, nx, ny, nz = dims
    rows[...] = jnp.zeros_like(rows)
    rows[6:7, :ny] = imap[...].astype(F32)
    for f in range(nf):
        o_ref[f, :ny] = b_ref[2 * f]
        for k, (src, n) in enumerate(((a_ref, 2 * f), (a_ref, 2 * f + 1), (b_ref, 2 * f + 1))):
            block = src[n].astype(F32)
            rows[2 * k : 2 * k + 1] = block[:1]
            rows[2 * k + 1 : 2 * k + 2] = block[ny - 1 :]
        o_ref[f, ny:] = rows[...].astype(BF)


def shift_pair(nz, down):
    row = lax.broadcasted_iota(jnp.int32, (2 * nz, 2 * nz), 0)
    col = lax.broadcasted_iota(jnp.int32, (2 * nz, 2 * nz), 1)
    second = col >= nz
    k = jnp.where(second, col - nz, col)
    if down:
        other = jnp.where(k == 0, nz - 1, k - 1)
    else:
        other = jnp.where(k == nz - 1, 0, k + 1)
    other = jnp.where(second, other + nz, other)
    one = lambda c: jnp.where(c, 1.0, 0.0)
    diff = one(row == other) - one(row == col)
    return (-diff if down else diff).astype(BF)


def section_kernel(dims, second, *refs):
    nf, nx, ny, nz = dims
    pairs = [(6, None), (4, 5), (0, 1), (2, 3)]
    parts = ny // 8

    def run(*accs):
        if second:
            dif, adv, base_ref, q_ref, s_ref, o_ref, fx, gs = refs
        else:
            dif, adv, q_ref, s_ref, o_ref, fx, gs = refs
        n = len(pairs)
        ups, downs = (accs[:n], accs[n : 2 * n]), (accs[2 * n : 3 * n], accs[3 * n :])
        d, c, level = scalars(dif, adv, nf)
        lo, hi = (1, nx - 2) if second else (0, nx - 1)
        closed = (0, ny - 2) if second else (ny - 1,)
        sub = lax.broadcasted_iota(jnp.int32, (8, nz), 0)
        fx[...] = jnp.zeros_like(fx)
        pltpu.matmul_push_rhs(shift_pair(nz, False), staging_register=0, mxu_index=0)
        pltpu.matmul_push_rhs(shift_pair(nz, True), staging_register=0, mxu_index=1)

        def at(x, k):
            return pl.ds(x * ny + k, 8, stride=parts)

        def layer(f, x):
            return [q_ref[f, at(x, k)] for k in range(parts)]

        def tall(v):
            return jnp.concatenate(v, 0).astype(BF)

        def push(x, bank, g, load=None):
            for p, (f0, f1) in enumerate(pairs):
                lhs = jnp.concatenate([tall(layer(f0, x)), tall(g if f1 is None else layer(f1, x))], 1)
                pltpu.matmul_acc_lhs(ups[bank][p], lhs, load_staged_rhs=load)
                pltpu.matmul_acc_lhs(downs[bank][p], lhs, load_staged_rhs=load)
                load = None

        def prepare(x, bank, g):
            ge = [gain(v) for v in layer(4, jnp.minimum(x + 1, hi))]
            for k in range(parts):
                gs[bank, 0, k] = g[k] + ge[k]
                face = g[k] + (g[k + 1] if k + 1 < parts else pltpu.roll(g[0], 7, 0))
                for y in closed:
                    if y % parts == k:
                        face = jnp.where(sub == y // parts, 0.0, face)
                gs[bank, 1, k] = face
                gs[bank, 2, k] = g[k] + g[k]
                m, a = masks(s_ref[at(jnp.minimum(x, hi), k)] >= level)
                gs[bank, 3, k] = m
                gs[bank, 4, k] = a
            return ge

        def compute(x, bank):
            xe, xw = jnp.minimum(x + 1, hi), jnp.maximum(x - 1, lo)
            for p, pair in enumerate(pairs):
                up, down = pltpu.matmul_pop(ups[bank][p]), pltpu.matmul_pop(downs[bank][p])
                piece = lambda v, k, h: v[8 * k : 8 * k + 8, h * nz : (h + 1) * nz]
                if pair[1] is None:
                    gz = [gs[bank, 2, k] + piece(up, k, 1) for k in range(parts)]
                    gzl = [gs[bank, 2, k] - piece(down, k, 1) for k in range(parts)]
                for h, f in enumerate(pair):
                    if f is None:
                        continue
                    q = layer(f, x)
                    fy = [gs[bank, 1, k] * ((q[k + 1] if k + 1 < parts else pltpu.roll(q[0], 7, 0)) - q[k])
                          for k in range(parts)]
                    for k in range(parts):
                        qe, qw = q_ref[f, at(xe, k)], q_ref[f, at(xw, k)]
                        flux = gs[bank, 0, k] * (qe - q[k])
                        total = flux - fx[f, k]
                        fx[f, k] = flux
                        total += fy[k] - (fy[k - 1] if k else pltpu.roll(fy[-1], 1, 0))
                        total += gz[k] * piece(up, k, h) - gzl[k] * piece(down, k, h)
                        new = q[k] + (d[f] * (gs[bank, 3, k] * total) - c[f] * (gs[bank, 4, k] * (qe - qw)))
                        if second:
                            new = 0.5 * (base_ref[f, at(x, k)] + new)
                        o_ref[f, at(x, k)] = new

        def step(i, g):
            x = 2 * i + lo
            push(x + 1, 1, g)
            g = prepare(x + 1, 1, g)
            compute(x, 0)
            push(jnp.minimum(x + 2, hi), 0, g)
            g = prepare(x + 2, 0, g)
            compute(x + 1, 1)
            return g

        g = [gain(v) for v in layer(4, lo)]
        push(lo, 0, g, 0)
        lax.fori_loop(0, (hi + 1 - lo) // 2, step, prepare(lo, 0, g))
        for acc in ups[0] + downs[0]:
            pltpu.matmul_pop(acc)

    accs = [pltpu.ACC(m)((ny, 2 * nz), F32) for m in (0, 1) for _ in range(2 * len(pairs))]
    pl.run_scoped(run, *accs)


def border_kernel(dims, two, *refs):
    nf, nx, ny, nz = dims
    if two:
        dif, adv, imap, q_ref, first_ref, main_ref, s_ref, a_ref, b_ref, c1_ref, c2l_ref, c2h_ref = refs[:12]
        rest = refs[12:]
    else:
        (dif, adv, imap, q_ref, first_ref, main_ref, s_ref, a_ref, b_ref, c1_ref, c2l_ref, c2h_ref,
         face_ref, map_ref) = refs[:14]
        rest = refs[14:]
    out_ref, sm, lay, pla, qp, ms, cor, fl, fp, cx, cy, ep, ol, strips, zin, zout, sem = rest
    d, c, level = scalars(dif, adv, nf)
    comp = lax.axis_index("comp")
    stream, last = lax.axis_index("gx"), lax.axis_size("gx") - 1
    even = stream % 2 == 0
    parts = ny // 8
    sm[...] = shift_matrix(nz)

    mids = []
    for f in range(nf):
        mids.append(pltpu.make_async_copy(
            main_ref.at[f, pl.ds(2, nx - 4), pl.ds(8, ny - 16)],
            out_ref.at[f, pl.ds(2, nx - 4), pl.ds(8, ny - 16)], sem.at[0, f]))
        mids[-1].start()
    cuts = []
    for k, row in enumerate((0, ny - 8)):
        cuts.append(pltpu.make_async_copy(main_ref.at[:, :, pl.ds(row, 8)], strips.at[k], sem.at[1, k]))
        cuts[-1].start()

    FAR_LO, LO, HI, FAR_HI = range(4)
    inside = jnp.where(stream == last, 0.0, 1.0)
    for f in range(nf):
        av = [a_ref[2 * f].astype(F32), a_ref[2 * f + 1].astype(F32)]
        bv = [b_ref[2 * f].astype(F32), b_ref[2 * f + 1].astype(F32)]
        lay[FAR_LO, f] = jnp.where(even, bv[0], av[0])
        lay[LO, f] = jnp.where(even, bv[1], av[1])
        lay[HI, f] = jnp.where(even, av[0], bv[0]) * inside
        lay[FAR_HI, f] = jnp.where(even, av[1], bv[1]) * inside
        for n, k in enumerate((2 * nf + 1, 3 * nf + 1, 0, nf)):
            pla[n, f] = c1_ref[k + f].astype(F32)
        for n, y in enumerate((0, ny - 1)):
            qp[n, f] = q_ref[f, pl.ds(y, nx, stride=ny)]
        lo, hi = c2l_ref[f, pl.ds(ny, 16)].astype(F32), c2h_ref[f, pl.ds(ny, 16)].astype(F32)
        lo_b, hi_b = c2l_ref[f, pl.ds(ny - 16, 16)].astype(F32), c2h_ref[f, pl.ds(0, 16)].astype(F32)
        cor[0, f : f + 1] = jnp.where(even, lo[5:6], lo[3:4])
        cor[1, f : f + 1] = jnp.where(even, hi[4:5], hi[2:3])
        cor[2, f : f + 1] = jnp.where(even, lo[1:2], lo_b[15:16]) * inside
        cor[3, f : f + 1] = jnp.where(even, hi[0:1], hi_b[0:1]) * inside
    am, bm = a_ref[2 * nf].astype(F32), b_ref[2 * nf].astype(F32)
    ms[0] = jnp.where(even, bm, am)
    ms[1] = jnp.where(even, am, bm)
    ms[2] = c1_ref[4 * nf + 1].astype(F32)
    ms[3] = c1_ref[2 * nf].astype(F32)

    @pl.when(stream == 0)
    def _():
        start = lax.axis_index("gy") * ny
        if two:
            whole = 2 * ny
            mine = jnp.broadcast_to(imap[...].astype(F32), (1, ny))
            other = c2l_ref[0, pl.ds(ny, 16)].astype(F32)[6:7, :ny]
            mapping = jnp.concatenate([mine, other], axis=1)
            order = start
        else:
            whole = face_ref.shape[1]
            mapping = map_ref[...].astype(F32)
            order = 0
        rows = ny + 8
        r = lax.broadcasted_iota(jnp.int32, (rows, whole), 0)
        want = jnp.where(r < ny, r, jnp.where(r == ny, whole - 1, ny)) + start
        want = jnp.where(want >= whole, want - whole, want).astype(F32)
        t = lax.broadcasted_iota(jnp.int32, (rows, whole), 1) + order
        t = jnp.where(t >= whole, t - whole, t).astype(F32)
        u = lax.broadcasted_iota(jnp.int32, (whole, whole), 0) + order
        u = jnp.where(u >= whole, u - whole, u).astype(F32)
        one = lambda x: jnp.where(x, 1.0, 0.0)
        pick = one(t == want).astype(BF)
        targets = one(jnp.broadcast_to(mapping, (whole, whole)) == u).astype(BF)
        inlet = lax.dot_general(pick, targets, (((1,), (1,)), ((), ())), preferred_element_type=F32)
        feed = one(jnp.broadcast_to(mapping, (rows, whole)) == want)
        choose = jnp.where(comp == 1, inlet, feed).astype(BF)
        for f in range(nf):
            if two:
                face = jnp.concatenate([b_ref[2 * f], c2l_ref[f, pl.ds(0, ny)]], axis=0)
            else:
                face = face_ref[f]
            ghost = jnp.dot(choose, face, preferred_element_type=F32)
            lay[LO, f] = ghost[:ny]
            cor[0, f : f + 1] = ghost[ny : ny + 1]
            cor[1, f : f + 1] = ghost[ny + 1 : ny + 2]

    sub = lax.broadcasted_iota(jnp.int32, (8, nz), 0)
    every = range(parts)

    def held(ref, *at):
        return lambda f, k: ref[(*at, f, pl.ds(k, 8, stride=parts))]

    def q_layer(x):
        return lambda f, k: q_ref[f, pl.ds(x * ny + k, 8, stride=parts)]

    def q_plane(y):
        return held(qp, 0 if y == 0 else 1)

    def s_layer(x):
        return lambda k: s_ref[pl.ds(x * ny + k, 8, stride=parts)] >= level

    def s_plane(y):
        return lambda k: s_ref[pl.ds(k * ny + y, 8, stride=parts * ny)] >= level

    def s_halo(n):
        edge = level.astype(F32)
        return lambda k: ms[n, pl.ds(k, 8, stride=parts)] >= edge

    def gains(src):
        return [gain(src(4, k)) for k in every]

    def line(src, r):
        return lambda f: src(f, r % parts)[r // parts : r // parts + 1]

    def corner(n):
        return lambda f: cor[n, f : f + 1]

    def got_line(ref, n, r):
        return lambda f: ref[n, f, r : r + 1]

    def put(ref, n, vals):
        for f in range(nf):
            for k in every:
                ref[n, f, pl.ds(k, 8, stride=parts)] = vals[f][k]

    def products(centers):
        gs = []
        for n, src in enumerate(centers):
            gs.append(gains(src))
            tall = [src(f, k) for f in range(nf) for k in every] + gs[-1]
            zin[pl.ds(n * (nf + 1) * ny, (nf + 1) * ny)] = jnp.concatenate(tall, 0).astype(BF)
        zout[...] = jnp.dot(zin[...], sm[...], preferred_element_type=F32)
        return gs

    def slab(n, g, center, before, after, low, high, solid, along_outer):
        def z(f, k, h):
            return zout[(n * (nf + 1) + f) * ny + 8 * k : (n * (nf + 1) + f) * ny + 8 * k + 8, h * nz : (h + 1) * nz]

        def ups(v, edge):
            return v[1:] + [jnp.where(sub == 7, edge, pltpu.roll(v[0], 7, 0))]

        def downs(v, edge):
            return [jnp.where(sub == 0, edge, pltpu.roll(v[-1], 1, 0))] + v[:-1]

        gb, ga = gains(before), gains(after)
        gu, gd = ups(g, gain(high(4))), downs(g, gain(low(4)))
        ga, gb, gu, gd = ([x + y for x, y in zip(g, v)] for v in (ga, gb, gu, gd))
        gz = [2.0 * g[k] + z(nf, k, 0) for k in every]
        gzl = [2.0 * g[k] - z(nf, k, 1) for k in every]
        ma = [masks(solid(k)) for k in every]
        res = []
        for f in range(nf):
            q = [center(f, k) for k in every]
            qu, qd = ups(q, high(f)), downs(q, low(f))
            vals = []
            for k in every:
                da, db, du, dd = after(f, k) - q[k], q[k] - before(f, k), qu[k] - q[k], q[k] - qd[k]
                total = ga[k] * da - gb[k] * db + (gu[k] * du - gd[k] * dd)
                total += gz[k] * z(f, k, 0) - gzl[k] * z(f, k, 1)
                grad = da + db if along_outer else du + dd
                vals.append(q[k] + (d[f] * (ma[k][0] * total) - c[f] * (ma[k][1] * grad)))
            res.append(vals)
        return res

    def passed(here, there, solid, along_x, ahead):
        g = [x + y for x, y in zip(gains(here), gains(there))]
        ma = [masks(solid(k)) for k in every]
        res = []
        for f in range(nf):
            vals = []
            for k in every:
                diff = there(f, k) - here(f, k)
                add = d[f] * (ma[k][0] * (g[k] * diff))
                if along_x:
                    half = c[f] * (ma[k][1] * diff)
                    add = add - half if ahead else add + half
                vals.append(add)
            res.append(vals)
        return res

    g = products([held(lay, LO), held(lay, HI), held(pla, LO), held(pla, HI)])
    put(fl, 0, slab(0, g[0], held(lay, LO), held(lay, FAR_LO), q_layer(0), corner(0), corner(1), s_halo(0), True))
    put(fl, 5, slab(1, g[1], held(lay, HI), q_layer(nx - 1), held(lay, FAR_HI), corner(2), corner(3), s_halo(1), True))
    put(fp, 0, slab(2, g[2], held(pla, LO), held(pla, FAR_LO), q_plane(0), corner(0), corner(2), s_halo(2), False))
    put(fp, 5, slab(3, g[3], held(pla, HI), q_plane(ny - 1), held(pla, FAR_HI), corner(1), corner(3), s_halo(3), False))

    @pl.when(stream == 0)
    def _():
        fl[0] = lay[LO]

    @pl.when(stream == last)
    def _():
        fl[5] = jnp.zeros(fl.shape[1:], F32)

    put(cx, 0, passed(q_layer(0), held(lay, LO), s_layer(0), True, False))
    put(cx, 1, passed(q_layer(nx - 1), held(lay, HI), s_layer(nx - 1), True, True))
    put(cy, 0, passed(q_plane(0), held(pla, LO), s_plane(0), False, False))
    put(cy, 1, passed(q_plane(ny - 1), held(pla, HI), s_plane(ny - 1), False, True))
    for f in range(nf):
        for n, x in ((1, 0), (2, 1), (3, nx - 2), (4, nx - 1)):
            v = first_ref[f, x * ny : (x + 1) * ny]
            fl[n, f] = v + cx[n // 4, f] if n in (1, 4) else v
            fl[n, f, 0:1] += cy[0, f, x : x + 1]
            fl[n, f, ny - 1 : ny] += cy[1, f, x : x + 1]
        for n, y in ((1, 0), (2, 1), (3, ny - 2), (4, ny - 1)):
            v = first_ref[f, pl.ds(y, nx, stride=ny)]
            fp[n, f] = v + cy[n // 4, f] if n in (1, 4) else v
            fp[n, f, 0:1] += cx[0, f, y : y + 1]
            fp[n, f, nx - 1 : nx] += cx[1, f, y : y + 1]

    g = products([held(fl, 1), held(fl, 4), held(fp, 1), held(fp, 4)])

    def ended(src, vals):
        return [[0.5 * (src(f, k) + vals[f][k]) for k in every] for f in range(nf)]

    copies = []
    put(ep, 0, passed(held(fp, 2), held(fp, 1), s_plane(1), False, False))
    put(ep, 1, passed(held(fp, 3), held(fp, 4), s_plane(ny - 2), False, True))
    for n, (m, y, end, near) in enumerate(((1, 0, 0, 1), (4, ny - 1, 7, 6))):
        vals = slab(2 + n, g[2 + n], held(fp, m), held(fp, m - 1), held(fp, m + 1), got_line(fl, 0, y),
                    got_line(fl, 5, y), s_plane(y), False)
        put(cy, n, ended(q_plane(y), vals))
        cuts[n].wait()
        for f in range(nf):
            strips[n, f, :, end] = cy[n, f]
            strips[n, f, :, near] += 0.5 * ep[n, f]
        copies.append(pltpu.make_async_copy(
            strips.at[n, :, pl.ds(2, nx - 4)],
            out_ref.at[:, pl.ds(2, nx - 4), pl.ds(n * (ny - 8), 8)], sem.at[3, n]))
        copies[-1].start()
    put(cx, 0, passed(held(fl, 2), held(fl, 1), s_layer(1), True, False))
    put(cx, 1, passed(held(fl, 3), held(fl, 4), s_layer(nx - 2), True, True))
    for n, (m, x, near) in enumerate(((1, 0, 1), (4, nx - 1, nx - 2))):
        for f in range(nf):
            k = n + 1
            ol[k, f] = main_ref[f, near] + 0.5 * cx[n, f]
            ol[k, f, 0:1] = cy[0, f, near : near + 1]
            ol[k, f, 1:2] += 0.5 * ep[0, f, near : near + 1]
            ol[k, f, ny - 2 : ny - 1] += 0.5 * ep[1, f, near : near + 1]
            ol[k, f, ny - 1 : ny] = cy[1, f, near : near + 1]
        copies.append(pltpu.make_async_copy(ol.at[k], out_ref.at[:, near], sem.at[2, k]))
        copies[-1].start()
        vals = slab(n, g[n], held(fl, m), held(fl, m - 1), held(fl, m + 1), got_line(fp, 0, x), got_line(fp, 5, x),
                    s_layer(x), True)
        put(ol, 3 * n, ended(q_layer(x), vals))
        copies.append(pltpu.make_async_copy(ol.at[3 * n], out_ref.at[:, x], sem.at[2, 3 * n]))
        copies[-1].start()
    for copy in mids + copies:
        copy.wait()


VM = pl.BlockSpec(memory_space=pltpu.VMEM)
SM = pl.BlockSpec(memory_space=pltpu.SMEM)
HB = pl.BlockSpec(memory_space=pl.ANY)


def body(sizes, state, diffusivity, advection, solid_mask, iface_map):
    ngx, ngy = sizes
    q = state[0]
    nf, nx, ny, nz = q.shape
    dims = nf, nx, ny, nz
    two = ngy == 2

    flat, solid = q.reshape(nf, nx * ny, nz), solid_mask.reshape(nx * ny, nz)
    send_a, send_b, send_c = pl.pallas_call(
        functools.partial(gather_kernel, dims),
        out_shape=[jax.ShapeDtypeStruct((n, ny, nz), BF) for n in (2 * nf + 1, 2 * nf + 1, 4 * nf + 2)],
        in_specs=[VM] * 2,
        out_specs=[VM] * 3,
        compiler_params=pltpu.CompilerParams(vmem_limit_bytes=2 << 20),
    )(flat, solid)

    if two:
        swap = [(0, 1), (1, 0)]
        c1 = lax.ppermute(send_c, "gy", swap)
    else:
        up = [(j, (j + 1) % ngy) for j in range(ngy)]
        down = [(b, a) for a, b in up]
        half = 2 * nf + 1
        c1 = jnp.concatenate([lax.ppermute(send_c[:half], "gy", down), lax.ppermute(send_c[half:], "gy", up)], 0)

    def both(pairs):
        return pairs + [(b, a) for a, b in pairs]

    inner = both([(k, k + 1) for k in range(0, ngx, 2)])
    a = lax.ppermute(send_a, "gx", inner)
    outer = [(k * ngx + i, k * ngx + i + 1) for k in range(2) for i in range(1, ngx - 1, 2)]
    b = lax.ppermute(send_b, ("comp", "gx"), both(outer + [(0, ngx), (ngx - 1, 2 * ngx - 1)]))

    shape = jax.ShapeDtypeStruct((nf, nx * ny, nz), F32)
    cells = nf * nx * ny * nz

    def section(second, *args):
        return pl.pallas_call(
            functools.partial(section_kernel, dims, second),
            out_shape=shape,
            in_specs=[SM, SM] + [VM] * (len(args) + 1),
            out_specs=VM,
            scratch_shapes=[pltpu.VMEM((nf, ny // 8, 8, nz), F32), pltpu.VMEM((2, 5, ny // 8, 8, nz), F32)],
            compiler_params=pltpu.CompilerParams(vmem_limit_bytes=3 << 20),
            cost_estimate=pl.CostEstimate(flops=20 * cells, bytes_accessed=8 * cells, transcendentals=cells // 4),
        )(diffusivity, advection, *args, solid)

    first = section(False, flat)
    map_line = iface_map.reshape(1, ny)
    extra = pl.pallas_call(
        functools.partial(relay_kernel, dims),
        out_shape=jax.ShapeDtypeStruct((nf, ny + 16, nz), BF),
        in_specs=[VM] * 3 + [HB],
        out_specs=VM,
        scratch_shapes=[pltpu.VMEM((16, nz), F32)],
        compiler_params=pltpu.CompilerParams(vmem_limit_bytes=1 << 20),
    )(map_line, a, b, first)
    if two:
        c2 = lax.ppermute(extra, "gy", swap)
        c2l, c2h, more = c2, c2, []
    else:
        c2l, c2h = lax.ppermute(extra, "gy", up), lax.ppermute(extra, "gy", down)
        more = [lax.all_gather(b[: 2 * nf : 2], "gy", axis=1, tiled=True),
                lax.all_gather(iface_map, "gy", axis=0, tiled=True).reshape(1, -1)]

    main = section(True, flat, first)
    mb = pltpu.VMEM
    return pl.pallas_call(
        functools.partial(border_kernel, dims, two),
        out_shape=jax.ShapeDtypeStruct((nf, nx, ny, nz), F32),
        in_specs=[SM, SM, VM] + [VM] * (9 + len(more)),
        out_specs=HB,
        scratch_shapes=[
            mb((nz, 2 * nz), BF), mb((4, nf, ny, nz), F32), mb((4, nf, nx, nz), F32), mb((2, nf, nx, nz), F32), mb((4, ny, nz), F32),
            mb((4, 8, nz), F32), mb((6, nf, ny, nz), F32), mb((6, nf, nx, nz), F32), mb((2, nf, ny, nz), F32),
            mb((2, nf, nx, nz), F32), mb((2, nf, nx, nz), F32), mb((4, nf, ny, nz), F32), mb((2, nf, nx, 8, nz), F32),
            mb((4 * (nf + 1) * ny, nz), BF), mb((4 * (nf + 1) * ny, 2 * nz), F32),
            pltpu.SemaphoreType.DMA((4, 8)),
        ],
        compiler_params=pltpu.CompilerParams(vmem_limit_bytes=10 << 20),
        cost_estimate=pl.CostEstimate(flops=10 * cells, bytes_accessed=8 * cells, transcendentals=cells // 4),
    )(diffusivity, advection, map_line, flat, first, main.reshape(nf, nx, ny, nz), solid,
      a, b, c1, c2l, c2h, *more)[None]


def solution(mesh):
    sizes = mesh.shape["gx"], mesh.shape["gy"]
    return jax.shard_map(
        functools.partial(body, sizes),
        mesh=mesh,
        in_specs=(P("comp", None, "gx", "gy", None), P(), P(), P("gx", "gy", None), P("gy")),
        out_specs=P("comp", None, "gx", "gy", None),
        check_vma=False,
    )
```

```python
import functools

import jax
import jax.numpy as jnp
from jax import lax
from jax.experimental import pallas as pl
from jax.experimental.pallas import tpu as pltpu
from jax.sharding import PartitionSpec as P

RATIO = 1.5
GAIN = 0.4
LOG2E = 1.4426950408889634
BF = jnp.bfloat16
F32 = jnp.float32


def gain(q):
    return jnp.exp2(GAIN * LOG2E * jnp.tanh(q) - 1.0)


def shift_matrix(nz):
    row = lax.broadcasted_iota(jnp.int32, (nz, 2 * nz), 0)
    col = lax.broadcasted_iota(jnp.int32, (nz, 2 * nz), 1)
    k = jnp.where(col < nz, col, col - nz)
    up = jnp.where(k + 1 == nz, 0, k + 1)
    down = jnp.where(k == 0, nz - 1, k - 1)
    one = lambda c: jnp.where(c, 1.0, 0.0)
    own = one(row == k)
    return jnp.where(col < nz, one(row == up) - own, own - one(row == down)).astype(BF)


def scalars(dif, adv, nf):
    comp = lax.axis_index("comp")
    sign = (2 * comp - 1).astype(F32)
    return [dif[comp, f] for f in range(nf)], [adv[comp, f] * sign for f in range(nf)], 2 - comp


def masks(solid):
    return jnp.where(solid, RATIO, 1.0), jnp.where(solid, 0.0, 0.5)


def gather_kernel(dims, q_ref, s_ref, a_ref, b_ref, c_ref):
    nf, nx, ny, nz = dims
    even = lax.axis_index("gx") % 2 == 0
    def layer(ref, f, k):
        at = pl.multiple_of(k * ny, ny)
        return (ref[pl.ds(at, ny)] if f is None else ref[f, pl.ds(at, ny)]).astype(F32).astype(BF)

    a0, b0 = jnp.where(even, nx - 2, 0), jnp.where(even, 0, nx - 2)
    a1, b1 = jnp.where(even, nx - 1, 0), jnp.where(even, 0, nx - 1)
    for f in range(nf):
        for k in range(2):
            a_ref[2 * f + k] = layer(q_ref, f, a0 + k)
            b_ref[2 * f + k] = layer(q_ref, f, b0 + k)
        for k, y in enumerate((0, 1, ny - 2, ny - 1)):
            c_ref[k * nf + k // 2 + f] = q_ref[f, pl.ds(y, nx, stride=ny)].astype(BF)
    a_ref[2 * nf] = layer(s_ref, None, a1)
    b_ref[2 * nf] = layer(s_ref, None, b1)
    for k, y in ((2 * nf, 0), (4 * nf + 1, ny - 1)):
        c_ref[k] = s_ref[pl.ds(y, nx, stride=ny)].astype(F32).astype(BF)


def relay_kernel(dims, imap, a_ref, b_ref, after_ref, o_ref, rows):
    nf, nx, ny, nz = dims
    rows[...] = jnp.zeros_like(rows)
    rows[6:7, :ny] = imap[...].astype(F32)
    for f in range(nf):
        o_ref[f, :ny] = b_ref[2 * f]
        for k, (src, n) in enumerate(((a_ref, 2 * f), (a_ref, 2 * f + 1), (b_ref, 2 * f + 1))):
            block = src[n].astype(F32)
            rows[2 * k : 2 * k + 1] = block[:1]
            rows[2 * k + 1 : 2 * k + 2] = block[ny - 1 :]
        o_ref[f, ny:] = rows[...].astype(BF)


def shift_pair(nz, down):
    row = lax.broadcasted_iota(jnp.int32, (2 * nz, 2 * nz), 0)
    col = lax.broadcasted_iota(jnp.int32, (2 * nz, 2 * nz), 1)
    second = col >= nz
    k = jnp.where(second, col - nz, col)
    if down:
        other = jnp.where(k == 0, nz - 1, k - 1)
    else:
        other = jnp.where(k == nz - 1, 0, k + 1)
    other = jnp.where(second, other + nz, other)
    one = lambda c: jnp.where(c, 1.0, 0.0)
    diff = one(row == other) - one(row == col)
    return (-diff if down else diff).astype(BF)


def section_kernel(dims, second, *refs):
    nf, nx, ny, nz = dims
    pairs = [(6, None), (4, 5), (0, 1), (2, 3)]
    parts = ny // 8

    def run(*accs):
        if second:
            dif, adv, base_ref, q_ref, s_ref, o_ref, fx, gs = refs
        else:
            dif, adv, q_ref, s_ref, o_ref, fx, gs = refs
        n = len(pairs)
        ups, downs = (accs[:n], accs[n : 2 * n]), (accs[2 * n : 3 * n], accs[3 * n :])
        d, c, level = scalars(dif, adv, nf)
        lo, hi = (1, nx - 2) if second else (0, nx - 1)
        closed = (0, ny - 2) if second else (ny - 1,)
        sub = lax.broadcasted_iota(jnp.int32, (8, nz), 0)
        fx[...] = jnp.zeros_like(fx)
        pltpu.matmul_push_rhs(shift_pair(nz, False), staging_register=0, mxu_index=0)
        pltpu.matmul_push_rhs(shift_pair(nz, True), staging_register=0, mxu_index=1)

        def at(x, k):
            return pl.ds(x * ny + k, 8, stride=parts)

        def layer(f, x):
            return [q_ref[f, at(x, k)] for k in range(parts)]

        def tall(v):
            return jnp.concatenate(v, 0).astype(BF)

        def push(x, bank, g, load=None):
            for p, (f0, f1) in enumerate(pairs):
                lhs = jnp.concatenate([tall(layer(f0, x)), tall(g if f1 is None else layer(f1, x))], 1)
                pltpu.matmul_acc_lhs(ups[bank][p], lhs, load_staged_rhs=load)
                pltpu.matmul_acc_lhs(downs[bank][p], lhs, load_staged_rhs=load)
                load = None

        def prepare(x, bank, g):
            ge = [gain(v) for v in layer(4, jnp.minimum(x + 1, hi))]
            for k in range(parts):
                gs[bank, 0, k] = g[k] + ge[k]
                face = g[k] + (g[k + 1] if k + 1 < parts else pltpu.roll(g[0], 7, 0))
                for y in closed:
                    if y % parts == k:
                        face = jnp.where(sub == y // parts, 0.0, face)
                gs[bank, 1, k] = face
                gs[bank, 2, k] = g[k] + g[k]
                m, a = masks(s_ref[at(jnp.minimum(x, hi), k)] >= level)
                gs[bank, 3, k] = m
                gs[bank, 4, k] = a
            return ge

        def compute(x, bank):
            xe, xw = jnp.minimum(x + 1, hi), jnp.maximum(x - 1, lo)
            for p, pair in enumerate(pairs):
                up, down = pltpu.matmul_pop(ups[bank][p]), pltpu.matmul_pop(downs[bank][p])
                piece = lambda v, k, h: v[8 * k : 8 * k + 8, h * nz : (h + 1) * nz]
                if pair[1] is None:
                    gz = [gs[bank, 2, k] + piece(up, k, 1) for k in range(parts)]
                    gzl = [gs[bank, 2, k] - piece(down, k, 1) for k in range(parts)]
                for h, f in enumerate(pair):
                    if f is None:
                        continue
                    q = layer(f, x)
                    fy = [gs[bank, 1, k] * ((q[k + 1] if k + 1 < parts else pltpu.roll(q[0], 7, 0)) - q[k])
                          for k in range(parts)]
                    for k in range(parts):
                        qe, qw = q_ref[f, at(xe, k)], q_ref[f, at(xw, k)]
                        flux = gs[bank, 0, k] * (qe - q[k])
                        total = flux - fx[f, k]
                        fx[f, k] = flux
                        total += fy[k] - (fy[k - 1] if k else pltpu.roll(fy[-1], 1, 0))
                        total += gz[k] * piece(up, k, h) - gzl[k] * piece(down, k, h)
                        new = q[k] + (d[f] * (gs[bank, 3, k] * total) - c[f] * (gs[bank, 4, k] * (qe - qw)))
                        if second:
                            new = 0.5 * (base_ref[f, at(x, k)] + new)
                        o_ref[f, at(x, k)] = new

        def step(i, g):
            x = 2 * i + lo
            push(x + 1, 1, g)
            g = prepare(x + 1, 1, g)
            compute(x, 0)
            push(jnp.minimum(x + 2, hi), 0, g)
            g = prepare(x + 2, 0, g)
            compute(x + 1, 1)
            return g

        g = [gain(v) for v in layer(4, lo)]
        push(lo, 0, g, 0)
        lax.fori_loop(0, (hi + 1 - lo) // 2, step, prepare(lo, 0, g))
        for acc in ups[0] + downs[0]:
            pltpu.matmul_pop(acc)

    accs = [pltpu.ACC(m)((ny, 2 * nz), F32) for m in (0, 1) for _ in range(2 * len(pairs))]
    pl.run_scoped(run, *accs)


def border_kernel(dims, two, *refs):
    nf, nx, ny, nz = dims
    if two:
        dif, adv, imap, q_ref, first_ref, main_ref, s_ref, a_ref, b_ref, c1_ref, c2l_ref, c2h_ref = refs[:12]
        rest = refs[12:]
    else:
        (dif, adv, imap, q_ref, first_ref, main_ref, s_ref, a_ref, b_ref, c1_ref, c2l_ref, c2h_ref,
         face_ref, map_ref) = refs[:14]
        rest = refs[14:]
    out_ref, sm, lay, pla, qp, ms, cor, fl, fp, cx, cy, ep, ol, strips, zout, sem = rest
    d, c, level = scalars(dif, adv, nf)
    comp = lax.axis_index("comp")
    stream, last = lax.axis_index("gx"), lax.axis_size("gx") - 1
    even = stream % 2 == 0
    parts = ny // 8
    sm[...] = shift_matrix(nz)

    mids = []
    for f in range(nf):
        mids.append(pltpu.make_async_copy(
            main_ref.at[f, pl.ds(2, nx - 4), pl.ds(8, ny - 16)],
            out_ref.at[f, pl.ds(2, nx - 4), pl.ds(8, ny - 16)], sem.at[0, f]))
        mids[-1].start()
    cuts = []
    for k, row in enumerate((0, ny - 8)):
        cuts.append(pltpu.make_async_copy(main_ref.at[:, :, pl.ds(row, 8)], strips.at[k], sem.at[1, k]))
        cuts[-1].start()

    FAR_LO, LO, HI, FAR_HI = range(4)
    inside = jnp.where(stream == last, 0.0, 1.0)
    for f in range(nf):
        av = [a_ref[2 * f].astype(F32), a_ref[2 * f + 1].astype(F32)]
        bv = [b_ref[2 * f].astype(F32), b_ref[2 * f + 1].astype(F32)]
        lay[FAR_LO, f] = jnp.where(even, bv[0], av[0])
        lay[LO, f] = jnp.where(even, bv[1], av[1])
        lay[HI, f] = jnp.where(even, av[0], bv[0]) * inside
        lay[FAR_HI, f] = jnp.where(even, av[1], bv[1]) * inside
        for n, k in enumerate((2 * nf + 1, 3 * nf + 1, 0, nf)):
            pla[n, f] = c1_ref[k + f].astype(F32)
        for n, y in enumerate((0, ny - 1)):
            qp[n, f] = q_ref[f, pl.ds(y, nx, stride=ny)]
        lo, hi = c2l_ref[f, pl.ds(ny, 16)].astype(F32), c2h_ref[f, pl.ds(ny, 16)].astype(F32)
        lo_b, hi_b = c2l_ref[f, pl.ds(ny - 16, 16)].astype(F32), c2h_ref[f, pl.ds(0, 16)].astype(F32)
        cor[0, f : f + 1] = jnp.where(even, lo[5:6], lo[3:4])
        cor[1, f : f + 1] = jnp.where(even, hi[4:5], hi[2:3])
        cor[2, f : f + 1] = jnp.where(even, lo[1:2], lo_b[15:16]) * inside
        cor[3, f : f + 1] = jnp.where(even, hi[0:1], hi_b[0:1]) * inside
    am, bm = a_ref[2 * nf].astype(F32), b_ref[2 * nf].astype(F32)
    ms[0] = jnp.where(even, bm, am)
    ms[1] = jnp.where(even, am, bm)
    ms[2] = c1_ref[4 * nf + 1].astype(F32)
    ms[3] = c1_ref[2 * nf].astype(F32)

    @pl.when(stream == 0)
    def _():
        start = lax.axis_index("gy") * ny
        if two:
            whole = 2 * ny
            mine = jnp.broadcast_to(imap[...].astype(F32), (1, ny))
            other = c2l_ref[0, pl.ds(ny, 16)].astype(F32)[6:7, :ny]
            mapping = jnp.concatenate([mine, other], axis=1)
            order = start
        else:
            whole = face_ref.shape[1]
            mapping = map_ref[...].astype(F32)
            order = 0
        rows = ny + 8
        r = lax.broadcasted_iota(jnp.int32, (rows, whole), 0)
        want = jnp.where(r < ny, r, jnp.where(r == ny, whole - 1, ny)) + start
        want = jnp.where(want >= whole, want - whole, want).astype(F32)
        t = lax.broadcasted_iota(jnp.int32, (rows, whole), 1) + order
        t = jnp.where(t >= whole, t - whole, t).astype(F32)
        u = lax.broadcasted_iota(jnp.int32, (whole, whole), 0) + order
        u = jnp.where(u >= whole, u - whole, u).astype(F32)
        one = lambda x: jnp.where(x, 1.0, 0.0)
        pick = one(t == want).astype(BF)
        targets = one(jnp.broadcast_to(mapping, (whole, whole)) == u).astype(BF)
        inlet = lax.dot_general(pick, targets, (((1,), (1,)), ((), ())), preferred_element_type=F32)
        feed = one(jnp.broadcast_to(mapping, (rows, whole)) == want)
        choose = jnp.where(comp == 1, inlet, feed).astype(BF)
        for f in range(nf):
            if two:
                face = jnp.concatenate([b_ref[2 * f], c2l_ref[f, pl.ds(0, ny)]], axis=0)
            else:
                face = face_ref[f]
            ghost = jnp.dot(choose, face, preferred_element_type=F32)
            lay[LO, f] = ghost[:ny]
            cor[0, f : f + 1] = ghost[ny : ny + 1]
            cor[1, f : f + 1] = ghost[ny + 1 : ny + 2]

    sub = lax.broadcasted_iota(jnp.int32, (8, nz), 0)
    every = range(parts)

    def held(ref, *at):
        return lambda f, k: ref[(*at, f, pl.ds(k, 8, stride=parts))]

    def q_layer(x):
        return lambda f, k: q_ref[f, pl.ds(x * ny + k, 8, stride=parts)]

    def q_plane(y):
        return held(qp, 0 if y == 0 else 1)

    def s_layer(x):
        return lambda k: s_ref[pl.ds(x * ny + k, 8, stride=parts)] >= level

    def s_plane(y):
        return lambda k: s_ref[pl.ds(k * ny + y, 8, stride=parts * ny)] >= level

    def s_halo(n):
        edge = level.astype(F32)
        return lambda k: ms[n, pl.ds(k, 8, stride=parts)] >= edge

    def gains(src):
        return [gain(src(4, k)) for k in every]

    def line(src, r):
        return lambda f: src(f, r % parts)[r // parts : r // parts + 1]

    def corner(n):
        return lambda f: cor[n, f : f + 1]

    def got_line(ref, n, r):
        return lambda f: ref[n, f, r : r + 1]

    def put(ref, n, vals):
        for f in range(nf):
            for k in every:
                ref[n, f, pl.ds(k, 8, stride=parts)] = vals[f][k]

    def products(centers):
        gs = []
        for n, src in enumerate(centers):
            gs.append(gains(src))
            tall = [src(f, k) for f in range(nf) for k in every] + gs[-1]
            zout[n] = jnp.dot(jnp.concatenate(tall, 0).astype(BF), sm[...], preferred_element_type=F32)
        return gs

    def slab(n, g, center, before, after, low, high, solid, along_outer):
        def z(f, k, h):
            return zout[n, f * ny + 8 * k : f * ny + 8 * k + 8, h * nz : (h + 1) * nz]

        def ups(v, edge):
            return v[1:] + [jnp.where(sub == 7, edge, pltpu.roll(v[0], 7, 0))]

        def downs(v, edge):
            return [jnp.where(sub == 0, edge, pltpu.roll(v[-1], 1, 0))] + v[:-1]

        gb, ga = gains(before), gains(after)
        gu, gd = ups(g, gain(high(4))), downs(g, gain(low(4)))
        ga, gb, gu, gd = ([x + y for x, y in zip(g, v)] for v in (ga, gb, gu, gd))
        gz = [2.0 * g[k] + z(nf, k, 0) for k in every]
        gzl = [2.0 * g[k] - z(nf, k, 1) for k in every]
        ma = [masks(solid(k)) for k in every]
        res = []
        for f in range(nf):
            q = [center(f, k) for k in every]
            qu, qd = ups(q, high(f)), downs(q, low(f))
            vals = []
            for k in every:
                da, db, du, dd = after(f, k) - q[k], q[k] - before(f, k), qu[k] - q[k], q[k] - qd[k]
                total = ga[k] * da - gb[k] * db + (gu[k] * du - gd[k] * dd)
                total += gz[k] * z(f, k, 0) - gzl[k] * z(f, k, 1)
                grad = da + db if along_outer else du + dd
                vals.append(q[k] + (d[f] * (ma[k][0] * total) - c[f] * (ma[k][1] * grad)))
            res.append(vals)
        return res

    def passed(here, there, solid, along_x, ahead):
        g = [x + y for x, y in zip(gains(here), gains(there))]
        ma = [masks(solid(k)) for k in every]
        res = []
        for f in range(nf):
            vals = []
            for k in every:
                diff = there(f, k) - here(f, k)
                add = d[f] * (ma[k][0] * (g[k] * diff))
                if along_x:
                    half = c[f] * (ma[k][1] * diff)
                    add = add - half if ahead else add + half
                vals.append(add)
            res.append(vals)
        return res

    g = products([held(lay, LO), held(lay, HI), held(pla, LO), held(pla, HI)])
    ghost, ahead = held(lay, LO), jnp.where(stream == last, 0.0, 1.0)
    vals = slab(0, g[0], held(lay, LO), held(lay, FAR_LO), q_layer(0), corner(0), corner(1), s_halo(0), True)
    put(fl, 0, [[jnp.where(stream == 0, ghost(f, k), vals[f][k]) for k in every] for f in range(nf)])
    vals = slab(1, g[1], held(lay, HI), q_layer(nx - 1), held(lay, FAR_HI), corner(2), corner(3), s_halo(1), True)
    put(fl, 5, [[ahead * vals[f][k] for k in every] for f in range(nf)])
    put(fp, 0, slab(2, g[2], held(pla, LO), held(pla, FAR_LO), q_plane(0), corner(0), corner(2), s_halo(2), False))
    put(fp, 5, slab(3, g[3], held(pla, HI), q_plane(ny - 1), held(pla, FAR_HI), corner(1), corner(3), s_halo(3), False))

    put(cx, 0, passed(q_layer(0), held(lay, LO), s_layer(0), True, False))
    put(cx, 1, passed(q_layer(nx - 1), held(lay, HI), s_layer(nx - 1), True, True))
    put(cy, 0, passed(q_plane(0), held(pla, LO), s_plane(0), False, False))
    put(cy, 1, passed(q_plane(ny - 1), held(pla, HI), s_plane(ny - 1), False, True))
    for f in range(nf):
        for n, x in ((1, 0), (2, 1), (3, nx - 2), (4, nx - 1)):
            v = first_ref[f, x * ny : (x + 1) * ny]
            fl[n, f] = v + cx[n // 4, f] if n in (1, 4) else v
            fl[n, f, 0:1] += cy[0, f, x : x + 1]
            fl[n, f, ny - 1 : ny] += cy[1, f, x : x + 1]
        for n, y in ((1, 0), (2, 1), (3, ny - 2), (4, ny - 1)):
            v = first_ref[f, pl.ds(y, nx, stride=ny)]
            fp[n, f] = v + cy[n // 4, f] if n in (1, 4) else v
            fp[n, f, 0:1] += cx[0, f, y : y + 1]
            fp[n, f, nx - 1 : nx] += cx[1, f, y : y + 1]

    g = products([held(fl, 1), held(fl, 4), held(fp, 1), held(fp, 4)])

    def ended(src, vals):
        return [[0.5 * (src(f, k) + vals[f][k]) for k in every] for f in range(nf)]

    copies = []
    put(ep, 0, passed(held(fp, 2), held(fp, 1), s_plane(1), False, False))
    put(ep, 1, passed(held(fp, 3), held(fp, 4), s_plane(ny - 2), False, True))
    for n, (m, y, end, near) in enumerate(((1, 0, 0, 1), (4, ny - 1, 7, 6))):
        vals = slab(2 + n, g[2 + n], held(fp, m), held(fp, m - 1), held(fp, m + 1), got_line(fl, 0, y),
                    got_line(fl, 5, y), s_plane(y), False)
        put(cy, n, ended(q_plane(y), vals))
        cuts[n].wait()
        for f in range(nf):
            strips[n, f, :, end] = cy[n, f]
            strips[n, f, :, near] += 0.5 * ep[n, f]
        copies.append(pltpu.make_async_copy(
            strips.at[n, :, pl.ds(2, nx - 4)],
            out_ref.at[:, pl.ds(2, nx - 4), pl.ds(n * (ny - 8), 8)], sem.at[3, n]))
        copies[-1].start()
    put(cx, 0, passed(held(fl, 2), held(fl, 1), s_layer(1), True, False))
    put(cx, 1, passed(held(fl, 3), held(fl, 4), s_layer(nx - 2), True, True))
    for n, (m, x, near) in enumerate(((1, 0, 1), (4, nx - 1, nx - 2))):
        for f in range(nf):
            k = n + 1
            ol[k, f] = main_ref[f, near] + 0.5 * cx[n, f]
            ol[k, f, 0:1] = cy[0, f, near : near + 1]
            ol[k, f, 1:2] += 0.5 * ep[0, f, near : near + 1]
            ol[k, f, ny - 2 : ny - 1] += 0.5 * ep[1, f, near : near + 1]
            ol[k, f, ny - 1 : ny] = cy[1, f, near : near + 1]
        copies.append(pltpu.make_async_copy(ol.at[k], out_ref.at[:, near], sem.at[2, k]))
        copies[-1].start()
        vals = slab(n, g[n], held(fl, m), held(fl, m - 1), held(fl, m + 1), got_line(fp, 0, x), got_line(fp, 5, x),
                    s_layer(x), True)
        put(ol, 3 * n, ended(q_layer(x), vals))
        copies.append(pltpu.make_async_copy(ol.at[3 * n], out_ref.at[:, x], sem.at[2, 3 * n]))
        copies[-1].start()
    for copy in mids + copies:
        copy.wait()


VM = pl.BlockSpec(memory_space=pltpu.VMEM)
SM = pl.BlockSpec(memory_space=pltpu.SMEM)
HB = pl.BlockSpec(memory_space=pl.ANY)


def body(sizes, state, diffusivity, advection, solid_mask, iface_map):
    ngx, ngy = sizes
    q = state[0]
    nf, nx, ny, nz = q.shape
    dims = nf, nx, ny, nz
    two = ngy == 2

    flat, solid = q.reshape(nf, nx * ny, nz), solid_mask.reshape(nx * ny, nz)
    send_a, send_b, send_c = pl.pallas_call(
        functools.partial(gather_kernel, dims),
        out_shape=[jax.ShapeDtypeStruct((n, ny, nz), BF) for n in (2 * nf + 1, 2 * nf + 1, 4 * nf + 2)],
        in_specs=[VM] * 2,
        out_specs=[VM] * 3,
        compiler_params=pltpu.CompilerParams(vmem_limit_bytes=2 << 20),
    )(flat, solid)

    if two:
        swap = [(0, 1), (1, 0)]
        c1 = lax.ppermute(send_c, "gy", swap)
    else:
        up = [(j, (j + 1) % ngy) for j in range(ngy)]
        down = [(b, a) for a, b in up]
        half = 2 * nf + 1
        c1 = jnp.concatenate([lax.ppermute(send_c[:half], "gy", down), lax.ppermute(send_c[half:], "gy", up)], 0)

    def both(pairs):
        return pairs + [(b, a) for a, b in pairs]

    inner = both([(k, k + 1) for k in range(0, ngx, 2)])
    a = lax.ppermute(send_a, "gx", inner)
    outer = [(k * ngx + i, k * ngx + i + 1) for k in range(2) for i in range(1, ngx - 1, 2)]
    b = lax.ppermute(send_b, ("comp", "gx"), both(outer + [(0, ngx), (ngx - 1, 2 * ngx - 1)]))

    shape = jax.ShapeDtypeStruct((nf, nx * ny, nz), F32)
    cells = nf * nx * ny * nz

    def section(second, *args):
        return pl.pallas_call(
            functools.partial(section_kernel, dims, second),
            out_shape=shape,
            in_specs=[SM, SM] + [VM] * (len(args) + 1),
            out_specs=VM,
            scratch_shapes=[pltpu.VMEM((nf, ny // 8, 8, nz), F32), pltpu.VMEM((2, 5, ny // 8, 8, nz), F32)],
            compiler_params=pltpu.CompilerParams(vmem_limit_bytes=3 << 20),
            cost_estimate=pl.CostEstimate(flops=20 * cells, bytes_accessed=8 * cells, transcendentals=cells // 4),
        )(diffusivity, advection, *args, solid)

    first = section(False, flat)
    map_line = iface_map.reshape(1, ny)
    extra = pl.pallas_call(
        functools.partial(relay_kernel, dims),
        out_shape=jax.ShapeDtypeStruct((nf, ny + 16, nz), BF),
        in_specs=[VM] * 3 + [HB],
        out_specs=VM,
        scratch_shapes=[pltpu.VMEM((16, nz), F32)],
        compiler_params=pltpu.CompilerParams(vmem_limit_bytes=1 << 20),
    )(map_line, a, b, first)
    if two:
        c2 = lax.ppermute(extra, "gy", swap)
        c2l, c2h, more = c2, c2, []
    else:
        c2l, c2h = lax.ppermute(extra, "gy", up), lax.ppermute(extra, "gy", down)
        more = [lax.all_gather(b[: 2 * nf : 2], "gy", axis=1, tiled=True),
                lax.all_gather(iface_map, "gy", axis=0, tiled=True).reshape(1, -1)]

    main = section(True, flat, first)
    mb = pltpu.VMEM
    return pl.pallas_call(
        functools.partial(border_kernel, dims, two),
        out_shape=jax.ShapeDtypeStruct((nf, nx, ny, nz), F32),
        in_specs=[SM, SM, VM] + [VM] * (9 + len(more)),
        out_specs=HB,
        scratch_shapes=[
            mb((nz, 2 * nz), BF), mb((4, nf, ny, nz), F32), mb((4, nf, nx, nz), F32), mb((2, nf, nx, nz), F32), mb((4, ny, nz), F32),
            mb((4, 8, nz), F32), mb((6, nf, ny, nz), F32), mb((6, nf, nx, nz), F32), mb((2, nf, ny, nz), F32),
            mb((2, nf, nx, nz), F32), mb((2, nf, nx, nz), F32), mb((4, nf, ny, nz), F32), mb((2, nf, nx, 8, nz), F32),
            mb((4, (nf + 1) * ny, 2 * nz), F32),
            pltpu.SemaphoreType.DMA((4, 8)),
        ],
        compiler_params=pltpu.CompilerParams(vmem_limit_bytes=10 << 20),
        cost_estimate=pl.CostEstimate(flops=10 * cells, bytes_accessed=8 * cells, transcendentals=cells // 4),
    )(diffusivity, advection, map_line, flat, first, main.reshape(nf, nx, ny, nz), solid,
      a, b, c1, c2l, c2h, *more)[None]


def solution(mesh):
    sizes = mesh.shape["gx"], mesh.shape["gy"]
    return jax.shard_map(
        functools.partial(body, sizes),
        mesh=mesh,
        in_specs=(P("comp", None, "gx", "gy", None), P(), P(), P("gx", "gy", None), P("gy")),
        out_specs=P("comp", None, "gx", "gy", None),
        check_vma=False,
    )
```

```python
import functools

import jax
import jax.numpy as jnp
from jax import lax
from jax.experimental import pallas as pl
from jax.experimental.pallas import tpu as pltpu
from jax.sharding import PartitionSpec as P

RATIO = 1.5
GAIN = 0.4
LOG2E = 1.4426950408889634
BF = jnp.bfloat16
F32 = jnp.float32


def gain(q):
    return jnp.exp2(GAIN * LOG2E * jnp.tanh(q) - 1.0)


def shift_matrix(nz):
    row = lax.broadcasted_iota(jnp.int32, (nz, 2 * nz), 0)
    col = lax.broadcasted_iota(jnp.int32, (nz, 2 * nz), 1)
    k = jnp.where(col < nz, col, col - nz)
    up = jnp.where(k + 1 == nz, 0, k + 1)
    down = jnp.where(k == 0, nz - 1, k - 1)
    one = lambda c: jnp.where(c, 1.0, 0.0)
    own = one(row == k)
    return jnp.where(col < nz, one(row == up) - own, own - one(row == down)).astype(BF)


def scalars(dif, adv, nf):
    comp = lax.axis_index("comp")
    sign = (2 * comp - 1).astype(F32)
    return [dif[comp, f] for f in range(nf)], [adv[comp, f] * sign for f in range(nf)], 2 - comp


def masks(solid):
    return jnp.where(solid, RATIO, 1.0), jnp.where(solid, 0.0, 0.5)


def gather_kernel(dims, q_ref, s_ref, a_ref, b_ref, c_ref):
    nf, nx, ny, nz = dims
    even = lax.axis_index("gx") % 2 == 0
    def layer(ref, f, k):
        at = pl.multiple_of(k * ny, ny)
        return (ref[pl.ds(at, ny)] if f is None else ref[f, pl.ds(at, ny)]).astype(F32).astype(BF)

    a0, b0 = jnp.where(even, nx - 2, 0), jnp.where(even, 0, nx - 2)
    a1, b1 = jnp.where(even, nx - 1, 0), jnp.where(even, 0, nx - 1)
    for f in range(nf):
        for k in range(2):
            a_ref[2 * f + k] = layer(q_ref, f, a0 + k)
            b_ref[2 * f + k] = layer(q_ref, f, b0 + k)
        for k, y in enumerate((0, 1, ny - 2, ny - 1)):
            c_ref[k * nf + k // 2 + f] = q_ref[f, pl.ds(y, nx, stride=ny)].astype(BF)
    a_ref[2 * nf] = layer(s_ref, None, a1)
    b_ref[2 * nf] = layer(s_ref, None, b1)
    for k, y in ((2 * nf, 0), (4 * nf + 1, ny - 1)):
        c_ref[k] = s_ref[pl.ds(y, nx, stride=ny)].astype(F32).astype(BF)


def relay_kernel(dims, imap, a_ref, b_ref, after_ref, o_ref, rows):
    nf, nx, ny, nz = dims
    rows[...] = jnp.zeros_like(rows)
    rows[6:7, :ny] = imap[...].astype(F32)
    for f in range(nf):
        o_ref[f, :ny] = b_ref[2 * f]
        for k, (src, n) in enumerate(((a_ref, 2 * f), (a_ref, 2 * f + 1), (b_ref, 2 * f + 1))):
            block = src[n].astype(F32)
            rows[2 * k : 2 * k + 1] = block[:1]
            rows[2 * k + 1 : 2 * k + 2] = block[ny - 1 :]
        o_ref[f, ny:] = rows[...].astype(BF)


def shift_pair(nz, down):
    row = lax.broadcasted_iota(jnp.int32, (2 * nz, 2 * nz), 0)
    col = lax.broadcasted_iota(jnp.int32, (2 * nz, 2 * nz), 1)
    second = col >= nz
    k = jnp.where(second, col - nz, col)
    if down:
        other = jnp.where(k == 0, nz - 1, k - 1)
    else:
        other = jnp.where(k == nz - 1, 0, k + 1)
    other = jnp.where(second, other + nz, other)
    one = lambda c: jnp.where(c, 1.0, 0.0)
    diff = one(row == other) - one(row == col)
    return (-diff if down else diff).astype(BF)


def section_kernel(dims, second, *refs):
    nf, nx, ny, nz = dims
    pairs = [(6, None), (4, 5), (0, 1), (2, 3)]
    parts = ny // 8

    def run(*accs):
        if second:
            dif, adv, base_ref, q_ref, s_ref, o_ref, fx, gs = refs
        else:
            dif, adv, q_ref, s_ref, o_ref, fx, gs = refs
        n = len(pairs)
        ups, downs = (accs[:n], accs[n : 2 * n]), (accs[2 * n : 3 * n], accs[3 * n :])
        d, c, level = scalars(dif, adv, nf)
        lo, hi = (1, nx - 2) if second else (0, nx - 1)
        deep = next(n for n in (8, 6, 4, 2) if (hi + 1 - lo) % n == 0)
        closed = (0, ny - 2) if second else (ny - 1,)
        sub = lax.broadcasted_iota(jnp.int32, (8, nz), 0)
        fx[...] = jnp.zeros_like(fx)
        pltpu.matmul_push_rhs(shift_pair(nz, False), staging_register=0, mxu_index=0)
        pltpu.matmul_push_rhs(shift_pair(nz, True), staging_register=0, mxu_index=1)

        def at(x, k):
            return pl.ds(x * ny + k, 8, stride=parts)

        def layer(f, x):
            return [q_ref[f, at(x, k)] for k in range(parts)]

        def tall(v):
            return jnp.concatenate(v, 0).astype(BF)

        def push(x, bank, g, load=None):
            for p, (f0, f1) in enumerate(pairs):
                lhs = jnp.concatenate([tall(layer(f0, x)), tall(g if f1 is None else layer(f1, x))], 1)
                pltpu.matmul_acc_lhs(ups[bank][p], lhs, load_staged_rhs=load)
                pltpu.matmul_acc_lhs(downs[bank][p], lhs, load_staged_rhs=load)
                load = None

        def prepare(x, bank, g):
            ge = [gain(v) for v in layer(4, jnp.minimum(x + 1, hi))]
            for k in range(parts):
                gs[bank, 0, k] = g[k] + ge[k]
                face = g[k] + (g[k + 1] if k + 1 < parts else pltpu.roll(g[0], 7, 0))
                for y in closed:
                    if y % parts == k:
                        face = jnp.where(sub == y // parts, 0.0, face)
                gs[bank, 1, k] = face
                gs[bank, 2, k] = g[k] + g[k]
                m, a = masks(s_ref[at(jnp.minimum(x, hi), k)] >= level)
                gs[bank, 3, k] = m
                gs[bank, 4, k] = a
            return ge

        def compute(x, bank):
            xe, xw = jnp.minimum(x + 1, hi), jnp.maximum(x - 1, lo)
            for p, pair in enumerate(pairs):
                up, down = pltpu.matmul_pop(ups[bank][p]), pltpu.matmul_pop(downs[bank][p])
                piece = lambda v, k, h: v[8 * k : 8 * k + 8, h * nz : (h + 1) * nz]
                if pair[1] is None:
                    gz = [gs[bank, 2, k] + piece(up, k, 1) for k in range(parts)]
                    gzl = [gs[bank, 2, k] - piece(down, k, 1) for k in range(parts)]
                for h, f in enumerate(pair):
                    if f is None:
                        continue
                    q = layer(f, x)
                    fy = [gs[bank, 1, k] * ((q[k + 1] if k + 1 < parts else pltpu.roll(q[0], 7, 0)) - q[k])
                          for k in range(parts)]
                    for k in range(parts):
                        qe, qw = q_ref[f, at(xe, k)], q_ref[f, at(xw, k)]
                        flux = gs[bank, 0, k] * (qe - q[k])
                        total = flux - fx[f, k]
                        fx[f, k] = flux
                        total += fy[k] - (fy[k - 1] if k else pltpu.roll(fy[-1], 1, 0))
                        total += gz[k] * piece(up, k, h) - gzl[k] * piece(down, k, h)
                        new = q[k] + (d[f] * (gs[bank, 3, k] * total) - c[f] * (gs[bank, 4, k] * (qe - qw)))
                        if second:
                            new = 0.5 * (base_ref[f, at(x, k)] + new)
                        o_ref[f, at(x, k)] = new

        def step(i, g):
            for j in range(0, deep, 2):
                x = deep * i + lo + j
                push(x + 1, 1, g)
                g = prepare(x + 1, 1, g)
                compute(x, 0)
                push(jnp.minimum(x + 2, hi), 0, g)
                g = prepare(x + 2, 0, g)
                compute(x + 1, 1)
            return g

        g = [gain(v) for v in layer(4, lo)]
        push(lo, 0, g, 0)
        lax.fori_loop(0, (hi + 1 - lo) // deep, step, prepare(lo, 0, g))
        for acc in ups[0] + downs[0]:
            pltpu.matmul_pop(acc)

    accs = [pltpu.ACC(m)((ny, 2 * nz), F32) for m in (0, 1) for _ in range(2 * len(pairs))]
    pl.run_scoped(run, *accs)


def border_kernel(dims, two, *refs):
    nf, nx, ny, nz = dims
    if two:
        dif, adv, imap, q_ref, first_ref, main_ref, s_ref, a_ref, b_ref, c1_ref, c2l_ref, c2h_ref = refs[:12]
        rest = refs[12:]
    else:
        (dif, adv, imap, q_ref, first_ref, main_ref, s_ref, a_ref, b_ref, c1_ref, c2l_ref, c2h_ref,
         face_ref, map_ref) = refs[:14]
        rest = refs[14:]
    out_ref, sm, lay, pla, qp, ms, cor, fl, fp, cx, cy, ep, ol, strips, zout, sem = rest
    d, c, level = scalars(dif, adv, nf)
    comp = lax.axis_index("comp")
    stream, last = lax.axis_index("gx"), lax.axis_size("gx") - 1
    even = stream % 2 == 0
    parts = ny // 8
    sm[...] = shift_matrix(nz)

    mids = []
    for f in range(nf):
        mids.append(pltpu.make_async_copy(
            main_ref.at[f, pl.ds(2, nx - 4), pl.ds(8, ny - 16)],
            out_ref.at[f, pl.ds(2, nx - 4), pl.ds(8, ny - 16)], sem.at[0, f]))
        mids[-1].start()
    cuts = []
    for k, row in enumerate((0, ny - 8)):
        cuts.append(pltpu.make_async_copy(main_ref.at[:, :, pl.ds(row, 8)], strips.at[k], sem.at[1, k]))
        cuts[-1].start()

    FAR_LO, LO, HI, FAR_HI = range(4)
    inside = jnp.where(stream == last, 0.0, 1.0)
    for f in range(nf):
        av = [a_ref[2 * f].astype(F32), a_ref[2 * f + 1].astype(F32)]
        bv = [b_ref[2 * f].astype(F32), b_ref[2 * f + 1].astype(F32)]
        lay[FAR_LO, f] = jnp.where(even, bv[0], av[0])
        lay[LO, f] = jnp.where(even, bv[1], av[1])
        lay[HI, f] = jnp.where(even, av[0], bv[0]) * inside
        lay[FAR_HI, f] = jnp.where(even, av[1], bv[1]) * inside
        for n, k in enumerate((2 * nf + 1, 3 * nf + 1, 0, nf)):
            pla[n, f] = c1_ref[k + f].astype(F32)
        for n, y in enumerate((0, ny - 1)):
            qp[n, f] = q_ref[f, pl.ds(y, nx, stride=ny)]
        lo, hi = c2l_ref[f, pl.ds(ny, 16)].astype(F32), c2h_ref[f, pl.ds(ny, 16)].astype(F32)
        lo_b, hi_b = c2l_ref[f, pl.ds(ny - 16, 16)].astype(F32), c2h_ref[f, pl.ds(0, 16)].astype(F32)
        cor[0, f : f + 1] = jnp.where(even, lo[5:6], lo[3:4])
        cor[1, f : f + 1] = jnp.where(even, hi[4:5], hi[2:3])
        cor[2, f : f + 1] = jnp.where(even, lo[1:2], lo_b[15:16]) * inside
        cor[3, f : f + 1] = jnp.where(even, hi[0:1], hi_b[0:1]) * inside
    am, bm = a_ref[2 * nf].astype(F32), b_ref[2 * nf].astype(F32)
    ms[0] = jnp.where(even, bm, am)
    ms[1] = jnp.where(even, am, bm)
    ms[2] = c1_ref[4 * nf + 1].astype(F32)
    ms[3] = c1_ref[2 * nf].astype(F32)

    @pl.when(stream == 0)
    def _():
        start = lax.axis_index("gy") * ny
        if two:
            whole = 2 * ny
            mine = jnp.broadcast_to(imap[...].astype(F32), (1, ny))
            other = c2l_ref[0, pl.ds(ny, 16)].astype(F32)[6:7, :ny]
            mapping = jnp.concatenate([mine, other], axis=1)
            order = start
        else:
            whole = face_ref.shape[1]
            mapping = map_ref[...].astype(F32)
            order = 0
        rows = ny + 8
        r = lax.broadcasted_iota(jnp.int32, (rows, whole), 0)
        want = jnp.where(r < ny, r, jnp.where(r == ny, whole - 1, ny)) + start
        want = jnp.where(want >= whole, want - whole, want).astype(F32)
        t = lax.broadcasted_iota(jnp.int32, (rows, whole), 1) + order
        t = jnp.where(t >= whole, t - whole, t).astype(F32)
        u = lax.broadcasted_iota(jnp.int32, (whole, whole), 0) + order
        u = jnp.where(u >= whole, u - whole, u).astype(F32)
        one = lambda x: jnp.where(x, 1.0, 0.0)
        pick = one(t == want).astype(BF)
        targets = one(jnp.broadcast_to(mapping, (whole, whole)) == u).astype(BF)
        inlet = lax.dot_general(pick, targets, (((1,), (1,)), ((), ())), preferred_element_type=F32)
        feed = one(jnp.broadcast_to(mapping, (rows, whole)) == want)
        choose = jnp.where(comp == 1, inlet, feed).astype(BF)
        for f in range(nf):
            if two:
                face = jnp.concatenate([b_ref[2 * f], c2l_ref[f, pl.ds(0, ny)]], axis=0)
            else:
                face = face_ref[f]
            ghost = jnp.dot(choose, face, preferred_element_type=F32)
            lay[LO, f] = ghost[:ny]
            cor[0, f : f + 1] = ghost[ny : ny + 1]
            cor[1, f : f + 1] = ghost[ny + 1 : ny + 2]

    sub = lax.broadcasted_iota(jnp.int32, (8, nz), 0)
    every = range(parts)

    def held(ref, *at):
        return lambda f, k: ref[(*at, f, pl.ds(k, 8, stride=parts))]

    def q_layer(x):
        return lambda f, k: q_ref[f, pl.ds(x * ny + k, 8, stride=parts)]

    def q_plane(y):
        return held(qp, 0 if y == 0 else 1)

    def s_layer(x):
        return lambda k: s_ref[pl.ds(x * ny + k, 8, stride=parts)] >= level

    def s_plane(y):
        return lambda k: s_ref[pl.ds(k * ny + y, 8, stride=parts * ny)] >= level

    def s_halo(n):
        edge = level.astype(F32)
        return lambda k: ms[n, pl.ds(k, 8, stride=parts)] >= edge

    def gains(src):
        return [gain(src(4, k)) for k in every]

    def line(src, r):
        return lambda f: src(f, r % parts)[r // parts : r // parts + 1]

    def corner(n):
        return lambda f: cor[n, f : f + 1]

    def got_line(ref, n, r):
        return lambda f: ref[n, f, r : r + 1]

    def put(ref, n, vals):
        for f in range(nf):
            for k in every:
                ref[n, f, pl.ds(k, 8, stride=parts)] = vals[f][k]

    def products(centers):
        gs = []
        for n, src in enumerate(centers):
            gs.append(gains(src))
            tall = [src(f, k) for f in range(nf) for k in every] + gs[-1]
            zout[n] = jnp.dot(jnp.concatenate(tall, 0).astype(BF), sm[...], preferred_element_type=F32)
        return gs

    def slab(n, g, center, before, after, low, high, solid, along_outer):
        def z(f, k, h):
            return zout[n, f * ny + 8 * k : f * ny + 8 * k + 8, h * nz : (h + 1) * nz]

        def ups(v, edge):
            return v[1:] + [jnp.where(sub == 7, edge, pltpu.roll(v[0], 7, 0))]

        def downs(v, edge):
            return [jnp.where(sub == 0, edge, pltpu.roll(v[-1], 1, 0))] + v[:-1]

        gb, ga = gains(before), gains(after)
        gu, gd = ups(g, gain(high(4))), downs(g, gain(low(4)))
        ga, gb, gu, gd = ([x + y for x, y in zip(g, v)] for v in (ga, gb, gu, gd))
        gz = [2.0 * g[k] + z(nf, k, 0) for k in every]
        gzl = [2.0 * g[k] - z(nf, k, 1) for k in every]
        ma = [masks(solid(k)) for k in every]
        res = []
        for f in range(nf):
            q = [center(f, k) for k in every]
            qu, qd = ups(q, high(f)), downs(q, low(f))
            vals = []
            for k in every:
                da, db, du, dd = after(f, k) - q[k], q[k] - before(f, k), qu[k] - q[k], q[k] - qd[k]
                total = ga[k] * da - gb[k] * db + (gu[k] * du - gd[k] * dd)
                total += gz[k] * z(f, k, 0) - gzl[k] * z(f, k, 1)
                grad = da + db if along_outer else du + dd
                vals.append(q[k] + (d[f] * (ma[k][0] * total) - c[f] * (ma[k][1] * grad)))
            res.append(vals)
        return res

    def passed(here, there, solid, along_x, ahead):
        g = [x + y for x, y in zip(gains(here), gains(there))]
        ma = [masks(solid(k)) for k in every]
        res = []
        for f in range(nf):
            vals = []
            for k in every:
                diff = there(f, k) - here(f, k)
                add = d[f] * (ma[k][0] * (g[k] * diff))
                if along_x:
                    half = c[f] * (ma[k][1] * diff)
                    add = add - half if ahead else add + half
                vals.append(add)
            res.append(vals)
        return res

    g = products([held(lay, LO), held(lay, HI), held(pla, LO), held(pla, HI)])
    ghost, ahead = held(lay, LO), jnp.where(stream == last, 0.0, 1.0)
    vals = slab(0, g[0], held(lay, LO), held(lay, FAR_LO), q_layer(0), corner(0), corner(1), s_halo(0), True)
    put(fl, 0, [[jnp.where(stream == 0, ghost(f, k), vals[f][k]) for k in every] for f in range(nf)])
    vals = slab(1, g[1], held(lay, HI), q_layer(nx - 1), held(lay, FAR_HI), corner(2), corner(3), s_halo(1), True)
    put(fl, 5, [[ahead * vals[f][k] for k in every] for f in range(nf)])
    put(fp, 0, slab(2, g[2], held(pla, LO), held(pla, FAR_LO), q_plane(0), corner(0), corner(2), s_halo(2), False))
    put(fp, 5, slab(3, g[3], held(pla, HI), q_plane(ny - 1), held(pla, FAR_HI), corner(1), corner(3), s_halo(3), False))

    put(cx, 0, passed(q_layer(0), held(lay, LO), s_layer(0), True, False))
    put(cx, 1, passed(q_layer(nx - 1), held(lay, HI), s_layer(nx - 1), True, True))
    put(cy, 0, passed(q_plane(0), held(pla, LO), s_plane(0), False, False))
    put(cy, 1, passed(q_plane(ny - 1), held(pla, HI), s_plane(ny - 1), False, True))
    for f in range(nf):
        for n, x in ((1, 0), (2, 1), (3, nx - 2), (4, nx - 1)):
            v = first_ref[f, x * ny : (x + 1) * ny]
            fl[n, f] = v + cx[n // 4, f] if n in (1, 4) else v
            fl[n, f, 0:1] += cy[0, f, x : x + 1]
            fl[n, f, ny - 1 : ny] += cy[1, f, x : x + 1]
        for n, y in ((1, 0), (2, 1), (3, ny - 2), (4, ny - 1)):
            v = first_ref[f, pl.ds(y, nx, stride=ny)]
            fp[n, f] = v + cy[n // 4, f] if n in (1, 4) else v
            fp[n, f, 0:1] += cx[0, f, y : y + 1]
            fp[n, f, nx - 1 : nx] += cx[1, f, y : y + 1]

    g = products([held(fl, 1), held(fl, 4), held(fp, 1), held(fp, 4)])

    def ended(src, vals):
        return [[0.5 * (src(f, k) + vals[f][k]) for k in every] for f in range(nf)]

    copies = []
    put(ep, 0, passed(held(fp, 2), held(fp, 1), s_plane(1), False, False))
    put(ep, 1, passed(held(fp, 3), held(fp, 4), s_plane(ny - 2), False, True))
    for n, (m, y, end, near) in enumerate(((1, 0, 0, 1), (4, ny - 1, 7, 6))):
        vals = slab(2 + n, g[2 + n], held(fp, m), held(fp, m - 1), held(fp, m + 1), got_line(fl, 0, y),
                    got_line(fl, 5, y), s_plane(y), False)
        put(cy, n, ended(q_plane(y), vals))
        cuts[n].wait()
        for f in range(nf):
            strips[n, f, :, end] = cy[n, f]
            strips[n, f, :, near] += 0.5 * ep[n, f]
        copies.append(pltpu.make_async_copy(
            strips.at[n, :, pl.ds(2, nx - 4)],
            out_ref.at[:, pl.ds(2, nx - 4), pl.ds(n * (ny - 8), 8)], sem.at[3, n]))
        copies[-1].start()
    put(cx, 0, passed(held(fl, 2), held(fl, 1), s_layer(1), True, False))
    put(cx, 1, passed(held(fl, 3), held(fl, 4), s_layer(nx - 2), True, True))
    for n, (m, x, near) in enumerate(((1, 0, 1), (4, nx - 1, nx - 2))):
        for f in range(nf):
            k = n + 1
            ol[k, f] = main_ref[f, near] + 0.5 * cx[n, f]
            ol[k, f, 0:1] = cy[0, f, near : near + 1]
            ol[k, f, 1:2] += 0.5 * ep[0, f, near : near + 1]
            ol[k, f, ny - 2 : ny - 1] += 0.5 * ep[1, f, near : near + 1]
            ol[k, f, ny - 1 : ny] = cy[1, f, near : near + 1]
        copies.append(pltpu.make_async_copy(ol.at[k], out_ref.at[:, near], sem.at[2, k]))
        copies[-1].start()
        vals = slab(n, g[n], held(fl, m), held(fl, m - 1), held(fl, m + 1), got_line(fp, 0, x), got_line(fp, 5, x),
                    s_layer(x), True)
        put(ol, 3 * n, ended(q_layer(x), vals))
        copies.append(pltpu.make_async_copy(ol.at[3 * n], out_ref.at[:, x], sem.at[2, 3 * n]))
        copies[-1].start()
    for copy in mids + copies:
        copy.wait()


VM = pl.BlockSpec(memory_space=pltpu.VMEM)
SM = pl.BlockSpec(memory_space=pltpu.SMEM)
HB = pl.BlockSpec(memory_space=pl.ANY)


def body(sizes, state, diffusivity, advection, solid_mask, iface_map):
    ngx, ngy = sizes
    q = state[0]
    nf, nx, ny, nz = q.shape
    dims = nf, nx, ny, nz
    two = ngy == 2

    flat, solid = q.reshape(nf, nx * ny, nz), solid_mask.reshape(nx * ny, nz)
    send_a, send_b, send_c = pl.pallas_call(
        functools.partial(gather_kernel, dims),
        out_shape=[jax.ShapeDtypeStruct((n, ny, nz), BF) for n in (2 * nf + 1, 2 * nf + 1, 4 * nf + 2)],
        in_specs=[VM] * 2,
        out_specs=[VM] * 3,
        compiler_params=pltpu.CompilerParams(vmem_limit_bytes=2 << 20),
    )(flat, solid)

    if two:
        swap = [(0, 1), (1, 0)]
        c1 = lax.ppermute(send_c, "gy", swap)
    else:
        up = [(j, (j + 1) % ngy) for j in range(ngy)]
        down = [(b, a) for a, b in up]
        half = 2 * nf + 1
        c1 = jnp.concatenate([lax.ppermute(send_c[:half], "gy", down), lax.ppermute(send_c[half:], "gy", up)], 0)

    def both(pairs):
        return pairs + [(b, a) for a, b in pairs]

    inner = both([(k, k + 1) for k in range(0, ngx, 2)])
    a = lax.ppermute(send_a, "gx", inner)
    outer = [(k * ngx + i, k * ngx + i + 1) for k in range(2) for i in range(1, ngx - 1, 2)]
    b = lax.ppermute(send_b, ("comp", "gx"), both(outer + [(0, ngx), (ngx - 1, 2 * ngx - 1)]))

    shape = jax.ShapeDtypeStruct((nf, nx * ny, nz), F32)
    cells = nf * nx * ny * nz

    def section(second, *args):
        return pl.pallas_call(
            functools.partial(section_kernel, dims, second),
            out_shape=shape,
            in_specs=[SM, SM] + [VM] * (len(args) + 1),
            out_specs=VM,
            scratch_shapes=[pltpu.VMEM((nf, ny // 8, 8, nz), F32), pltpu.VMEM((2, 5, ny // 8, 8, nz), F32)],
            compiler_params=pltpu.CompilerParams(vmem_limit_bytes=3 << 20),
            cost_estimate=pl.CostEstimate(flops=20 * cells, bytes_accessed=8 * cells, transcendentals=cells // 4),
        )(diffusivity, advection, *args, solid)

    first = section(False, flat)
    map_line = iface_map.reshape(1, ny)
    extra = pl.pallas_call(
        functools.partial(relay_kernel, dims),
        out_shape=jax.ShapeDtypeStruct((nf, ny + 16, nz), BF),
        in_specs=[VM] * 3 + [HB],
        out_specs=VM,
        scratch_shapes=[pltpu.VMEM((16, nz), F32)],
        compiler_params=pltpu.CompilerParams(vmem_limit_bytes=1 << 20),
    )(map_line, a, b, first)
    if two:
        c2 = lax.ppermute(extra, "gy", swap)
        c2l, c2h, more = c2, c2, []
    else:
        c2l, c2h = lax.ppermute(extra, "gy", up), lax.ppermute(extra, "gy", down)
        more = [lax.all_gather(b[: 2 * nf : 2], "gy", axis=1, tiled=True),
                lax.all_gather(iface_map, "gy", axis=0, tiled=True).reshape(1, -1)]

    main = section(True, flat, first)
    mb = pltpu.VMEM
    return pl.pallas_call(
        functools.partial(border_kernel, dims, two),
        out_shape=jax.ShapeDtypeStruct((nf, nx, ny, nz), F32),
        in_specs=[SM, SM, VM] + [VM] * (9 + len(more)),
        out_specs=HB,
        scratch_shapes=[
            mb((nz, 2 * nz), BF), mb((4, nf, ny, nz), F32), mb((4, nf, nx, nz), F32), mb((2, nf, nx, nz), F32), mb((4, ny, nz), F32),
            mb((4, 8, nz), F32), mb((6, nf, ny, nz), F32), mb((6, nf, nx, nz), F32), mb((2, nf, ny, nz), F32),
            mb((2, nf, nx, nz), F32), mb((2, nf, nx, nz), F32), mb((4, nf, ny, nz), F32), mb((2, nf, nx, 8, nz), F32),
            mb((4, (nf + 1) * ny, 2 * nz), F32),
            pltpu.SemaphoreType.DMA((4, 8)),
        ],
        compiler_params=pltpu.CompilerParams(vmem_limit_bytes=10 << 20),
        cost_estimate=pl.CostEstimate(flops=10 * cells, bytes_accessed=8 * cells, transcendentals=cells // 4),
    )(diffusivity, advection, map_line, flat, first, main.reshape(nf, nx, ny, nz), solid,
      a, b, c1, c2l, c2h, *more)[None]


def solution(mesh):
    sizes = mesh.shape["gx"], mesh.shape["gy"]
    return jax.shard_map(
        functools.partial(body, sizes),
        mesh=mesh,
        in_specs=(P("comp", None, "gx", "gy", None), P(), P(), P("gx", "gy", None), P("gy")),
        out_specs=P("comp", None, "gx", "gy", None),
        check_vma=False,
    )
```

```python
import functools

import jax
import jax.numpy as jnp
from jax import lax
from jax.experimental import pallas as pl
from jax.experimental.pallas import tpu as pltpu
from jax.sharding import PartitionSpec as P

RATIO = 1.5
GAIN = 0.4
LOG2E = 1.4426950408889634
BF = jnp.bfloat16
F32 = jnp.float32


def gain(q):
    return jnp.exp2(GAIN * LOG2E * jnp.tanh(q) - 1.0)


def shift_matrix(nz):
    row = lax.broadcasted_iota(jnp.int32, (nz, 2 * nz), 0)
    col = lax.broadcasted_iota(jnp.int32, (nz, 2 * nz), 1)
    k = jnp.where(col < nz, col, col - nz)
    up = jnp.where(k + 1 == nz, 0, k + 1)
    down = jnp.where(k == 0, nz - 1, k - 1)
    one = lambda c: jnp.where(c, 1.0, 0.0)
    own = one(row == k)
    return jnp.where(col < nz, one(row == up) - own, own - one(row == down)).astype(BF)


def scalars(dif, adv, nf):
    comp = lax.axis_index("comp")
    sign = (2 * comp - 1).astype(F32)
    return [dif[comp, f] for f in range(nf)], [adv[comp, f] * sign for f in range(nf)], 2 - comp


def masks(solid):
    return jnp.where(solid, RATIO, 1.0), jnp.where(solid, 0.0, 0.5)


def gather_kernel(dims, q_ref, s_ref, a_ref, b_ref, c_ref):
    nf, nx, ny, nz = dims
    even = lax.axis_index("gx") % 2 == 0
    def layer(ref, f, k):
        at = pl.multiple_of(k * ny, ny)
        return (ref[pl.ds(at, ny)] if f is None else ref[f, pl.ds(at, ny)]).astype(F32).astype(BF)

    a0, b0 = jnp.where(even, nx - 2, 0), jnp.where(even, 0, nx - 2)
    a1, b1 = jnp.where(even, nx - 1, 0), jnp.where(even, 0, nx - 1)
    for f in range(nf):
        for k in range(2):
            a_ref[2 * f + k] = layer(q_ref, f, a0 + k)
            b_ref[2 * f + k] = layer(q_ref, f, b0 + k)
        for k, y in enumerate((0, 1, ny - 2, ny - 1)):
            c_ref[k * nf + k // 2 + f] = q_ref[f, pl.ds(y, nx, stride=ny)].astype(BF)
    a_ref[2 * nf] = layer(s_ref, None, a1)
    b_ref[2 * nf] = layer(s_ref, None, b1)
    for k, y in ((2 * nf, 0), (4 * nf + 1, ny - 1)):
        c_ref[k] = s_ref[pl.ds(y, nx, stride=ny)].astype(F32).astype(BF)


def relay_kernel(dims, imap, a_ref, b_ref, after_ref, o_ref, rows):
    nf, nx, ny, nz = dims
    rows[...] = jnp.zeros_like(rows)
    rows[6:7, :ny] = imap[...].astype(F32)
    for f in range(nf):
        o_ref[f, :ny] = b_ref[2 * f]
        for k, (src, n) in enumerate(((a_ref, 2 * f), (a_ref, 2 * f + 1), (b_ref, 2 * f + 1))):
            block = src[n].astype(F32)
            rows[2 * k : 2 * k + 1] = block[:1]
            rows[2 * k + 1 : 2 * k + 2] = block[ny - 1 :]
        o_ref[f, ny:] = rows[...].astype(BF)


def shift_pair(nz, down):
    row = lax.broadcasted_iota(jnp.int32, (2 * nz, 2 * nz), 0)
    col = lax.broadcasted_iota(jnp.int32, (2 * nz, 2 * nz), 1)
    second = col >= nz
    k = jnp.where(second, col - nz, col)
    if down:
        other = jnp.where(k == 0, nz - 1, k - 1)
    else:
        other = jnp.where(k == nz - 1, 0, k + 1)
    other = jnp.where(second, other + nz, other)
    one = lambda c: jnp.where(c, 1.0, 0.0)
    diff = one(row == other) - one(row == col)
    return (-diff if down else diff).astype(BF)


def section_kernel(dims, second, *refs):
    nf, nx, ny, nz = dims
    pairs = [(6, None), (4, 5), (0, 1), (2, 3)]
    parts = ny // 8

    def run(*accs):
        if second:
            dif, adv, base_ref, q_ref, s_ref, o_ref, fx, gs = refs
        else:
            dif, adv, q_ref, s_ref, o_ref, fx, gs = refs
        n = len(pairs)
        ups, downs = (accs[:n], accs[n : 2 * n]), (accs[2 * n : 3 * n], accs[3 * n :])
        d, c, level = scalars(dif, adv, nf)
        lo, hi = (1, nx - 2) if second else (0, nx - 1)
        deep = next(n for n in (16, 10, 2) if (hi + 1 - lo) % n == 0)
        closed = (0, ny - 2) if second else (ny - 1,)
        sub = lax.broadcasted_iota(jnp.int32, (8, nz), 0)
        fx[...] = jnp.zeros_like(fx)
        pltpu.matmul_push_rhs(shift_pair(nz, False), staging_register=0, mxu_index=0)
        pltpu.matmul_push_rhs(shift_pair(nz, True), staging_register=0, mxu_index=1)

        def at(x, k):
            return pl.ds(x * ny + k, 8, stride=parts)

        def layer(f, x):
            return [q_ref[f, at(x, k)] for k in range(parts)]

        def tall(v):
            return jnp.concatenate(v, 0).astype(BF)

        def push(x, bank, g, load=None):
            for p, (f0, f1) in enumerate(pairs):
                lhs = jnp.concatenate([tall(layer(f0, x)), tall(g if f1 is None else layer(f1, x))], 1)
                pltpu.matmul_acc_lhs(ups[bank][p], lhs, load_staged_rhs=load)
                pltpu.matmul_acc_lhs(downs[bank][p], lhs, load_staged_rhs=load)
                load = None

        def prepare(x, bank, g):
            ge = [gain(v) for v in layer(4, jnp.minimum(x + 1, hi))]
            for k in range(parts):
                gs[bank, 0, k] = g[k] + ge[k]
                face = g[k] + (g[k + 1] if k + 1 < parts else pltpu.roll(g[0], 7, 0))
                for y in closed:
                    if y % parts == k:
                        face = jnp.where(sub == y // parts, 0.0, face)
                gs[bank, 1, k] = face
                gs[bank, 2, k] = g[k] + g[k]
                m, a = masks(s_ref[at(jnp.minimum(x, hi), k)] >= level)
                gs[bank, 3, k] = m
                gs[bank, 4, k] = a
            return ge

        def compute(x, bank):
            xe, xw = jnp.minimum(x + 1, hi), jnp.maximum(x - 1, lo)
            for p, pair in enumerate(pairs):
                up, down = pltpu.matmul_pop(ups[bank][p]), pltpu.matmul_pop(downs[bank][p])
                piece = lambda v, k, h: v[8 * k : 8 * k + 8, h * nz : (h + 1) * nz]
                if pair[1] is None:
                    gz = [gs[bank, 2, k] + piece(up, k, 1) for k in range(parts)]
                    gzl = [gs[bank, 2, k] - piece(down, k, 1) for k in range(parts)]
                for h, f in enumerate(pair):
                    if f is None:
                        continue
                    q = layer(f, x)
                    fy = [gs[bank, 1, k] * ((q[k + 1] if k + 1 < parts else pltpu.roll(q[0], 7, 0)) - q[k])
                          for k in range(parts)]
                    for k in range(parts):
                        qe, qw = q_ref[f, at(xe, k)], q_ref[f, at(xw, k)]
                        flux = gs[bank, 0, k] * (qe - q[k])
                        total = flux - fx[f, k]
                        fx[f, k] = flux
                        total += fy[k] - (fy[k - 1] if k else pltpu.roll(fy[-1], 1, 0))
                        total += gz[k] * piece(up, k, h) - gzl[k] * piece(down, k, h)
                        new = q[k] + (d[f] * (gs[bank, 3, k] * total) - c[f] * (gs[bank, 4, k] * (qe - qw)))
                        if second:
                            new = 0.5 * (base_ref[f, at(x, k)] + new)
                        o_ref[f, at(x, k)] = new

        def step(i, g):
            for j in range(0, deep, 2):
                x = deep * i + lo + j
                push(x + 1, 1, g)
                g = prepare(x + 1, 1, g)
                compute(x, 0)
                push(jnp.minimum(x + 2, hi), 0, g)
                g = prepare(x + 2, 0, g)
                compute(x + 1, 1)
            return g

        g = [gain(v) for v in layer(4, lo)]
        push(lo, 0, g, 0)
        lax.fori_loop(0, (hi + 1 - lo) // deep, step, prepare(lo, 0, g))
        for acc in ups[0] + downs[0]:
            pltpu.matmul_pop(acc)

    accs = [pltpu.ACC(m)((ny, 2 * nz), F32) for m in (0, 1) for _ in range(2 * len(pairs))]
    pl.run_scoped(run, *accs)


def border_kernel(dims, two, *refs):
    nf, nx, ny, nz = dims
    if two:
        dif, adv, imap, q_ref, first_ref, main_ref, s_ref, a_ref, b_ref, c1_ref, c2l_ref, c2h_ref = refs[:12]
        rest = refs[12:]
    else:
        (dif, adv, imap, q_ref, first_ref, main_ref, s_ref, a_ref, b_ref, c1_ref, c2l_ref, c2h_ref,
         face_ref, map_ref) = refs[:14]
        rest = refs[14:]
    out_ref, sm, lay, pla, qp, ms, cor, fl, fp, cx, cy, ep, ol, strips, zout, sem = rest
    d, c, level = scalars(dif, adv, nf)
    comp = lax.axis_index("comp")
    stream, last = lax.axis_index("gx"), lax.axis_size("gx") - 1
    even = stream % 2 == 0
    parts = ny // 8
    sm[...] = shift_matrix(nz)

    mids = []
    for f in range(nf):
        mids.append(pltpu.make_async_copy(
            main_ref.at[f, pl.ds(2, nx - 4), pl.ds(8, ny - 16)],
            out_ref.at[f, pl.ds(2, nx - 4), pl.ds(8, ny - 16)], sem.at[0, f]))
        mids[-1].start()
    cuts = []
    for k, row in enumerate((0, ny - 8)):
        cuts.append(pltpu.make_async_copy(main_ref.at[:, :, pl.ds(row, 8)], strips.at[k], sem.at[1, k]))
        cuts[-1].start()

    FAR_LO, LO, HI, FAR_HI = range(4)
    inside = jnp.where(stream == last, 0.0, 1.0)
    for f in range(nf):
        av = [a_ref[2 * f].astype(F32), a_ref[2 * f + 1].astype(F32)]
        bv = [b_ref[2 * f].astype(F32), b_ref[2 * f + 1].astype(F32)]
        lay[FAR_LO, f] = jnp.where(even, bv[0], av[0])
        lay[LO, f] = jnp.where(even, bv[1], av[1])
        lay[HI, f] = jnp.where(even, av[0], bv[0]) * inside
        lay[FAR_HI, f] = jnp.where(even, av[1], bv[1]) * inside
        for n, k in enumerate((2 * nf + 1, 3 * nf + 1, 0, nf)):
            pla[n, f] = c1_ref[k + f].astype(F32)
        for n, y in enumerate((0, ny - 1)):
            qp[n, f] = q_ref[f, pl.ds(y, nx, stride=ny)]
        lo, hi = c2l_ref[f, pl.ds(ny, 16)].astype(F32), c2h_ref[f, pl.ds(ny, 16)].astype(F32)
        lo_b, hi_b = c2l_ref[f, pl.ds(ny - 16, 16)].astype(F32), c2h_ref[f, pl.ds(0, 16)].astype(F32)
        cor[0, f : f + 1] = jnp.where(even, lo[5:6], lo[3:4])
        cor[1, f : f + 1] = jnp.where(even, hi[4:5], hi[2:3])
        cor[2, f : f + 1] = jnp.where(even, lo[1:2], lo_b[15:16]) * inside
        cor[3, f : f + 1] = jnp.where(even, hi[0:1], hi_b[0:1]) * inside
    am, bm = a_ref[2 * nf].astype(F32), b_ref[2 * nf].astype(F32)
    ms[0] = jnp.where(even, bm, am)
    ms[1] = jnp.where(even, am, bm)
    ms[2] = c1_ref[4 * nf + 1].astype(F32)
    ms[3] = c1_ref[2 * nf].astype(F32)

    @pl.when(stream == 0)
    def _():
        start = lax.axis_index("gy") * ny
        if two:
            whole = 2 * ny
            mine = jnp.broadcast_to(imap[...].astype(F32), (1, ny))
            other = c2l_ref[0, pl.ds(ny, 16)].astype(F32)[6:7, :ny]
            mapping = jnp.concatenate([mine, other], axis=1)
            order = start
        else:
            whole = face_ref.shape[1]
            mapping = map_ref[...].astype(F32)
            order = 0
        rows = ny + 8
        r = lax.broadcasted_iota(jnp.int32, (rows, whole), 0)
        want = jnp.where(r < ny, r, jnp.where(r == ny, whole - 1, ny)) + start
        want = jnp.where(want >= whole, want - whole, want).astype(F32)
        t = lax.broadcasted_iota(jnp.int32, (rows, whole), 1) + order
        t = jnp.where(t >= whole, t - whole, t).astype(F32)
        u = lax.broadcasted_iota(jnp.int32, (whole, whole), 0) + order
        u = jnp.where(u >= whole, u - whole, u).astype(F32)
        one = lambda x: jnp.where(x, 1.0, 0.0)
        pick = one(t == want).astype(BF)
        targets = one(jnp.broadcast_to(mapping, (whole, whole)) == u).astype(BF)
        inlet = lax.dot_general(pick, targets, (((1,), (1,)), ((), ())), preferred_element_type=F32)
        feed = one(jnp.broadcast_to(mapping, (rows, whole)) == want)
        choose = jnp.where(comp == 1, inlet, feed).astype(BF)
        for f in range(nf):
            if two:
                face = jnp.concatenate([b_ref[2 * f], c2l_ref[f, pl.ds(0, ny)]], axis=0)
            else:
                face = face_ref[f]
            ghost = jnp.dot(choose, face, preferred_element_type=F32)
            lay[LO, f] = ghost[:ny]
            cor[0, f : f + 1] = ghost[ny : ny + 1]
            cor[1, f : f + 1] = ghost[ny + 1 : ny + 2]

    sub = lax.broadcasted_iota(jnp.int32, (8, nz), 0)
    every = range(parts)

    def held(ref, *at):
        return lambda f, k: ref[(*at, f, pl.ds(k, 8, stride=parts))]

    def q_layer(x):
        return lambda f, k: q_ref[f, pl.ds(x * ny + k, 8, stride=parts)]

    def q_plane(y):
        return held(qp, 0 if y == 0 else 1)

    def s_layer(x):
        return lambda k: s_ref[pl.ds(x * ny + k, 8, stride=parts)] >= level

    def s_plane(y):
        return lambda k: s_ref[pl.ds(k * ny + y, 8, stride=parts * ny)] >= level

    def s_halo(n):
        edge = level.astype(F32)
        return lambda k: ms[n, pl.ds(k, 8, stride=parts)] >= edge

    def gains(src):
        return [gain(src(4, k)) for k in every]

    def line(src, r):
        return lambda f: src(f, r % parts)[r // parts : r // parts + 1]

    def corner(n):
        return lambda f: cor[n, f : f + 1]

    def got_line(ref, n, r):
        return lambda f: ref[n, f, r : r + 1]

    def put(ref, n, vals):
        for f in range(nf):
            for k in every:
                ref[n, f, pl.ds(k, 8, stride=parts)] = vals[f][k]

    def products(centers):
        gs = []
        for n, src in enumerate(centers):
            gs.append(gains(src))
            tall = [src(f, k) for f in range(nf) for k in every] + gs[-1]
            zout[n] = jnp.dot(jnp.concatenate(tall, 0).astype(BF), sm[...], preferred_element_type=F32)
        return gs

    def slab(n, g, center, before, after, low, high, solid, along_outer):
        def z(f, k, h):
            return zout[n, f * ny + 8 * k : f * ny + 8 * k + 8, h * nz : (h + 1) * nz]

        def ups(v, edge):
            return v[1:] + [jnp.where(sub == 7, edge, pltpu.roll(v[0], 7, 0))]

        def downs(v, edge):
            return [jnp.where(sub == 0, edge, pltpu.roll(v[-1], 1, 0))] + v[:-1]

        gb, ga = gains(before), gains(after)
        gu, gd = ups(g, gain(high(4))), downs(g, gain(low(4)))
        ga, gb, gu, gd = ([x + y for x, y in zip(g, v)] for v in (ga, gb, gu, gd))
        gz = [2.0 * g[k] + z(nf, k, 0) for k in every]
        gzl = [2.0 * g[k] - z(nf, k, 1) for k in every]
        ma = [masks(solid(k)) for k in every]
        res = []
        for f in range(nf):
            q = [center(f, k) for k in every]
            qu, qd = ups(q, high(f)), downs(q, low(f))
            vals = []
            for k in every:
                da, db, du, dd = after(f, k) - q[k], q[k] - before(f, k), qu[k] - q[k], q[k] - qd[k]
                total = ga[k] * da - gb[k] * db + (gu[k] * du - gd[k] * dd)
                total += gz[k] * z(f, k, 0) - gzl[k] * z(f, k, 1)
                grad = da + db if along_outer else du + dd
                vals.append(q[k] + (d[f] * (ma[k][0] * total) - c[f] * (ma[k][1] * grad)))
            res.append(vals)
        return res

    def passed(here, there, solid, along_x, ahead):
        g = [x + y for x, y in zip(gains(here), gains(there))]
        ma = [masks(solid(k)) for k in every]
        res = []
        for f in range(nf):
            vals = []
            for k in every:
                diff = there(f, k) - here(f, k)
                add = d[f] * (ma[k][0] * (g[k] * diff))
                if along_x:
                    half = c[f] * (ma[k][1] * diff)
                    add = add - half if ahead else add + half
                vals.append(add)
            res.append(vals)
        return res

    g = products([held(lay, LO), held(lay, HI), held(pla, LO), held(pla, HI)])
    ghost, ahead = held(lay, LO), jnp.where(stream == last, 0.0, 1.0)
    vals = slab(0, g[0], held(lay, LO), held(lay, FAR_LO), q_layer(0), corner(0), corner(1), s_halo(0), True)
    put(fl, 0, [[jnp.where(stream == 0, ghost(f, k), vals[f][k]) for k in every] for f in range(nf)])
    vals = slab(1, g[1], held(lay, HI), q_layer(nx - 1), held(lay, FAR_HI), corner(2), corner(3), s_halo(1), True)
    put(fl, 5, [[ahead * vals[f][k] for k in every] for f in range(nf)])
    put(fp, 0, slab(2, g[2], held(pla, LO), held(pla, FAR_LO), q_plane(0), corner(0), corner(2), s_halo(2), False))
    put(fp, 5, slab(3, g[3], held(pla, HI), q_plane(ny - 1), held(pla, FAR_HI), corner(1), corner(3), s_halo(3), False))

    put(cx, 0, passed(q_layer(0), held(lay, LO), s_layer(0), True, False))
    put(cx, 1, passed(q_layer(nx - 1), held(lay, HI), s_layer(nx - 1), True, True))
    put(cy, 0, passed(q_plane(0), held(pla, LO), s_plane(0), False, False))
    put(cy, 1, passed(q_plane(ny - 1), held(pla, HI), s_plane(ny - 1), False, True))
    for f in range(nf):
        for n, x in ((1, 0), (2, 1), (3, nx - 2), (4, nx - 1)):
            v = first_ref[f, x * ny : (x + 1) * ny]
            fl[n, f] = v + cx[n // 4, f] if n in (1, 4) else v
            fl[n, f, 0:1] += cy[0, f, x : x + 1]
            fl[n, f, ny - 1 : ny] += cy[1, f, x : x + 1]
        for n, y in ((1, 0), (2, 1), (3, ny - 2), (4, ny - 1)):
            v = first_ref[f, pl.ds(y, nx, stride=ny)]
            fp[n, f] = v + cy[n // 4, f] if n in (1, 4) else v
            fp[n, f, 0:1] += cx[0, f, y : y + 1]
            fp[n, f, nx - 1 : nx] += cx[1, f, y : y + 1]

    g = products([held(fl, 1), held(fl, 4), held(fp, 1), held(fp, 4)])

    def ended(src, vals):
        return [[0.5 * (src(f, k) + vals[f][k]) for k in every] for f in range(nf)]

    copies = []
    put(ep, 0, passed(held(fp, 2), held(fp, 1), s_plane(1), False, False))
    put(ep, 1, passed(held(fp, 3), held(fp, 4), s_plane(ny - 2), False, True))
    for n, (m, y, end, near) in enumerate(((1, 0, 0, 1), (4, ny - 1, 7, 6))):
        vals = slab(2 + n, g[2 + n], held(fp, m), held(fp, m - 1), held(fp, m + 1), got_line(fl, 0, y),
                    got_line(fl, 5, y), s_plane(y), False)
        put(cy, n, ended(q_plane(y), vals))
        cuts[n].wait()
        for f in range(nf):
            strips[n, f, :, end] = cy[n, f]
            strips[n, f, :, near] += 0.5 * ep[n, f]
        copies.append(pltpu.make_async_copy(
            strips.at[n, :, pl.ds(2, nx - 4)],
            out_ref.at[:, pl.ds(2, nx - 4), pl.ds(n * (ny - 8), 8)], sem.at[3, n]))
        copies[-1].start()
    put(cx, 0, passed(held(fl, 2), held(fl, 1), s_layer(1), True, False))
    put(cx, 1, passed(held(fl, 3), held(fl, 4), s_layer(nx - 2), True, True))
    for n, (m, x, near) in enumerate(((1, 0, 1), (4, nx - 1, nx - 2))):
        for f in range(nf):
            k = n + 1
            ol[k, f] = main_ref[f, near] + 0.5 * cx[n, f]
            ol[k, f, 0:1] = cy[0, f, near : near + 1]
            ol[k, f, 1:2] += 0.5 * ep[0, f, near : near + 1]
            ol[k, f, ny - 2 : ny - 1] += 0.5 * ep[1, f, near : near + 1]
            ol[k, f, ny - 1 : ny] = cy[1, f, near : near + 1]
        copies.append(pltpu.make_async_copy(ol.at[k], out_ref.at[:, near], sem.at[2, k]))
        copies[-1].start()
        vals = slab(n, g[n], held(fl, m), held(fl, m - 1), held(fl, m + 1), got_line(fp, 0, x), got_line(fp, 5, x),
                    s_layer(x), True)
        put(ol, 3 * n, ended(q_layer(x), vals))
        copies.append(pltpu.make_async_copy(ol.at[3 * n], out_ref.at[:, x], sem.at[2, 3 * n]))
        copies[-1].start()
    for copy in mids + copies:
        copy.wait()


VM = pl.BlockSpec(memory_space=pltpu.VMEM)
SM = pl.BlockSpec(memory_space=pltpu.SMEM)
HB = pl.BlockSpec(memory_space=pl.ANY)


def body(sizes, state, diffusivity, advection, solid_mask, iface_map):
    ngx, ngy = sizes
    q = state[0]
    nf, nx, ny, nz = q.shape
    dims = nf, nx, ny, nz
    two = ngy == 2

    flat, solid = q.reshape(nf, nx * ny, nz), solid_mask.reshape(nx * ny, nz)
    send_a, send_b, send_c = pl.pallas_call(
        functools.partial(gather_kernel, dims),
        out_shape=[jax.ShapeDtypeStruct((n, ny, nz), BF) for n in (2 * nf + 1, 2 * nf + 1, 4 * nf + 2)],
        in_specs=[VM] * 2,
        out_specs=[VM] * 3,
        compiler_params=pltpu.CompilerParams(vmem_limit_bytes=2 << 20),
    )(flat, solid)

    if two:
        swap = [(0, 1), (1, 0)]
        c1 = lax.ppermute(send_c, "gy", swap)
    else:
        up = [(j, (j + 1) % ngy) for j in range(ngy)]
        down = [(b, a) for a, b in up]
        half = 2 * nf + 1
        c1 = jnp.concatenate([lax.ppermute(send_c[:half], "gy", down), lax.ppermute(send_c[half:], "gy", up)], 0)

    def both(pairs):
        return pairs + [(b, a) for a, b in pairs]

    inner = both([(k, k + 1) for k in range(0, ngx, 2)])
    a = lax.ppermute(send_a, "gx", inner)
    outer = [(k * ngx + i, k * ngx + i + 1) for k in range(2) for i in range(1, ngx - 1, 2)]
    b = lax.ppermute(send_b, ("comp", "gx"), both(outer + [(0, ngx), (ngx - 1, 2 * ngx - 1)]))

    shape = jax.ShapeDtypeStruct((nf, nx * ny, nz), F32)
    cells = nf * nx * ny * nz

    def section(second, *args):
        return pl.pallas_call(
            functools.partial(section_kernel, dims, second),
            out_shape=shape,
            in_specs=[SM, SM] + [VM] * (len(args) + 1),
            out_specs=VM,
            scratch_shapes=[pltpu.VMEM((nf, ny // 8, 8, nz), F32), pltpu.VMEM((2, 5, ny // 8, 8, nz), F32)],
            compiler_params=pltpu.CompilerParams(vmem_limit_bytes=3 << 20),
            cost_estimate=pl.CostEstimate(flops=20 * cells, bytes_accessed=8 * cells, transcendentals=cells // 4),
        )(diffusivity, advection, *args, solid)

    first = section(False, flat)
    map_line = iface_map.reshape(1, ny)
    extra = pl.pallas_call(
        functools.partial(relay_kernel, dims),
        out_shape=jax.ShapeDtypeStruct((nf, ny + 16, nz), BF),
        in_specs=[VM] * 3 + [HB],
        out_specs=VM,
        scratch_shapes=[pltpu.VMEM((16, nz), F32)],
        compiler_params=pltpu.CompilerParams(vmem_limit_bytes=1 << 20),
    )(map_line, a, b, first)
    if two:
        c2 = lax.ppermute(extra, "gy", swap)
        c2l, c2h, more = c2, c2, []
    else:
        c2l, c2h = lax.ppermute(extra, "gy", up), lax.ppermute(extra, "gy", down)
        more = [lax.all_gather(b[: 2 * nf : 2], "gy", axis=1, tiled=True),
                lax.all_gather(iface_map, "gy", axis=0, tiled=True).reshape(1, -1)]

    main = section(True, flat, first)
    mb = pltpu.VMEM
    return pl.pallas_call(
        functools.partial(border_kernel, dims, two),
        out_shape=jax.ShapeDtypeStruct((nf, nx, ny, nz), F32),
        in_specs=[SM, SM, VM] + [VM] * (9 + len(more)),
        out_specs=HB,
        scratch_shapes=[
            mb((nz, 2 * nz), BF), mb((4, nf, ny, nz), F32), mb((4, nf, nx, nz), F32), mb((2, nf, nx, nz), F32), mb((4, ny, nz), F32),
            mb((4, 8, nz), F32), mb((6, nf, ny, nz), F32), mb((6, nf, nx, nz), F32), mb((2, nf, ny, nz), F32),
            mb((2, nf, nx, nz), F32), mb((2, nf, nx, nz), F32), mb((4, nf, ny, nz), F32), mb((2, nf, nx, 8, nz), F32),
            mb((4, (nf + 1) * ny, 2 * nz), F32),
            pltpu.SemaphoreType.DMA((4, 8)),
        ],
        compiler_params=pltpu.CompilerParams(vmem_limit_bytes=10 << 20),
        cost_estimate=pl.CostEstimate(flops=10 * cells, bytes_accessed=8 * cells, transcendentals=cells // 4),
    )(diffusivity, advection, map_line, flat, first, main.reshape(nf, nx, ny, nz), solid,
      a, b, c1, c2l, c2h, *more)[None]


def solution(mesh):
    sizes = mesh.shape["gx"], mesh.shape["gy"]
    return jax.shard_map(
        functools.partial(body, sizes),
        mesh=mesh,
        in_specs=(P("comp", None, "gx", "gy", None), P(), P(), P("gx", "gy", None), P("gy")),
        out_specs=P("comp", None, "gx", "gy", None),
        check_vma=False,
    )
```
